32 devices in a mesh: dom: 8 (over z, y), grp: 4 (over x, core).
Axes of the slice: x: 2, y: 2, z: 4, core: 2. Of those that a mesh axis runs over, the one named last changes fastest.
Arguments:
- state_coeffs: float32 [6, 35, 2048], P(None, None, ('dom', 'grp')), may hold values from -6 to 6
- residual_in: float32 [6, 35, 2048], P(None, None, ('dom', 'grp')), may hold values from -6 to 6
- orders: int32 [2048], P(('dom', 'grp')), may hold values from 1 to 4
- neighbours: int32 [4, 2048], P(None, ('dom', 'grp')), may hold values from -1 to 2047, as said below
- neighbour_face: int32 [4, 2048], P(None, ('dom', 'grp')), may hold values from 0 to 3
- orientation: int32 [4, 2048], P(None, ('dom', 'grp')), may hold values from 0 to 5
- precond: bfloat16 [210, 430080], P(None, ('dom', 'grp'))
- source: float32 [6, 6, 2048], P(None, None, ('dom', 'grp'))
- flux_jacobian: float32 [3, 6, 6, 2048], P(None, None, None, ('dom', 'grp')), may hold values from -1.5 to 1.5
- geometry: float32 [3, 3, 2048], P(None, None, ('dom', 'grp')), may hold values from -3.5 to 3.5
- stiffness: float32 [3, 35, 35], replicated, may hold values from -1 to 1
- trace_matrix: float32 [4, 15, 35], replicated, may hold values from -1 to 1
Outputs:
- solution: float32 [6, 35, 2048], P(None, None, ('dom', 'grp'))
- hessenberg: float32 [7, 6], replicated
The draws below stay inside these ranges and needn't reach their ends.
Inputs may be any that keep to these rules, and one draw needn't show every extreme that they name: `neighbours`: each entry is -1 or an element other than the face's own, differing from it by at most 64; that difference is reached in every draw.
All inputs are finite; a program needn't handle non-finite values.
Results may differ from the reference program's by a relative error of at most 0.00068.
Values sent between devices are 32-bit elements; how exact they have to be, the bound alone decides.
No kernel may reach another device: no remote copies, remote signals or barrier semaphores. Data moves between devices by JAX's collectives and lax.ppermute only.
A program may use at most 128 MiB of HBM per device.

```python
import jax
import jax.numpy as jnp
from jax import lax

MAXORD = 4
NV = 6
NB = 35
NQ = 15
E_DEV = 64
ITERS = 6
ELEMS = 2048


def draw_neighbours(key, part):
    elements = jnp.arange(ELEMS, dtype=jnp.int32)[None, :]
    faces = jnp.arange(4, dtype=jnp.int32)[:, None]
    offsets = jax.random.randint(jax.random.fold_in(key, 11), (4, ELEMS), -E_DEV, E_DEV + 1)
    offsets = jnp.where(offsets == 0, 1, offsets)
    walls = jax.random.randint(jax.random.fold_in(key, 12), (4, ELEMS), 0, 10) == 0
    position = elements % E_DEV
    forced_low = (faces == 0) & (position == 0)
    forced_high = (faces == 1) & (position == E_DEV - 1)
    offsets = jnp.where(forced_low, -E_DEV, offsets)
    offsets = jnp.where(forced_high, E_DEV, offsets)
    target = elements + offsets
    walls = walls & jnp.logical_not(forced_low | forced_high)
    outside = (target < 0) | (target >= ELEMS)
    return jnp.where(walls | outside, -1, target).astype(jnp.int32)


def draw_precond(key, part):
    width = NV * NB
    row_ids = jnp.arange(width, dtype=jnp.int32)[:, None, None]
    col_ids = jnp.arange(width, dtype=jnp.int32)[None, None, :]
    identity = (row_ids == col_ids).astype(jnp.float32)
    noise = jax.random.normal(key, (width, ELEMS, width), jnp.float32)
    blocks = 0.25 * identity + 0.15 / width ** 0.5 * noise
    return blocks.reshape(width, ELEMS * width).astype(jnp.bfloat16)


def draw_source(key, part):
    row_ids = jnp.arange(NV, dtype=jnp.int32)[:, None, None]
    col_ids = jnp.arange(NV, dtype=jnp.int32)[None, :, None]
    identity = (row_ids == col_ids).astype(jnp.float32)
    strength = jax.random.uniform(jax.random.fold_in(key, 21), (NV, NV, ELEMS), jnp.float32, 2.0, 6.0)
    noise = 0.6 * jax.random.normal(jax.random.fold_in(key, 22), (NV, NV, ELEMS), jnp.float32)
    return identity * strength + noise


def set_ends(values, key, low, largest):
    spot = [jax.random.randint(jax.random.fold_in(key, axis), (), 0, length) for axis, length in enumerate(values.shape)]
    main_axis = values.shape.index(max(values.shape))
    beside = spot[:main_axis] + [(spot[main_axis] + 1) % values.shape[main_axis]] + spot[main_axis + 1:]
    return values.at[tuple(spot)].set(low).at[tuple(beside)].set(largest)


def block_levels(rng, dims, cuts, smallest, largest):
    def one(axis_at, parts):
        heights = jax.random.uniform(jax.random.fold_in(jax.random.fold_in(rng, 6), axis_at), (parts,), jnp.float32, smallest / len(cuts), largest / len(cuts))
        return jnp.repeat(jnp.exp(heights), dims[axis_at] // parts).reshape((-1,) + (1,) * (len(dims) - axis_at - 1))

    level = one(*cuts[0])
    for cut in cuts[1:]:
        level = level * one(*cut)
    return level


def bell_draw(own_key, shape, deviation, bound, split=(), kind=jnp.bfloat16):
    level = block_levels(own_key, shape, split, -0.22, 0.18) if split else 1.0
    result = jax.random.normal(own_key, shape, jnp.float32) * deviation * level
    return jnp.minimum(jnp.maximum(result, -bound), bound).astype(kind)


def setup_inputs(seed: int = 0) -> dict:
    arg_keys = jax.random.split(jax.random.key(seed), 13)
    return {
        "state_coeffs": bell_draw(arg_keys[0], (NV, NB, ELEMS), 1.0, 6.0, ((2, 32),), jnp.float32),
        "residual_in": bell_draw(arg_keys[1], (NV, NB, ELEMS), 1.0, 6.0, ((2, 32),), jnp.float32),
        "orders": set_ends(jax.random.randint(arg_keys[2], (ELEMS,), 1, MAXORD + 1), jax.random.fold_in(arg_keys[2], 1), 1, MAXORD).astype(jnp.int32),
        "neighbours": draw_neighbours(jax.random.fold_in(arg_keys[12], 71), 0),
        "neighbour_face": set_ends(jax.random.randint(arg_keys[4], (4, ELEMS), 0, 4), jax.random.fold_in(arg_keys[4], 1), 0, 3).astype(jnp.int32),
        "orientation": set_ends(jax.random.randint(arg_keys[5], (4, ELEMS), 0, 6), jax.random.fold_in(arg_keys[5], 1), 0, 5).astype(jnp.int32),
        "precond": draw_precond(jax.random.fold_in(arg_keys[12], 71), 0),
        "source": draw_source(jax.random.fold_in(arg_keys[12], 71), 0),
        "flux_jacobian": bell_draw(arg_keys[8], (3, NV, NV, ELEMS), (3 * NV) ** -0.5, 1.5, ((3, 32),), jnp.float32),
        "geometry": bell_draw(arg_keys[9], (3, 3, ELEMS), 3 ** -0.5, 3.5, ((2, 32),), jnp.float32),
        "stiffness": bell_draw(arg_keys[10], (3, NB, NB), NB ** -0.5, 1.0, (), jnp.float32),
        "trace_matrix": bell_draw(arg_keys[11], (4, NQ, NB), NB ** -0.5, 1.0, (), jnp.float32),
    }


EPSILON = 1e-06

def basis_count(orders):
    return (orders + 1) * (orders + 2) * (orders + 3) // 6

def order_mask(orders, nbasis):
    basis_ids = jnp.arange(nbasis, dtype=jnp.int32)[:, None]
    return (basis_ids < basis_count(orders)[None, :]).astype(jnp.float32)[None]

def point_order(orientation, npoints):
    points = jnp.arange(npoints, dtype=jnp.int32)[None, :, None]
    rotation = orientation[:, None, :] % 3
    reflected = orientation[:, None, :] // 3
    moved = (points + npoints // 3 * rotation) % npoints
    return jnp.where(reflected == 1, npoints - 1 - moved, moved)

def face_traces(field_vec, trace_matrix):
    return jnp.einsum('fqb,vbe->vfqe', trace_matrix, field_vec, precision=lax.Precision.HIGHEST)

def facing(traces_all, target, live_face, neighbour_face, orientation):
    nvar, nface, npts, span_len = traces_all.shape
    flat_traces = traces_all.reshape(nvar, nface * npts * span_len)
    flat_index = (neighbour_face[:, None, :] * npts + point_order(orientation, npts)) * span_len + target[:, None, :]
    gathered = jnp.take(flat_traces, flat_index.reshape(-1), axis=1)
    gathered = gathered.reshape(nvar, nface, npts, target.shape[1])
    return gathered * live_face[None, :, None, :]

def operate(field_vec, own_traces, other_traces, gain, coupling, source, stiffness, trace_matrix, basis_mask):
    high = lax.Precision.HIGHEST
    face_term = jnp.einsum('fqb,vfqe->vbe', trace_matrix, gain * (own_traces - other_traces), precision=high)
    stiff_moved = jnp.einsum('dcb,vbe->dvce', stiffness, field_vec, precision=high)
    volume_term = jnp.einsum('dwve,dvce->wce', coupling, stiff_moved, precision=high)
    source_term = jnp.einsum('wve,vbe->wbe', source, field_vec, precision=high)
    return (volume_term + source_term + face_term) * basis_mask

def precondition(vector, precond, basis_mask):
    shape_in = vector.shape
    width = shape_in[0] * shape_in[1]
    blocks = precond.reshape(width, shape_in[2], width)
    flat_vec = (vector * basis_mask).astype(jnp.bfloat16).reshape(width, shape_in[2])
    applied = jnp.einsum('iej,je->ie', blocks, flat_vec, preferred_element_type=jnp.float32)
    return applied.reshape(shape_in) * basis_mask

def least_squares(hess, start_value):
    ncols = hess.shape[1]
    upper = [[hess[i, j] for j in range(ncols)] for i in range(ncols + 1)]
    right_vec = [start_value] + [jnp.zeros((), jnp.float32) for i in range(ncols)]
    for k in range(ncols):
        lead = upper[k][k]
        below = upper[k + 1][k]
        radius = jnp.sqrt(lead * lead + below * below)
        cosine = lead / radius
        sine_val = below / radius
        for j in range(k, ncols):
            top_val = upper[k][j]
            low_val = upper[k + 1][j]
            upper[k][j] = cosine * top_val + sine_val * low_val
            upper[k + 1][j] = cosine * low_val - sine_val * top_val
        top_val = right_vec[k]
        low_val = right_vec[k + 1]
        right_vec[k] = cosine * top_val + sine_val * low_val
        right_vec[k + 1] = cosine * low_val - sine_val * top_val
    coeffs = [None] * ncols
    for k in reversed(range(ncols)):
        accum = right_vec[k]
        for j in range(k + 1, ncols):
            accum = accum - upper[k][j] * coeffs[j]
        coeffs[k] = accum / upper[k][k]
    return coeffs

def reference(state_coeffs, residual_in, orders, neighbours, neighbour_face, orientation, precond, source, flux_jacobian, geometry, stiffness, trace_matrix):
    high = lax.Precision.HIGHEST
    elem_count = state_coeffs.shape[2]
    basis_mask = order_mask(orders, state_coeffs.shape[1])
    live_face = (neighbours >= 0).astype(jnp.float32)
    target = jnp.clip(neighbours, 0, elem_count - 1).astype(jnp.int32)
    coupling = jnp.einsum('dke,dwve->kwve', geometry, flux_jacobian, precision=high)
    state_tr = face_traces(state_coeffs, trace_matrix)
    gain = 1.0 + 0.5 * jnp.abs(state_tr + facing(state_tr, target, live_face, neighbour_face, orientation))
    start_vec = residual_in * basis_mask
    start_value = jnp.sqrt(jnp.sum(start_vec * start_vec) + EPSILON)
    basis = [start_vec / start_value]
    hess = jnp.zeros((ITERS + 1, ITERS), jnp.float32)
    searches = []
    for k in range(ITERS):
        search = precondition(basis[k], precond, basis_mask)
        traces_all = face_traces(search, trace_matrix)
        other = facing(traces_all, target, live_face, neighbour_face, orientation)
        image = operate(search, traces_all, other, gain, coupling, source, stiffness, trace_matrix, basis_mask)
        krylov_stack = jnp.stack(basis)
        projection = jnp.einsum('kvbe,vbe->k', krylov_stack, image, precision=high)
        image = image - jnp.einsum('k,kvbe->vbe', projection, krylov_stack, precision=high)
        norm_value = jnp.sqrt(jnp.sum(image * image) + EPSILON)
        hess = hess.at[:k + 1, k].set(projection)
        hess = hess.at[k + 1, k].set(norm_value)
        if k + 1 < ITERS:
            basis.append(image / norm_value)
        searches.append(search)
    coeffs = least_squares(hess, start_value)
    solution = coeffs[0] * searches[0]
    for k in range(1, ITERS):
        solution = solution + coeffs[k] * searches[k]
    return (solution, hess)
```

```python
import functools

import jax
import jax.numpy as jnp
from jax import lax
from jax.experimental import pallas as pl
from jax.experimental.pallas import tpu as pltpu
from jax.sharding import PartitionSpec as P

ITERS = 6
EPSILON = 1e-06
AXES = ("dom", "grp")
F32 = jnp.float32
BF16 = jnp.bfloat16
VMEM = pl.BlockSpec(memory_space=pltpu.VMEM)
SMEM = pl.BlockSpec(memory_space=pltpu.SMEM)


def ceil_to(n, m):
    return -(-n // m) * m


def iota(shape, dim):
    return lax.broadcasted_iota(jnp.int32, shape, dim)


def split3(x):
    hi = x.astype(BF16).astype(F32)
    rest = x - hi
    mid = rest.astype(BF16).astype(F32)
    return hi, mid, rest - mid


def stack_rhs(parts, axis):
    hi, mid, lo = parts
    return jnp.concatenate([hi, mid, lo, hi, mid, hi], axis=axis).astype(BF16)


def stack_lhs(x):
    hi, mid, lo = split3(x)
    return jnp.concatenate([hi, hi, hi, mid, mid, lo], axis=1).astype(BF16)


def dot(a, b):
    return jnp.dot(a, b, preferred_element_type=F32)


def pad_rows(x, rows):
    return jnp.concatenate([x, jnp.zeros((rows - x.shape[0], x.shape[1]), x.dtype)], axis=0)


class Sizes:
    def __init__(self, nv, nb, ne, nq, peers):
        self.nv, self.nb, self.ne, self.nq, self.peers = nv, nb, ne, nq, peers
        self.nbp = ceil_to(nb, 8)
        self.nqp = ceil_to(nq, 8)
        self.lanes = nv * ne
        self.width = nv * nb
        self.kwidth = ceil_to(self.width, 128)
        self.pair = 2 * ne


def to_wide(read, sz):
    return pad_rows(jnp.concatenate([read(v) for v in range(sz.nv)], axis=1), sz.nbp)


def partial_rows(values, peers):
    lane = iota((1, 128), 1)
    row = jnp.zeros((1, 128), F32)
    for i, val in enumerate(values):
        row = jnp.where(lane == i, val, row)
    return jnp.broadcast_to(row, (peers, 128))


def full_sum(x):
    return jnp.sum(jnp.sum(x, axis=0, keepdims=True), axis=1, keepdims=True)


def total_scalars(red, count):
    row = jnp.sum(red, axis=0, keepdims=True)
    lane = iota((1, 128), 1)
    return [jnp.sum(jnp.where(lane == i, row, 0.0), axis=1, keepdims=True) for i in range(count)]


def init_kernel(
    sz, me_ref, res_ref, state_ref, orders_ref, nbr_ref, face_ref, orient_ref, source_ref, flux_ref, geo_ref,
    stiff_ref, trace_ref, start_ref, state2_ref, mask_ref, hot_ref, coup_ref, sel_ref, own_ref, near_ref, back_ref,
    part_ref,
):
    nv, nb, ne, nq, nbp, nqp = sz.nv, sz.nb, sz.ne, sz.nq, sz.nbp, sz.nqp
    orders = orders_ref[...]
    count = (orders + 1) * (orders + 2) * (orders + 3) // 6
    count = jnp.concatenate([count] * nv, axis=1)
    mask = (iota((nbp, sz.lanes), 0) < count).astype(F32)
    mask_ref[...] = mask
    start = to_wide(lambda v: res_ref[v], sz) * mask
    start_ref[...] = start
    part_ref[...] = partial_rows([full_sum(start * start)], sz.peers)
    state2_ref[...] = to_wide(lambda v: state_ref[v], sz)

    me = me_ref[0]
    nbr = nbr_ref[...]
    rel = jnp.where(nbr >= 0, nbr - me * ne + ne, -4 * ne)
    cols = jnp.concatenate(
        [piece for f in range(4) for piece in (rel[f : f + 1], rel[f : f + 1] + 3 * ne * (rel[f : f + 1] >= 0).astype(jnp.int32))],
        axis=1,
    )
    rows = iota((3 * sz.pair, 4 * sz.pair), 0)
    block = rows // sz.pair
    even = lax.rem(me, 2) == 0
    chip_side = jnp.where(even, 2, 0)
    side = jnp.where(block == 0, 1, jnp.where(block == 1, chip_side, 2 - chip_side))
    inner = rows - block * sz.pair
    parity = (inner >= ne).astype(jnp.int32)
    code = side * ne + inner - parity * ne + 3 * ne * parity
    hot_ref[...] = (code == cols).astype(F32).astype(BF16)

    face = face_ref[...]
    orient = orient_ref[...]
    flip = (orient >= 3).astype(jnp.int32)
    choice = flip * 4 + face
    turn = orient - 3 * flip
    sel_ref[...] = jnp.concatenate([jnp.concatenate([choice, turn], axis=0)] * nv, axis=1)

    for k in range(3):
        pieces = []
        for w in range(nv):
            tile = jnp.zeros((nv, ne), F32)
            for d in range(3):
                tile = tile + geo_ref[d, k : k + 1, :] * flux_ref[d, w]
            pieces.append(tile if w == 0 else jnp.concatenate([tile[w:], tile[:w]], axis=0))
        coup_ref[k] = jnp.concatenate(pieces, axis=1)
    pieces = []
    for w in range(nv):
        tile = source_ref[w]
        pieces.append(tile if w == 0 else jnp.concatenate([tile[w:], tile[:w]], axis=0))
    coup_ref[3] = jnp.concatenate(pieces, axis=1)

    def pad2(x, rows):
        x = jnp.concatenate([x, jnp.zeros((x.shape[0], nbp - x.shape[1]), F32)], axis=1)
        return pad_rows(x, rows)

    traces = [trace_ref[f] for f in range(4)]
    plain = [pad2(t, nqp) for t in traces]
    flipped = [
        pad2(jnp.concatenate([t[q : q + 1] for q in reversed(range(nq))], axis=0), nqp) for t in traces
    ]
    volume = [pad2(stiff_ref[d], nbp) for d in range(3)]
    own_ref[...] = stack_lhs(jnp.concatenate(plain + volume, axis=0))
    near_ref[...] = stack_lhs(jnp.concatenate(plain + flipped, axis=0))
    back_ref[...] = stack_lhs(jnp.concatenate(plain, axis=0).T)


def relay_kernel(sz, p_ref, out_ref):
    width, kwidth, ne = sz.width, sz.kwidth, sz.ne
    total = width * ne
    zeros = jnp.zeros((width, kwidth - width), F32)
    for e in range(ne):
        low = e * width // 128 * 128
        high = min(ceil_to((e + 1) * width, 128), total)
        shift = e * width - low
        window = p_ref[:, low:high].astype(F32)
        piece = window[:, shift : shift + width]
        out_ref[e] = jnp.concatenate([piece, zeros], axis=1).astype(BF16)


def apply_blocks(sz, vec, mask, blocks_ref):
    nb, ne, nv = sz.nb, sz.ne, sz.nv
    tall = jnp.concatenate([vec[:nb, v * ne : (v + 1) * ne] for v in range(nv)], axis=0)
    tall = pad_rows(tall, sz.kwidth)
    lane = iota((1, ne), 1)

    def step(e, acc):
        picked = jnp.where(lane == e, tall, 0.0).astype(BF16)
        return acc + dot(blocks_ref[e], picked)

    acc = lax.fori_loop(0, ne, step, jnp.zeros((sz.width, ne), F32), unroll=4)
    wide = jnp.concatenate([acc[v * nb : (v + 1) * nb] for v in range(nv)], axis=1)
    return pad_rows(wide, sz.nbp) * mask


def precond_kernel(sz, step, *refs):
    red_ref, vec_ref, mask_ref, blocks_ref = refs[:4]
    mask = mask_ref[...]
    vec = vec_ref[...]
    if step == 0:
        state_ref, z_ref, v_ref, h_ref = refs[4:]
        norm = jnp.sqrt(total_scalars(red_ref[...], 1)[0] + EPSILON)
        values = [norm]
    else:
        basis = refs[4 : 4 + step]
        z_ref, v_ref, h_ref = refs[4 + step :]
        scalars = total_scalars(red_ref[...], step + 1)
        proj, square = scalars[:step], scalars[step]
        for h, b in zip(proj, basis):
            vec = vec - h * b[...]
            square = square - h * h
        norm = jnp.sqrt(square + EPSILON)
        values = proj + [norm]
    new = vec / norm
    v_ref[...] = new
    h_ref[...] = partial_rows(values, 1)
    search = apply_blocks(sz, new, mask, blocks_ref)
    if step == 0:
        z_ref[: sz.nbp] = search
        z_ref[sz.nbp :] = state_ref[...]
    else:
        z_ref[...] = search


def roll_blocks(x, blocks, ne):
    shift = blocks * ne
    if shift == 0:
        return x
    return jnp.concatenate([x[:, shift:], x[:, :shift]], axis=1)


def local_kernel(sz, z_ref, own_ref, coup_ref, vol_ref, tr_ref):
    search = z_ref[: sz.nbp]
    out = dot(own_ref[...], stack_rhs(split3(search), 0))
    faces = 4 * sz.nqp
    tr_ref[...] = out[:faces]
    acc = jnp.zeros((sz.nbp, sz.lanes), F32)
    for d in range(4):
        moved = search if d == 3 else out[faces + d * sz.nbp : faces + (d + 1) * sz.nbp]
        for s in range(sz.nv):
            acc = acc + coup_ref[d, s : s + 1, :] * roll_blocks(moved, s, sz.ne)
    vol_ref[...] = acc


def neighbour_traces(sz, own, chip, far, hot_ref, near_ref, sel_ref):
    nbp, nqp, pair = sz.nbp, sz.nqp, sz.pair
    parts = [split3(x) for x in (own, chip, far)]
    pairs = sz.lanes // pair
    lhs = jnp.concatenate(
        [
            jnp.concatenate([parts[side][n][:, p * pair : (p + 1) * pair] for side in range(3)], axis=1)
            for n in range(3)
            for p in range(pairs)
        ],
        axis=0,
    ).astype(BF16)
    got = dot(lhs, hot_ref[...])
    result = []
    for f in range(4):
        picked = [
            jnp.concatenate(
                [
                    got[(n * pairs + p) * nbp : (n * pairs + p + 1) * nbp, f * pair : (f + 1) * pair]
                    for p in range(pairs)
                ],
                axis=1,
            )
            for n in range(3)
        ]
        every = dot(near_ref[...], stack_rhs(picked, 0))
        choice = sel_ref[f : f + 1, :]
        turn = sel_ref[4 + f : 5 + f, :]
        tr = every[:nqp]
        for g in range(1, 8):
            tr = jnp.where(choice == g, every[g * nqp : (g + 1) * nqp], tr)
        nq, third = sz.nq, sz.nq // 3
        fill = tr[nq:]
        once = jnp.concatenate([tr[third:nq], tr[:third], fill], axis=0)
        twice = jnp.concatenate([tr[2 * third : nq], tr[: 2 * third], fill], axis=0)
        result.append(jnp.where(turn == 0, tr, jnp.where(turn == 1, once, twice)))
    return jnp.concatenate(result, axis=0)


def gain_kernel(sz, z_ref, chip_ref, far_ref, hot_ref, near_ref, own_ref, sel_ref, gain_ref):
    nbp = sz.nbp
    state = z_ref[nbp:]
    tr = dot(own_ref[: 4 * sz.nqp], stack_rhs(split3(state), 0))
    other = neighbour_traces(sz, state, chip_ref[nbp:], far_ref[nbp:], hot_ref, near_ref, sel_ref)
    gain_ref[...] = 1.0 + 0.5 * jnp.abs(tr + other)


def image_kernel(sz, step, *refs):
    z_ref, chip_ref, far_ref, hot_ref, near_ref, sel_ref, gain_ref, back_ref, vol_ref, tr_ref, mask_ref = refs[:11]
    basis = refs[11 : 12 + step]
    w_ref, part_ref = refs[12 + step :]
    nbp = sz.nbp
    other = neighbour_traces(sz, z_ref[:nbp], chip_ref[:nbp], far_ref[:nbp], hot_ref, near_ref, sel_ref)
    flux = gain_ref[...] * (tr_ref[...] - other)
    face = dot(back_ref[...], stack_rhs(split3(flux), 0))
    image = (vol_ref[...] + face) * mask_ref[...]
    w_ref[...] = image
    values = [full_sum(b[...] * image) for b in basis] + [full_sum(image * image)]
    part_ref[...] = partial_rows(values, sz.peers)


def finish_kernel(sz, *refs):
    red_ref, heads, searches = refs[0], refs[1 : 1 + ITERS], refs[1 + ITERS : 1 + 2 * ITERS]
    out_ref, hess_ref = refs[1 + 2 * ITERS :]
    lane = iota((1, 128), 1)

    def entry(row, i):
        return jnp.sum(jnp.where(lane == i, row, 0.0), axis=1, keepdims=True)

    start_value = entry(heads[0][...], 0)
    zero = jnp.zeros((1, 1), F32)
    upper = [[zero] * ITERS for _ in range(ITERS + 1)]
    for k in range(ITERS - 1):
        row = heads[k + 1][...]
        for i in range(k + 2):
            upper[i][k] = entry(row, i)
    scalars = total_scalars(red_ref[...], ITERS + 1)
    square = scalars[ITERS]
    for i in range(ITERS):
        upper[i][ITERS - 1] = scalars[i]
        square = square - scalars[i] * scalars[i]
    upper[ITERS][ITERS - 1] = jnp.sqrt(square + EPSILON)
    shape = hess_ref.shape
    row_id, col_id = iota(shape, 0), iota(shape, 1)
    hess = jnp.zeros(shape, F32)
    for i in range(ITERS + 1):
        for k in range(max(i - 1, 0), ITERS):
            hess = jnp.where((row_id == i) & (col_id == k), upper[i][k], hess)
    hess_ref[...] = hess
    right = [start_value] + [zero] * ITERS
    for k in range(ITERS):
        lead, below = upper[k][k], upper[k + 1][k]
        radius = jnp.sqrt(lead * lead + below * below)
        cosine, sine = lead / radius, below / radius
        for j in range(k, ITERS):
            top, low = upper[k][j], upper[k + 1][j]
            upper[k][j] = cosine * top + sine * low
            upper[k + 1][j] = cosine * low - sine * top
        top, low = right[k], right[k + 1]
        right[k] = cosine * top + sine * low
        right[k + 1] = cosine * low - sine * top
    coeffs = [None] * ITERS
    for k in reversed(range(ITERS)):
        acc = right[k]
        for j in range(k + 1, ITERS):
            acc = acc - upper[k][j] * coeffs[j]
        coeffs[k] = acc / upper[k][k]
    total = coeffs[0] * searches[0][: sz.nbp]
    for k in range(1, ITERS):
        total = total + coeffs[k] * searches[k][: sz.nbp]
    for v in range(sz.nv):
        out_ref[v] = total[: sz.nb, v * sz.ne : (v + 1) * sz.ne]


def call(kernel, name, out_shape, *args, smem_first=False, limit=None):
    specs = [VMEM] * len(args)
    if smem_first:
        specs[0] = SMEM
    return pl.pallas_call(
        kernel,
        name=name,
        out_shape=out_shape,
        in_specs=specs,
        out_specs=jax.tree.map(lambda _: VMEM, out_shape),
        compiler_params=pltpu.CompilerParams(vmem_limit_bytes=limit or 32 * 2**20),
    )(*args)


def shape(*dims, dtype=F32):
    return jax.ShapeDtypeStruct(dims, dtype)


def body(
    peers, state_coeffs, residual_in, orders, neighbours, neighbour_face, orientation, precond, source,
    flux_jacobian, geometry, stiffness, trace_matrix,
):
    nv, nb, ne = state_coeffs.shape
    sz = Sizes(nv, nb, ne, trace_matrix.shape[1], peers)
    lanes, nbp, nqp = sz.lanes, sz.nbp, sz.nqp
    me = lax.axis_index(AXES).astype(jnp.int32).reshape(1)
    wide = shape(nbp, lanes)
    parts = shape(peers, 128)
    start, state, mask, hot, coup, sel, own, near, back, part = call(
        functools.partial(init_kernel, sz),
        "init",
        (
            wide, wide, wide,
            shape(3 * sz.pair, 4 * sz.pair, dtype=BF16),
            shape(4, nv, lanes),
            shape(8, lanes, dtype=jnp.int32),
            shape(4 * nqp + 3 * nbp, 6 * nbp, dtype=BF16),
            shape(8 * nqp, 6 * nbp, dtype=BF16),
            shape(nbp, 24 * nqp, dtype=BF16),
            parts,
        ),
        me, residual_in, state_coeffs, orders.reshape(1, ne), neighbours, neighbour_face, orientation, source,
        flux_jacobian, geometry, stiffness, trace_matrix,
        smem_first=True,
    )
    blocks = call(
        functools.partial(relay_kernel, sz), "relay", shape(ne, sz.width, sz.kwidth, dtype=BF16), precond
    )

    def exchange(rows):
        return lax.all_to_all(rows, AXES, 0, 0, tiled=True)

    on_chip = [(i, i ^ 1) for i in range(peers)]
    odd = range(1, peers - 1, 2)
    off_chip = [(i, i + 1) for i in odd] + [(i + 1, i) for i in odd]

    heads, searches, basis = [], [], []
    vec, gain = start, None
    for k in range(ITERS):
        red = exchange(part)
        z_shape = shape(2 * nbp, lanes) if k == 0 else wide
        extra = [state] if k == 0 else basis
        search, new, head = call(
            functools.partial(precond_kernel, sz, k), f"precond{k}", (z_shape, wide, shape(1, 128)),
            red, vec, mask, blocks, *extra,
        )
        basis = basis + [new]
        heads.append(head)
        searches.append(search)
        far = lax.ppermute(search, AXES, off_chip)
        chip = lax.ppermute(search, AXES, on_chip)
        vol, tr = call(
            functools.partial(local_kernel, sz), "local", (wide, shape(4 * nqp, lanes)), search, own, coup
        )
        if k == 0:
            gain = call(
                functools.partial(gain_kernel, sz), "gain", shape(4 * nqp, lanes),
                search, chip, far, hot, near, own, sel,
            )
        vec, part = call(
            functools.partial(image_kernel, sz, k), f"image{k}", (wide, parts),
            search, chip, far, hot, near, sel, gain, back, vol, tr, mask, *basis,
        )
    red = exchange(part)
    return call(
        functools.partial(finish_kernel, sz), "finish", (shape(nv, nb, ne), shape(ITERS + 1, ITERS)),
        red, *heads, *searches,
    )


def solution(mesh):
    placed = (
        P(None, None, AXES),
        P(None, None, AXES),
        P(AXES),
        P(None, AXES),
        P(None, AXES),
        P(None, AXES),
        P(None, AXES),
        P(None, None, AXES),
        P(None, None, None, AXES),
        P(None, None, AXES),
        P(),
        P(),
    )
    peers = 1
    for axis in AXES:
        peers *= mesh.shape[axis]
    return jax.shard_map(
        functools.partial(body, peers),
        mesh=mesh,
        in_specs=placed,
        out_specs=(P(None, None, AXES), P()),
        check_vma=False,
    )
```

```python
import functools

import jax
import jax.numpy as jnp
from jax import lax
from jax.experimental import pallas as pl
from jax.experimental.pallas import tpu as pltpu
from jax.sharding import PartitionSpec as P

ITERS = 6
EPSILON = 1e-06
AXES = ("dom", "grp")
F32 = jnp.float32
BF16 = jnp.bfloat16
CHUNK = 256
VMEM = pl.BlockSpec(memory_space=pltpu.VMEM)
ANY = pl.BlockSpec(memory_space=pl.ANY)
SMEM = pl.BlockSpec(memory_space=pltpu.SMEM)


def ceil_to(n, m):
    return -(-n // m) * m


def iota(shape, dim):
    return lax.broadcasted_iota(jnp.int32, shape, dim)


def split3(x):
    hi = x.astype(BF16).astype(F32)
    rest = x - hi
    mid = rest.astype(BF16).astype(F32)
    return hi, mid, rest - mid


def stack_rhs(parts, axis):
    hi, mid, lo = parts
    return jnp.concatenate([hi, mid, lo, hi, mid, hi], axis=axis).astype(BF16)


def stack_lhs(x):
    hi, mid, lo = split3(x)
    return jnp.concatenate([hi, hi, hi, mid, mid, lo], axis=1).astype(BF16)


def dot(a, b):
    return jnp.dot(a, b, preferred_element_type=F32)


def pad_rows(x, rows):
    return jnp.concatenate([x, jnp.zeros((rows - x.shape[0], x.shape[1]), x.dtype)], axis=0)


class Sizes:
    def __init__(self, nv, nb, ne, nq, peers):
        self.nv, self.nb, self.ne, self.nq, self.peers = nv, nb, ne, nq, peers
        self.nbp = ceil_to(nb, 8)
        self.nqp = ceil_to(nq, 8)
        self.lanes = nv * ne
        self.width = nv * nb
        self.kwidth = ceil_to(self.width, 128)
        self.pair = 2 * ne


def to_wide(read, sz):
    return pad_rows(jnp.concatenate([read(v) for v in range(sz.nv)], axis=1), sz.nbp)


def partial_rows(values, peers):
    lane = iota((1, 128), 1)
    row = jnp.zeros((1, 128), F32)
    for i, val in enumerate(values):
        row = jnp.where(lane == i, val, row)
    return jnp.broadcast_to(row, (peers, 128))


def full_sum(x):
    return jnp.sum(jnp.sum(x, axis=0, keepdims=True), axis=1, keepdims=True)


def total_scalars(red, count):
    row = jnp.sum(red, axis=0, keepdims=True)
    lane = iota((1, 128), 1)
    return [jnp.sum(jnp.where(lane == i, row, 0.0), axis=1, keepdims=True) for i in range(count)]


def fetch(pairs, sems):
    copies = [pltpu.make_async_copy(src, dst, sems.at[i]) for i, (src, dst) in enumerate(pairs)]
    for copy in copies:
        copy.start()
    for copy in copies:
        copy.wait()


def begin_kernel(sz, res_hbm, orders_hbm, start_ref, mask_ref, part_ref, res_ref, orders_ref, sems):
    fetch([(res_hbm, res_ref), (orders_hbm, orders_ref)], sems)
    orders = orders_ref[...]
    count = (orders + 1) * (orders + 2) * (orders + 3) // 6
    count = jnp.concatenate([count] * sz.nv, axis=1)
    mask = (iota((sz.nbp, sz.lanes), 0) < count).astype(F32)
    mask_ref[...] = mask
    start = to_wide(lambda v: res_ref[v], sz) * mask
    start_ref[...] = start
    part_ref[...] = partial_rows([full_sum(start * start)], sz.peers)


def init_kernel(sz, me_ref, *refs):
    args, outs, held, sems = refs[:9], refs[9:16], refs[16:25], refs[25]
    fetch(list(zip(args, held)), sems)
    state_ref, nbr_ref, face_ref, orient_ref, source_ref, flux_ref, geo_ref, stiff_ref, trace_ref = held
    state2_ref, hot_ref, coup_ref, sel_ref, own_ref, near_ref, back_ref = outs
    nv, nb, ne, nq, nbp, nqp = sz.nv, sz.nb, sz.ne, sz.nq, sz.nbp, sz.nqp
    state2_ref[...] = to_wide(lambda v: state_ref[v], sz)

    me = me_ref[0]
    nbr = nbr_ref[...]
    rel = jnp.where(nbr >= 0, nbr - me * ne + ne, -4 * ne)
    cols = jnp.concatenate(
        [piece for f in range(4) for piece in (rel[f : f + 1], rel[f : f + 1] + 3 * ne * (rel[f : f + 1] >= 0).astype(jnp.int32))],
        axis=1,
    )
    rows = iota((3 * sz.pair, 4 * sz.pair), 0)
    block = rows // sz.pair
    even = lax.rem(me, 2) == 0
    chip_side = jnp.where(even, 2, 0)
    side = jnp.where(block == 0, 1, jnp.where(block == 1, chip_side, 2 - chip_side))
    inner = rows - block * sz.pair
    parity = (inner >= ne).astype(jnp.int32)
    code = side * ne + inner - parity * ne + 3 * ne * parity
    hot_ref[...] = (code == cols).astype(F32).astype(BF16)

    face = face_ref[...]
    orient = orient_ref[...]
    flip = (orient >= 3).astype(jnp.int32)
    choice = flip * 4 + face
    turn = orient - 3 * flip
    sel_ref[...] = jnp.concatenate([jnp.concatenate([choice, turn], axis=0)] * nv, axis=1)

    for k in range(3):
        pieces = []
        for w in range(nv):
            tile = jnp.zeros((nv, ne), F32)
            for d in range(3):
                tile = tile + geo_ref[d, k : k + 1, :] * flux_ref[d, w]
            pieces.append(tile if w == 0 else jnp.concatenate([tile[w:], tile[:w]], axis=0))
        coup_ref[k] = jnp.concatenate(pieces, axis=1)
    pieces = []
    for w in range(nv):
        tile = source_ref[w]
        pieces.append(tile if w == 0 else jnp.concatenate([tile[w:], tile[:w]], axis=0))
    coup_ref[3] = jnp.concatenate(pieces, axis=1)

    def pad2(x, rows):
        x = jnp.concatenate([x, jnp.zeros((x.shape[0], nbp - x.shape[1]), F32)], axis=1)
        return pad_rows(x, rows)

    traces = [trace_ref[:, f, :] for f in range(4)]
    plain = [pad2(t, nqp) for t in traces]
    flipped = [
        pad2(jnp.concatenate([t[q : q + 1] for q in reversed(range(nq))], axis=0), nqp) for t in traces
    ]
    volume = [pad2(stiff_ref[d], nbp) for d in range(3)]
    own_ref[...] = stack_lhs(jnp.concatenate(plain + volume, axis=0))
    near_ref[...] = stack_lhs(jnp.concatenate(plain + flipped, axis=0))
    back_ref[...] = stack_lhs(jnp.concatenate(plain, axis=0).T)


def apply_blocks(sz, vec, mask, blocks_ref, ready):
    nb, ne, nv, width = sz.nb, sz.ne, sz.nv, sz.width
    tall = jnp.concatenate([vec[:nb, v * ne : (v + 1) * ne] for v in range(nv)], axis=0)
    turned = pad_rows(tall, CHUNK).T
    amount = lax.rem(iota((ne, 1), 0) * width, CHUNK)
    bit = 1
    while bit < CHUNK:
        if any(e * width % CHUNK & bit for e in range(ne)):
            turned = jnp.where((amount & bit) != 0, pltpu.roll(turned, bit, 1), turned)
        bit *= 2
    total = ne * width
    acc = [jnp.zeros((8, width), F32)] * (ne // 8)
    for low in range(0, total, CHUNK):
        high = min(low + CHUNK, total)
        ready(high)
        first, last = low // width // 8, (high - 1) // width // 8 + 1
        size = (8 * (last - first), high - low)
        entry = iota(size, 1) + low - (iota(size, 0) + 8 * first) * width
        lhs = jnp.where((entry >= 0) & (entry < width), turned[8 * first : 8 * last, : high - low], 0.0)
        out = lax.dot_general(
            lhs.astype(BF16), blocks_ref[:, low:high], (((1,), (1,)), ((), ())), preferred_element_type=F32
        )
        for g in range(first, last):
            acc[g] = acc[g] + out[8 * (g - first) : 8 * (g - first + 1)]
    done = jnp.concatenate(acc, axis=0)
    done = jnp.concatenate([done, jnp.zeros((ne, CHUNK - width), F32)], axis=1).T
    wide = jnp.concatenate([done[v * nb : (v + 1) * nb] for v in range(nv)], axis=1)
    return pad_rows(wide, sz.nbp) * mask


def precond_start_kernel(sz, red_ref, vec_ref, mask_ref, state_ref, p_hbm, z_ref, v_ref, h_ref, blocks_ref, sems):
    total, count = sz.ne * sz.width, sems.shape[0]
    step = ceil_to(-(-total // count), 128)
    edges = [(low, min(low + step, total)) for low in range(0, total, step)]
    copies = [
        pltpu.make_async_copy(p_hbm.at[:, low:high], blocks_ref.at[:, low:high], sems.at[i])
        for i, (low, high) in enumerate(edges)
    ]
    for copy in copies:
        copy.start()
    norm = jnp.sqrt(total_scalars(red_ref[...], 1)[0] + EPSILON)
    new = vec_ref[...] / norm
    v_ref[...] = new
    h_ref[...] = partial_rows([norm], 1)
    waited = []

    def ready(high):
        while len(waited) < len(edges) and edges[len(waited)][0] < high:
            copies[len(waited)].wait()
            waited.append(True)

    z_ref[: sz.nbp] = apply_blocks(sz, new, mask_ref[...], blocks_ref, ready)
    z_ref[sz.nbp :] = state_ref[...]


def precond_kernel(sz, step, *refs):
    red_ref, vec_ref, mask_ref, blocks_ref = refs[:4]
    basis = refs[4 : 4 + step]
    z_ref, v_ref, h_ref = refs[4 + step :]
    vec = vec_ref[...]
    scalars = total_scalars(red_ref[...], step + 1)
    proj, square = scalars[:step], scalars[step]
    for h, b in zip(proj, basis):
        vec = vec - h * b[...]
        square = square - h * h
    norm = jnp.sqrt(square + EPSILON)
    new = vec / norm
    v_ref[...] = new
    h_ref[...] = partial_rows(proj + [norm], 1)
    z_ref[...] = apply_blocks(sz, new, mask_ref[...], blocks_ref, lambda high: None)


def roll_blocks(x, blocks, ne):
    shift = blocks * ne
    if shift == 0:
        return x
    return jnp.concatenate([x[:, shift:], x[:, :shift]], axis=1)


def local_kernel(sz, z_ref, own_ref, coup_ref, vol_ref, tr_ref):
    search = z_ref[: sz.nbp]
    out = dot(own_ref[...], stack_rhs(split3(search), 0))
    faces = 4 * sz.nqp
    tr_ref[...] = out[:faces]
    acc = jnp.zeros((sz.nbp, sz.lanes), F32)
    for d in range(4):
        moved = search if d == 3 else out[faces + d * sz.nbp : faces + (d + 1) * sz.nbp]
        for s in range(sz.nv):
            acc = acc + coup_ref[d, s : s + 1, :] * roll_blocks(moved, s, sz.ne)
    vol_ref[...] = acc


def neighbour_traces(sz, own, chip, far, hot_ref, near_ref, sel_ref):
    nbp, nqp, pair = sz.nbp, sz.nqp, sz.pair
    parts = [split3(x) for x in (own, chip, far)]
    pairs = sz.lanes // pair
    lhs = jnp.concatenate(
        [
            jnp.concatenate([parts[side][n][:, p * pair : (p + 1) * pair] for side in range(3)], axis=1)
            for n in range(3)
            for p in range(pairs)
        ],
        axis=0,
    ).astype(BF16)
    got = dot(lhs, hot_ref[...])
    result = []
    for f in range(4):
        picked = [
            jnp.concatenate(
                [
                    got[(n * pairs + p) * nbp : (n * pairs + p + 1) * nbp, f * pair : (f + 1) * pair]
                    for p in range(pairs)
                ],
                axis=1,
            )
            for n in range(3)
        ]
        every = dot(near_ref[...], stack_rhs(picked, 0))
        choice = sel_ref[f : f + 1, :]
        turn = sel_ref[4 + f : 5 + f, :]
        tr = every[:nqp]
        for g in range(1, 8):
            tr = jnp.where(choice == g, every[g * nqp : (g + 1) * nqp], tr)
        nq, third = sz.nq, sz.nq // 3
        fill = tr[nq:]
        once = jnp.concatenate([tr[third:nq], tr[:third], fill], axis=0)
        twice = jnp.concatenate([tr[2 * third : nq], tr[: 2 * third], fill], axis=0)
        result.append(jnp.where(turn == 0, tr, jnp.where(turn == 1, once, twice)))
    return jnp.concatenate(result, axis=0)


def gain_kernel(sz, z_ref, chip_ref, far_ref, hot_ref, near_ref, own_ref, sel_ref, gain_ref):
    nbp = sz.nbp
    state = z_ref[nbp:]
    tr = dot(own_ref[: 4 * sz.nqp], stack_rhs(split3(state), 0))
    other = neighbour_traces(sz, state, chip_ref[nbp:], far_ref[nbp:], hot_ref, near_ref, sel_ref)
    gain_ref[...] = 1.0 + 0.5 * jnp.abs(tr + other)


def image_kernel(sz, step, *refs):
    z_ref, chip_ref, far_ref, hot_ref, near_ref, sel_ref, gain_ref, back_ref, vol_ref, tr_ref, mask_ref = refs[:11]
    basis = refs[11 : 12 + step]
    w_ref, part_ref = refs[12 + step :]
    nbp = sz.nbp
    other = neighbour_traces(sz, z_ref[:nbp], chip_ref[:nbp], far_ref[:nbp], hot_ref, near_ref, sel_ref)
    flux = gain_ref[...] * (tr_ref[...] - other)
    face = dot(back_ref[...], stack_rhs(split3(flux), 0))
    image = (vol_ref[...] + face) * mask_ref[...]
    w_ref[...] = image
    values = [full_sum(b[...] * image) for b in basis] + [full_sum(image * image)]
    part_ref[...] = partial_rows(values, sz.peers)


def finish_kernel(sz, *refs):
    red_ref, heads, searches = refs[0], refs[1 : 1 + ITERS], refs[1 + ITERS : 1 + 2 * ITERS]
    out_ref, hess_ref = refs[1 + 2 * ITERS :]
    lane = iota((1, 128), 1)

    def entry(row, i):
        return jnp.sum(jnp.where(lane == i, row, 0.0), axis=1, keepdims=True)

    start_value = entry(heads[0][...], 0)
    zero = jnp.zeros((1, 1), F32)
    upper = [[zero] * ITERS for _ in range(ITERS + 1)]
    for k in range(ITERS - 1):
        row = heads[k + 1][...]
        for i in range(k + 2):
            upper[i][k] = entry(row, i)
    scalars = total_scalars(red_ref[...], ITERS + 1)
    square = scalars[ITERS]
    for i in range(ITERS):
        upper[i][ITERS - 1] = scalars[i]
        square = square - scalars[i] * scalars[i]
    upper[ITERS][ITERS - 1] = jnp.sqrt(square + EPSILON)
    shape = hess_ref.shape
    row_id, col_id = iota(shape, 0), iota(shape, 1)
    hess = jnp.zeros(shape, F32)
    for i in range(ITERS + 1):
        for k in range(max(i - 1, 0), ITERS):
            hess = jnp.where((row_id == i) & (col_id == k), upper[i][k], hess)
    hess_ref[...] = hess
    right = [start_value] + [zero] * ITERS
    for k in range(ITERS):
        lead, below = upper[k][k], upper[k + 1][k]
        radius = jnp.sqrt(lead * lead + below * below)
        cosine, sine = lead / radius, below / radius
        for j in range(k, ITERS):
            top, low = upper[k][j], upper[k + 1][j]
            upper[k][j] = cosine * top + sine * low
            upper[k + 1][j] = cosine * low - sine * top
        top, low = right[k], right[k + 1]
        right[k] = cosine * top + sine * low
        right[k + 1] = cosine * low - sine * top
    coeffs = [None] * ITERS
    for k in reversed(range(ITERS)):
        acc = right[k]
        for j in range(k + 1, ITERS):
            acc = acc - upper[k][j] * coeffs[j]
        coeffs[k] = acc / upper[k][k]
    total = coeffs[0] * searches[0][: sz.nbp]
    for k in range(1, ITERS):
        total = total + coeffs[k] * searches[k][: sz.nbp]
    for v in range(sz.nv):
        out_ref[v] = total[: sz.nb, v * sz.ne : (v + 1) * sz.ne]


def call(kernel, name, out_shape, *args, specs=None, scratch=(), cost=None):
    return pl.pallas_call(
        kernel,
        name=name,
        out_shape=out_shape,
        in_specs=specs or [VMEM] * len(args),
        out_specs=jax.tree.map(lambda _: VMEM, out_shape),
        scratch_shapes=list(scratch),
        cost_estimate=cost,
        compiler_params=pltpu.CompilerParams(vmem_limit_bytes=24 * 2**20),
    )(*args)


def shape(*dims, dtype=F32):
    return jax.ShapeDtypeStruct(dims, dtype)


def copied(arrays):
    return [pltpu.VMEM(a.shape, a.dtype) for a in arrays] + [pltpu.SemaphoreType.DMA((len(arrays),))]


def body(
    peers, state_coeffs, residual_in, orders, neighbours, neighbour_face, orientation, precond, source,
    flux_jacobian, geometry, stiffness, trace_matrix,
):
    nv, nb, ne = state_coeffs.shape
    sz = Sizes(nv, nb, ne, trace_matrix.shape[1], peers)
    lanes, nbp, nqp = sz.lanes, sz.nbp, sz.nqp
    me = lax.axis_index(AXES).astype(jnp.int32).reshape(1)
    wide = shape(nbp, lanes)
    parts = shape(peers, 128)
    fetched = [residual_in, orders.reshape(1, ne)]
    start, mask, part = call(
        functools.partial(begin_kernel, sz), "begin", (wide, wide, parts), *fetched,
        specs=[ANY] * 2, scratch=copied(fetched),
    )
    fetched = [
        state_coeffs, neighbours, neighbour_face, orientation, source, flux_jacobian, geometry, stiffness,
        jnp.transpose(trace_matrix, (1, 0, 2)),
    ]
    state, hot, coup, sel, own, near, back = call(
        functools.partial(init_kernel, sz),
        "init",
        (
            wide,
            shape(3 * sz.pair, 4 * sz.pair, dtype=BF16),
            shape(4, nv, lanes),
            shape(8, lanes, dtype=jnp.int32),
            shape(4 * nqp + 3 * nbp, 6 * nbp, dtype=BF16),
            shape(8 * nqp, 6 * nbp, dtype=BF16),
            shape(nbp, 24 * nqp, dtype=BF16),
        ),
        me, *fetched, specs=[SMEM] + [ANY] * len(fetched), scratch=copied(fetched),
    )

    def exchange(rows):
        return lax.all_to_all(rows, AXES, 0, 0, tiled=True)

    on_chip = [(i, i ^ 1) for i in range(peers)]
    odd = range(1, peers - 1, 2)
    off_chip = [(i, i + 1) for i in odd] + [(i + 1, i) for i in odd]

    heads, searches, basis = [], [], []
    vec, gain = start, None
    for k in range(ITERS):
        red = exchange(part)
        if k == 0:
            search, new, head, blocks = call(
                functools.partial(precond_start_kernel, sz), "precond0",
                (shape(2 * nbp, lanes), wide, shape(1, 128), shape(*precond.shape, dtype=BF16)),
                red, vec, mask, state, precond, specs=[VMEM] * 4 + [ANY],
                scratch=[pltpu.SemaphoreType.DMA((7,))],
            )
        else:
            search, new, head = call(
                functools.partial(precond_kernel, sz, k), f"precond{k}", (wide, wide, shape(1, 128)),
                red, vec, mask, blocks, *basis,
            )
        basis = basis + [new]
        heads.append(head)
        searches.append(search)
        far = lax.ppermute(search, AXES, off_chip)
        chip = lax.ppermute(search, AXES, on_chip)
        vol, tr = call(
            functools.partial(local_kernel, sz), "local", (wide, shape(4 * nqp, lanes)), search, own, coup
        )
        if k == 0:
            gain = call(
                functools.partial(gain_kernel, sz), "gain", shape(4 * nqp, lanes),
                search, chip, far, hot, near, own, sel,
            )
        vec, part = call(
            functools.partial(image_kernel, sz, k), f"image{k}", (wide, parts),
            search, chip, far, hot, near, sel, gain, back, vol, tr, mask, *basis,
        )
    red = exchange(part)
    return call(
        functools.partial(finish_kernel, sz), "finish", (shape(nv, nb, ne), shape(ITERS + 1, ITERS)),
        red, *heads, *searches,
    )


def solution(mesh):
    placed = (
        P(None, None, AXES),
        P(None, None, AXES),
        P(AXES),
        P(None, AXES),
        P(None, AXES),
        P(None, AXES),
        P(None, AXES),
        P(None, None, AXES),
        P(None, None, None, AXES),
        P(None, None, AXES),
        P(),
        P(),
    )
    peers = 1
    for axis in AXES:
        peers *= mesh.shape[axis]
    return jax.shard_map(
        functools.partial(body, peers),
        mesh=mesh,
        in_specs=placed,
        out_specs=(P(None, None, AXES), P()),
        check_vma=False,
    )
```

```python
import functools

import jax
import jax.numpy as jnp
from jax import lax
from jax.experimental import pallas as pl
from jax.experimental.pallas import tpu as pltpu
from jax.sharding import PartitionSpec as P

ITERS = 6
EPSILON = 1e-06
AXES = ("dom", "grp")
F32 = jnp.float32
BF16 = jnp.bfloat16
CHUNK = 256
VMEM = pl.BlockSpec(memory_space=pltpu.VMEM)
ANY = pl.BlockSpec(memory_space=pl.ANY)
SMEM = pl.BlockSpec(memory_space=pltpu.SMEM)


def ceil_to(n, m):
    return -(-n // m) * m


def iota(shape, dim):
    return lax.broadcasted_iota(jnp.int32, shape, dim)


def split3(x):
    hi = x.astype(BF16).astype(F32)
    rest = x - hi
    mid = rest.astype(BF16).astype(F32)
    return hi, mid, rest - mid


def stack_rhs(parts, axis):
    hi, mid, lo = parts
    return jnp.concatenate([hi, mid, lo, hi, mid, hi], axis=axis).astype(BF16)


def stack_lhs(x):
    hi, mid, lo = split3(x)
    return jnp.concatenate([hi, hi, hi, mid, mid, lo], axis=1).astype(BF16)


def dot(a, b):
    return jnp.dot(a, b, preferred_element_type=F32)


def pad_rows(x, rows):
    return jnp.concatenate([x, jnp.zeros((rows - x.shape[0], x.shape[1]), x.dtype)], axis=0)


class Sizes:
    def __init__(self, nv, nb, ne, nq, peers):
        self.nv, self.nb, self.ne, self.nq, self.peers = nv, nb, ne, nq, peers
        self.nbp = ceil_to(nb, 8)
        self.nqp = ceil_to(nq, 8)
        self.lanes = nv * ne
        self.width = nv * nb
        self.kwidth = ceil_to(self.width, 128)
        self.pair = 2 * ne


def to_wide(read, sz):
    return pad_rows(jnp.concatenate([read(v) for v in range(sz.nv)], axis=1), sz.nbp)


def partial_rows(values, peers):
    lane = iota((1, 128), 1)
    row = jnp.zeros((1, 128), F32)
    for i, val in enumerate(values):
        row = jnp.where(lane == i, val, row)
    return jnp.broadcast_to(row, (peers, 128))


def full_sum(x):
    return jnp.sum(jnp.sum(x, axis=0, keepdims=True), axis=1, keepdims=True)


def total_scalars(red, count):
    row = jnp.sum(red, axis=0, keepdims=True)
    lane = iota((1, 128), 1)
    return [jnp.sum(jnp.where(lane == i, row, 0.0), axis=1, keepdims=True) for i in range(count)]


def fetch(pairs, sems):
    copies = [pltpu.make_async_copy(src, dst, sems.at[i]) for i, (src, dst) in enumerate(pairs)]
    for copy in copies:
        copy.start()
    for copy in copies:
        copy.wait()


def init_kernel(sz, me_ref, p_hbm, *refs):
    args, outs, held, sems, p_sem = refs[:11], refs[11:22], refs[22:33], refs[33], refs[34]
    blocks = pltpu.make_async_copy(p_hbm, outs[10], p_sem)
    blocks.start()
    fetch(list(zip(args, held)), sems)
    (res_ref, orders_ref, state_ref, nbr_ref, face_ref, orient_ref, source_ref, flux_ref, geo_ref, stiff_ref, trace_ref) = held
    start_ref, mask_ref, part_ref, state2_ref, hot_ref, coup_ref, sel_ref, own_ref, near_ref, back_ref = outs[:10]
    nv, nb, ne, nq, nbp, nqp = sz.nv, sz.nb, sz.ne, sz.nq, sz.nbp, sz.nqp
    orders = orders_ref[...]
    count = (orders + 1) * (orders + 2) * (orders + 3) // 6
    count = jnp.concatenate([count] * nv, axis=1)
    mask = (iota((nbp, sz.lanes), 0) < count).astype(F32)
    mask_ref[...] = mask
    start = to_wide(lambda v: res_ref[v], sz) * mask
    start_ref[...] = start
    part_ref[...] = partial_rows([full_sum(start * start)], sz.peers)
    state2_ref[...] = to_wide(lambda v: state_ref[v], sz)

    me = me_ref[0]
    nbr = nbr_ref[...]
    rel = jnp.where(nbr >= 0, nbr - me * ne + ne, -4 * ne)
    cols = jnp.concatenate(
        [piece for f in range(4) for piece in (rel[f : f + 1], rel[f : f + 1] + 3 * ne * (rel[f : f + 1] >= 0).astype(jnp.int32))],
        axis=1,
    )
    rows = iota((3 * sz.pair, 4 * sz.pair), 0)
    block = rows // sz.pair
    even = lax.rem(me, 2) == 0
    chip_side = jnp.where(even, 2, 0)
    side = jnp.where(block == 0, 1, jnp.where(block == 1, chip_side, 2 - chip_side))
    inner = rows - block * sz.pair
    parity = (inner >= ne).astype(jnp.int32)
    code = side * ne + inner - parity * ne + 3 * ne * parity
    hot_ref[...] = (code == cols).astype(F32).astype(BF16)

    face = face_ref[...]
    orient = orient_ref[...]
    flip = (orient >= 3).astype(jnp.int32)
    choice = flip * 4 + face
    turn = orient - 3 * flip
    sel_ref[...] = jnp.concatenate([jnp.concatenate([choice, turn], axis=0)] * nv, axis=1)

    for k in range(3):
        pieces = []
        for w in range(nv):
            tile = jnp.zeros((nv, ne), F32)
            for d in range(3):
                tile = tile + geo_ref[d, k : k + 1, :] * flux_ref[d, w]
            pieces.append(tile if w == 0 else jnp.concatenate([tile[w:], tile[:w]], axis=0))
        coup_ref[k] = jnp.concatenate(pieces, axis=1)
    pieces = []
    for w in range(nv):
        tile = source_ref[w]
        pieces.append(tile if w == 0 else jnp.concatenate([tile[w:], tile[:w]], axis=0))
    coup_ref[3] = jnp.concatenate(pieces, axis=1)

    def pad2(x, rows):
        x = jnp.concatenate([x, jnp.zeros((x.shape[0], nbp - x.shape[1]), F32)], axis=1)
        return pad_rows(x, rows)

    traces = [trace_ref[:, f, :] for f in range(4)]
    plain = [pad2(t, nqp) for t in traces]
    flipped = [
        pad2(jnp.concatenate([t[q : q + 1] for q in reversed(range(nq))], axis=0), nqp) for t in traces
    ]
    volume = [pad2(stiff_ref[d], nbp) for d in range(3)]
    own_ref[...] = stack_lhs(jnp.concatenate(plain + volume, axis=0))
    near_ref[...] = stack_lhs(jnp.concatenate(plain + flipped, axis=0))
    back_ref[...] = stack_lhs(jnp.concatenate(plain, axis=0).T)
    blocks.wait()


def apply_blocks(sz, vec, mask, blocks_ref):
    nb, ne, nv, width = sz.nb, sz.ne, sz.nv, sz.width
    tall = jnp.concatenate([vec[:nb, v * ne : (v + 1) * ne] for v in range(nv)], axis=0)
    turned = pad_rows(tall, CHUNK).T
    amount = lax.rem(iota((ne, 1), 0) * width, CHUNK)
    bit = 1
    while bit < CHUNK:
        if any(e * width % CHUNK & bit for e in range(ne)):
            turned = jnp.where((amount & bit) != 0, pltpu.roll(turned, bit, 1), turned)
        bit *= 2
    total = ne * width
    acc = [jnp.zeros((8, width), F32)] * (ne // 8)
    for low in range(0, total, CHUNK):
        high = min(low + CHUNK, total)
        first, last = low // width // 8, (high - 1) // width // 8 + 1
        size = (8 * (last - first), high - low)
        entry = iota(size, 1) + low - (iota(size, 0) + 8 * first) * width
        lhs = jnp.where((entry >= 0) & (entry < width), turned[8 * first : 8 * last, : high - low], 0.0)
        out = lax.dot_general(
            lhs.astype(BF16), blocks_ref[:, low:high], (((1,), (1,)), ((), ())), preferred_element_type=F32
        )
        for g in range(first, last):
            acc[g] = acc[g] + out[8 * (g - first) : 8 * (g - first + 1)]
    done = jnp.concatenate(acc, axis=0)
    done = jnp.concatenate([done, jnp.zeros((ne, CHUNK - width), F32)], axis=1).T
    wide = jnp.concatenate([done[v * nb : (v + 1) * nb] for v in range(nv)], axis=1)
    return pad_rows(wide, sz.nbp) * mask


def precond_start_kernel(sz, red_ref, vec_ref, mask_ref, blocks_ref, state_ref, z_ref, v_ref, h_ref):
    norm = jnp.sqrt(total_scalars(red_ref[...], 1)[0] + EPSILON)
    new = vec_ref[...] / norm
    v_ref[...] = new
    h_ref[...] = partial_rows([norm], 1)
    z_ref[: sz.nbp] = apply_blocks(sz, new, mask_ref[...], blocks_ref)
    z_ref[sz.nbp :] = state_ref[...]


def precond_kernel(sz, step, *refs):
    red_ref, vec_ref, mask_ref, blocks_ref = refs[:4]
    basis = refs[4 : 4 + step]
    z_ref, v_ref, h_ref = refs[4 + step :]
    vec = vec_ref[...]
    scalars = total_scalars(red_ref[...], step + 1)
    proj, square = scalars[:step], scalars[step]
    for h, b in zip(proj, basis):
        vec = vec - h * b[...]
        square = square - h * h
    norm = jnp.sqrt(square + EPSILON)
    new = vec / norm
    v_ref[...] = new
    h_ref[...] = partial_rows(proj + [norm], 1)
    z_ref[...] = apply_blocks(sz, new, mask_ref[...], blocks_ref)


def roll_blocks(x, blocks, ne):
    shift = blocks * ne
    if shift == 0:
        return x
    return jnp.concatenate([x[:, shift:], x[:, :shift]], axis=1)


def local_kernel(sz, z_ref, own_ref, coup_ref, vol_ref, tr_ref):
    search = z_ref[: sz.nbp]
    out = dot(own_ref[...], stack_rhs(split3(search), 0))
    faces = 4 * sz.nqp
    tr_ref[...] = out[:faces]
    acc = jnp.zeros((sz.nbp, sz.lanes), F32)
    for d in range(4):
        moved = search if d == 3 else out[faces + d * sz.nbp : faces + (d + 1) * sz.nbp]
        for s in range(sz.nv):
            acc = acc + coup_ref[d, s : s + 1, :] * roll_blocks(moved, s, sz.ne)
    vol_ref[...] = acc


def neighbour_traces(sz, own, chip, far, hot_ref, near_ref, sel_ref):
    nbp, nqp, pair = sz.nbp, sz.nqp, sz.pair
    parts = [split3(x) for x in (own, chip, far)]
    pairs = sz.lanes // pair
    lhs = jnp.concatenate(
        [
            jnp.concatenate([parts[side][n][:, p * pair : (p + 1) * pair] for side in range(3)], axis=1)
            for n in range(3)
            for p in range(pairs)
        ],
        axis=0,
    ).astype(BF16)
    got = dot(lhs, hot_ref[...])
    result = []
    for f in range(4):
        picked = [
            jnp.concatenate(
                [
                    got[(n * pairs + p) * nbp : (n * pairs + p + 1) * nbp, f * pair : (f + 1) * pair]
                    for p in range(pairs)
                ],
                axis=1,
            )
            for n in range(3)
        ]
        every = dot(near_ref[...], stack_rhs(picked, 0))
        choice = sel_ref[f : f + 1, :]
        turn = sel_ref[4 + f : 5 + f, :]
        tr = every[:nqp]
        for g in range(1, 8):
            tr = jnp.where(choice == g, every[g * nqp : (g + 1) * nqp], tr)
        nq, third = sz.nq, sz.nq // 3
        fill = tr[nq:]
        once = jnp.concatenate([tr[third:nq], tr[:third], fill], axis=0)
        twice = jnp.concatenate([tr[2 * third : nq], tr[: 2 * third], fill], axis=0)
        result.append(jnp.where(turn == 0, tr, jnp.where(turn == 1, once, twice)))
    return jnp.concatenate(result, axis=0)


def gain_kernel(sz, z_ref, chip_ref, far_ref, hot_ref, near_ref, own_ref, sel_ref, gain_ref):
    nbp = sz.nbp
    state = z_ref[nbp:]
    tr = dot(own_ref[: 4 * sz.nqp], stack_rhs(split3(state), 0))
    other = neighbour_traces(sz, state, chip_ref[nbp:], far_ref[nbp:], hot_ref, near_ref, sel_ref)
    gain_ref[...] = 1.0 + 0.5 * jnp.abs(tr + other)


def image_kernel(sz, step, *refs):
    z_ref, chip_ref, far_ref, hot_ref, near_ref, sel_ref, gain_ref, back_ref, vol_ref, tr_ref, mask_ref = refs[:11]
    basis = refs[11 : 12 + step]
    w_ref, part_ref = refs[12 + step :]
    nbp = sz.nbp
    other = neighbour_traces(sz, z_ref[:nbp], chip_ref[:nbp], far_ref[:nbp], hot_ref, near_ref, sel_ref)
    flux = gain_ref[...] * (tr_ref[...] - other)
    face = dot(back_ref[...], stack_rhs(split3(flux), 0))
    image = (vol_ref[...] + face) * mask_ref[...]
    w_ref[...] = image
    values = [full_sum(b[...] * image) for b in basis] + [full_sum(image * image)]
    part_ref[...] = partial_rows(values, sz.peers)


def finish_kernel(sz, *refs):
    red_ref, heads, searches = refs[0], refs[1 : 1 + ITERS], refs[1 + ITERS : 1 + 2 * ITERS]
    out_ref, hess_ref = refs[1 + 2 * ITERS :]
    lane = iota((1, 128), 1)

    def entry(row, i):
        return jnp.sum(jnp.where(lane == i, row, 0.0), axis=1, keepdims=True)

    start_value = entry(heads[0][...], 0)
    zero = jnp.zeros((1, 1), F32)
    upper = [[zero] * ITERS for _ in range(ITERS + 1)]
    for k in range(ITERS - 1):
        row = heads[k + 1][...]
        for i in range(k + 2):
            upper[i][k] = entry(row, i)
    scalars = total_scalars(red_ref[...], ITERS + 1)
    square = scalars[ITERS]
    for i in range(ITERS):
        upper[i][ITERS - 1] = scalars[i]
        square = square - scalars[i] * scalars[i]
    upper[ITERS][ITERS - 1] = jnp.sqrt(square + EPSILON)
    shape = hess_ref.shape
    row_id, col_id = iota(shape, 0), iota(shape, 1)
    hess = jnp.zeros(shape, F32)
    for i in range(ITERS + 1):
        for k in range(max(i - 1, 0), ITERS):
            hess = jnp.where((row_id == i) & (col_id == k), upper[i][k], hess)
    hess_ref[...] = hess
    right = [start_value] + [zero] * ITERS
    for k in range(ITERS):
        lead, below = upper[k][k], upper[k + 1][k]
        radius = jnp.sqrt(lead * lead + below * below)
        cosine, sine = lead / radius, below / radius
        for j in range(k, ITERS):
            top, low = upper[k][j], upper[k + 1][j]
            upper[k][j] = cosine * top + sine * low
            upper[k + 1][j] = cosine * low - sine * top
        top, low = right[k], right[k + 1]
        right[k] = cosine * top + sine * low
        right[k + 1] = cosine * low - sine * top
    coeffs = [None] * ITERS
    for k in reversed(range(ITERS)):
        acc = right[k]
        for j in range(k + 1, ITERS):
            acc = acc - upper[k][j] * coeffs[j]
        coeffs[k] = acc / upper[k][k]
    total = coeffs[0] * searches[0][: sz.nbp]
    for k in range(1, ITERS):
        total = total + coeffs[k] * searches[k][: sz.nbp]
    for v in range(sz.nv):
        out_ref[v] = total[: sz.nb, v * sz.ne : (v + 1) * sz.ne]


def call(kernel, name, out_shape, *args, specs=None, scratch=(), limit=24 * 2**20):
    return pl.pallas_call(
        kernel,
        name=name,
        out_shape=out_shape,
        in_specs=specs or [VMEM] * len(args),
        out_specs=jax.tree.map(lambda _: VMEM, out_shape),
        scratch_shapes=list(scratch),
        compiler_params=pltpu.CompilerParams(vmem_limit_bytes=limit),
    )(*args)


def shape(*dims, dtype=F32):
    return jax.ShapeDtypeStruct(dims, dtype)


def copied(arrays):
    return [pltpu.VMEM(a.shape, a.dtype) for a in arrays] + [pltpu.SemaphoreType.DMA((len(arrays),))]


def body(
    peers, state_coeffs, residual_in, orders, neighbours, neighbour_face, orientation, precond, source,
    flux_jacobian, geometry, stiffness, trace_matrix,
):
    nv, nb, ne = state_coeffs.shape
    sz = Sizes(nv, nb, ne, trace_matrix.shape[1], peers)
    lanes, nbp, nqp = sz.lanes, sz.nbp, sz.nqp
    me = lax.axis_index(AXES).astype(jnp.int32).reshape(1)
    wide = shape(nbp, lanes)
    parts = shape(peers, 128)
    fetched = [
        residual_in, orders.reshape(1, ne), state_coeffs, neighbours, neighbour_face, orientation, source, flux_jacobian,
        geometry, stiffness, jnp.transpose(trace_matrix, (1, 0, 2)),
    ]
    start, mask, part, state, hot, coup, sel, own, near, back, blocks = call(
        functools.partial(init_kernel, sz),
        "init",
        (
            wide, wide, parts, wide,
            shape(3 * sz.pair, 4 * sz.pair, dtype=BF16),
            shape(4, nv, lanes),
            shape(8, lanes, dtype=jnp.int32),
            shape(4 * nqp + 3 * nbp, 6 * nbp, dtype=BF16),
            shape(8 * nqp, 6 * nbp, dtype=BF16),
            shape(nbp, 24 * nqp, dtype=BF16),
            shape(*precond.shape, dtype=BF16),
        ),
        me, *[pltpu.with_memory_space_constraint(a, pltpu.HBM) for a in [precond] + fetched],
        specs=[SMEM] + [ANY] * (1 + len(fetched)), scratch=copied(fetched) + [pltpu.SemaphoreType.DMA],
    )

    def exchange(rows):
        return lax.all_to_all(rows, AXES, 0, 0, tiled=True)

    on_chip = [(i, i ^ 1) for i in range(peers)]
    odd = range(1, peers - 1, 2)
    off_chip = [(i, i + 1) for i in odd] + [(i + 1, i) for i in odd]

    heads, searches, basis = [], [], []
    vec, gain = start, None
    for k in range(ITERS):
        red = exchange(part)
        kernel = functools.partial(precond_kernel, sz, k) if k else functools.partial(precond_start_kernel, sz)
        extra = basis if k else [state]
        search, new, head = call(
            kernel, f"precond{k}", (shape(nbp if k else 2 * nbp, lanes), wide, shape(1, 128)),
            red, vec, mask, blocks, *extra,
        )
        basis = basis + [new]
        heads.append(head)
        searches.append(search)
        far = lax.ppermute(search, AXES, off_chip)
        chip = lax.ppermute(search, AXES, on_chip)
        vol, tr = call(
            functools.partial(local_kernel, sz), "local", (wide, shape(4 * nqp, lanes)), search, own, coup
        )
        if k == 0:
            gain = call(
                functools.partial(gain_kernel, sz), "gain", shape(4 * nqp, lanes),
                search, chip, far, hot, near, own, sel,
            )
        vec, part = call(
            functools.partial(image_kernel, sz, k), f"image{k}", (wide, parts),
            search, chip, far, hot, near, sel, gain, back, vol, tr, mask, *basis,
        )
    red = exchange(part)
    return call(
        functools.partial(finish_kernel, sz), "finish", (shape(nv, nb, ne), shape(ITERS + 1, ITERS)),
        red, *heads, *searches,
    )


def solution(mesh):
    placed = (
        P(None, None, AXES),
        P(None, None, AXES),
        P(AXES),
        P(None, AXES),
        P(None, AXES),
        P(None, AXES),
        P(None, AXES),
        P(None, None, AXES),
        P(None, None, None, AXES),
        P(None, None, AXES),
        P(),
        P(),
    )
    peers = 1
    for axis in AXES:
        peers *= mesh.shape[axis]
    return jax.shard_map(
        functools.partial(body, peers),
        mesh=mesh,
        in_specs=placed,
        out_specs=(P(None, None, AXES), P()),
        check_vma=False,
    )
```

```python
import functools

import jax
import jax.numpy as jnp
from jax import lax
from jax.experimental import pallas as pl
from jax.experimental.pallas import tpu as pltpu
from jax.sharding import PartitionSpec as P

ITERS = 6
EPSILON = 1e-06
AXES = ("dom", "grp")
F32 = jnp.float32
BF16 = jnp.bfloat16
CHUNK = 256
VMEM = pl.BlockSpec(memory_space=pltpu.VMEM)
ANY = pl.BlockSpec(memory_space=pl.ANY)
SMEM = pl.BlockSpec(memory_space=pltpu.SMEM)


def ceil_to(n, m):
    return -(-n // m) * m


def iota(shape, dim):
    return lax.broadcasted_iota(jnp.int32, shape, dim)


def split3(x):
    hi = x.astype(BF16).astype(F32)
    rest = x - hi
    mid = rest.astype(BF16).astype(F32)
    return hi, mid, rest - mid


def stack_rhs(parts, axis):
    hi, mid, lo = parts
    return jnp.concatenate([hi, mid, lo, hi, mid, hi], axis=axis).astype(BF16)


def stack_lhs(x):
    hi, mid, lo = split3(x)
    return jnp.concatenate([hi, hi, hi, mid, mid, lo], axis=1).astype(BF16)


def dot(a, b):
    return jnp.dot(a, b, preferred_element_type=F32)


def pad_rows(x, rows):
    return jnp.concatenate([x, jnp.zeros((rows - x.shape[0], x.shape[1]), x.dtype)], axis=0)


class Sizes:
    def __init__(self, nv, nb, ne, nq, peers):
        self.nv, self.nb, self.ne, self.nq, self.peers = nv, nb, ne, nq, peers
        self.nbp = ceil_to(nb, 8)
        self.nqp = ceil_to(nq, 8)
        self.lanes = nv * ne
        self.width = nv * nb
        self.kwidth = ceil_to(self.width, 128)
        self.pair = 2 * ne


def to_wide(read, sz):
    return pad_rows(jnp.concatenate([read(v) for v in range(sz.nv)], axis=1), sz.nbp)


def partial_rows(values, peers):
    lane = iota((1, 128), 1)
    row = jnp.zeros((1, 128), F32)
    for i, val in enumerate(values):
        row = jnp.where(lane == i, val, row)
    return jnp.broadcast_to(row, (peers, 128))


def full_sum(x):
    return jnp.sum(jnp.sum(x, axis=0, keepdims=True), axis=1, keepdims=True)


def total_scalars(red, count):
    row = jnp.sum(red, axis=0, keepdims=True)
    return [row[:, i : i + 1] for i in range(count)]


def fetch(pairs, sems):
    copies = [pltpu.make_async_copy(src, dst, sems.at[i]) for i, (src, dst) in enumerate(pairs)]
    for copy in copies:
        copy.start()
    for copy in copies:
        copy.wait()


def init_kernel(sz, me_ref, p_hbm, *refs):
    args, outs, held, sems, p_sem = refs[:11], refs[11:22], refs[22:33], refs[33], refs[34]
    blocks = pltpu.make_async_copy(p_hbm, outs[10], p_sem)
    blocks.start()
    fetch(list(zip(args, held)), sems)
    (res_ref, orders_ref, state_ref, nbr_ref, face_ref, orient_ref, source_ref, flux_ref, geo_ref, stiff_ref, trace_ref) = held
    start_ref, mask_ref, part_ref, state2_ref, hot_ref, coup_ref, sel_ref, own_ref, near_ref, back_ref = outs[:10]
    nv, nb, ne, nq, nbp, nqp = sz.nv, sz.nb, sz.ne, sz.nq, sz.nbp, sz.nqp
    orders = orders_ref[...]
    count = (orders + 1) * (orders + 2) * (orders + 3) // 6
    count = jnp.concatenate([count] * nv, axis=1)
    mask = (iota((nbp, sz.lanes), 0) < count).astype(F32)
    mask_ref[...] = mask
    start = to_wide(lambda v: res_ref[v], sz) * mask
    start_ref[...] = start
    part_ref[...] = partial_rows([full_sum(start * start)], sz.peers)
    state2_ref[...] = to_wide(lambda v: state_ref[v], sz)

    me = me_ref[0]
    nbr = nbr_ref[...]
    rel = jnp.where(nbr >= 0, nbr - me * ne + ne, -4 * ne)
    face, orient = face_ref[...], orient_ref[...]
    flip = (orient >= 3).astype(jnp.int32)
    choice, turn = flip * 4 + face, orient - 3 * flip

    def by_face(x):
        return jnp.concatenate([x[f : f + 1] for f in range(4)], axis=1)

    sel_ref[...] = jnp.concatenate([by_face(choice), by_face(turn)], axis=0)
    cols = by_face(rel)
    rows = iota((4 * ne, 4 * ne), 0)
    block = rows // ne
    inner = rows - block * ne
    chip_side = jnp.where(lax.rem(me, 2) == 0, 2, 0)
    for parity in range(2):
        own_block, chip_block, far_block = parity, 1 - parity, 2 + parity
        side = jnp.where(block == own_block, 1, jnp.where(block == chip_block, chip_side, 2 - chip_side))
        code = jnp.where(block == 5 - far_block, -ne, side * ne + inner)
        hot_ref[parity] = (code == cols).astype(F32).astype(BF16)

    for k in range(3):
        pieces = []
        for w in range(nv):
            tile = jnp.zeros((nv, ne), F32)
            for d in range(3):
                tile = tile + geo_ref[d, k : k + 1, :] * flux_ref[d, w]
            pieces.append(tile if w == 0 else jnp.concatenate([tile[w:], tile[:w]], axis=0))
        coup_ref[k] = jnp.concatenate(pieces, axis=1)
    pieces = []
    for w in range(nv):
        tile = source_ref[w]
        pieces.append(tile if w == 0 else jnp.concatenate([tile[w:], tile[:w]], axis=0))
    coup_ref[3] = jnp.concatenate(pieces, axis=1)

    def pad2(x, rows):
        x = jnp.concatenate([x, jnp.zeros((x.shape[0], nbp - x.shape[1]), F32)], axis=1)
        return pad_rows(x, rows)

    traces = [trace_ref[:, f, :] for f in range(4)]
    plain = [pad2(t, nqp) for t in traces]
    flipped = [
        pad2(jnp.concatenate([t[q : q + 1] for q in reversed(range(nq))], axis=0), nqp) for t in traces
    ]
    volume = [pad2(stiff_ref[d], nbp) for d in range(3)]
    own_ref[...] = stack_lhs(jnp.concatenate(plain + volume, axis=0))
    near_ref[...] = stack_lhs(jnp.concatenate(plain + flipped, axis=0))
    back_ref[...] = stack_lhs(jnp.concatenate(plain, axis=0).T)
    blocks.wait()


def apply_blocks(sz, vec, mask, blocks_ref):
    nb, ne, nv, width = sz.nb, sz.ne, sz.nv, sz.width
    tall = jnp.concatenate([vec[:nb, v * ne : (v + 1) * ne] for v in range(nv)], axis=0)
    turned = pad_rows(tall, CHUNK).T
    turned = jnp.concatenate(
        [pltpu.roll(turned[g : g + 8], g * width % CHUNK, 1) if g else turned[:8] for g in range(0, ne, 8)], axis=0
    )
    row = iota((ne, 1), 0)
    for bit in (1, 2, 4):
        turned = jnp.where((row & bit) != 0, pltpu.roll(turned, bit * width % CHUNK, 1), turned)
    total = ne * width
    acc = [jnp.zeros((8, width), F32)] * (ne // 8)
    for low in range(0, total, CHUNK):
        high = min(low + CHUNK, total)
        first, last = low // width // 8, (high - 1) // width // 8 + 1
        size = (8 * (last - first), high - low)
        entry = iota(size, 1) + low - (iota(size, 0) + 8 * first) * width
        lhs = jnp.where((entry >= 0) & (entry < width), turned[8 * first : 8 * last, : high - low], 0.0)
        out = lax.dot_general(
            lhs.astype(BF16), blocks_ref[:, low:high], (((1,), (1,)), ((), ())), preferred_element_type=F32
        )
        for g in range(first, last):
            acc[g] = acc[g] + out[8 * (g - first) : 8 * (g - first + 1)]
    done = jnp.concatenate(acc, axis=0)
    done = jnp.concatenate([done, jnp.zeros((ne, CHUNK - width), F32)], axis=1).T
    wide = jnp.concatenate([done[v * nb : (v + 1) * nb] for v in range(nv)], axis=1)
    return pad_rows(wide, sz.nbp) * mask


def precond_start_kernel(sz, red_ref, vec_ref, mask_ref, blocks_ref, state_ref, z_ref, v_ref, h_ref):
    norm = jnp.sqrt(total_scalars(red_ref[...], 1)[0] + EPSILON)
    new = vec_ref[...] * (1.0 / norm)
    v_ref[...] = new
    h_ref[...] = partial_rows([norm], 1)
    z_ref[: sz.nbp] = apply_blocks(sz, new, mask_ref[...], blocks_ref)
    z_ref[sz.nbp :] = state_ref[...]


def precond_kernel(sz, step, *refs):
    red_ref, vec_ref, mask_ref, blocks_ref = refs[:4]
    basis = refs[4 : 4 + step]
    z_ref, v_ref, h_ref = refs[4 + step :]
    vec = vec_ref[...]
    scalars = total_scalars(red_ref[...], step + 1)
    proj, square = scalars[:step], scalars[step]
    for h, b in zip(proj, basis):
        vec = vec - h * b[...]
        square = square - h * h
    norm = jnp.sqrt(square + EPSILON)
    new = vec * (1.0 / norm)
    v_ref[...] = new
    h_ref[...] = partial_rows(proj + [norm], 1)
    z_ref[...] = apply_blocks(sz, new, mask_ref[...], blocks_ref)


def roll_blocks(x, blocks, ne):
    shift = blocks * ne
    if shift == 0:
        return x
    return jnp.concatenate([x[:, shift:], x[:, :shift]], axis=1)


def local_kernel(sz, z_ref, own_ref, coup_ref, vol_ref, tr_ref):
    search = z_ref[: sz.nbp]
    out = dot(own_ref[...], stack_rhs(split3(search), 0))
    faces = 4 * sz.nqp
    tr_ref[...] = out[:faces]
    acc = jnp.zeros((sz.nbp, sz.lanes), F32)
    for d in range(4):
        moved = search if d == 3 else out[faces + d * sz.nbp : faces + (d + 1) * sz.nbp]
        for s in range(sz.nv):
            acc = acc + coup_ref[d, s : s + 1, :] * roll_blocks(moved, s, sz.ne)
    vol_ref[...] = acc


def neighbour_traces(sz, own, chip, far, hot_ref, near_ref, sel_ref):
    nbp, nqp, ne, pair = sz.nbp, sz.nqp, sz.ne, sz.pair
    pairs, cols = sz.lanes // pair, 4 * ne
    low_half = iota((1, pair), 1) < ne
    owns, chips, fars = split3(own), split3(chip), split3(far)
    lhs = ([], [])
    for n in range(3):
        for p in range(pairs):
            mine, theirs, away = (x[n][:, p * pair : (p + 1) * pair] for x in (owns, chips, fars))
            theirs = pltpu.roll(theirs, ne, 1)
            lhs[0].append(jnp.concatenate([jnp.where(low_half, mine, theirs), away], axis=1))
            lhs[1].append(jnp.concatenate([jnp.where(low_half, theirs, mine), away], axis=1))
    got = [dot(jnp.concatenate(lhs[i], axis=0).astype(BF16), hot_ref[i]) for i in range(2)]
    picked = [
        jnp.concatenate(
            [got[v % 2][(n * pairs + v // 2) * nbp : (n * pairs + v // 2 + 1) * nbp] for v in range(sz.nv)], axis=1
        )
        for n in range(3)
    ]
    every = dot(near_ref[...], stack_rhs(picked, 0))
    choice, turn = sel_ref[0:1, :], sel_ref[1:2, :]
    is_choice = [choice == g for g in range(8)]
    nq, third = sz.nq, sz.nq // 3
    seen = []
    for v in range(sz.nv):
        mine = every[:, v * cols : (v + 1) * cols]
        tr = mine[:nqp]
        for g in range(1, 8):
            tr = jnp.where(is_choice[g], mine[g * nqp : (g + 1) * nqp], tr)
        fill = tr[nq:]
        once = jnp.concatenate([tr[third:nq], tr[:third], fill], axis=0)
        twice = jnp.concatenate([tr[2 * third : nq], tr[: 2 * third], fill], axis=0)
        seen.append(jnp.where(turn == 0, tr, jnp.where(turn == 1, once, twice)))
    result = []
    for f in range(4):
        start = f // 2 * pair
        blocks = []
        for p in range(pairs):
            first, second = (seen[2 * p + i][:, start : start + pair] for i in range(2))
            if f % 2 == 0:
                second = pltpu.roll(second, ne, 1)
            else:
                first = pltpu.roll(first, ne, 1)
            blocks.append(jnp.where(low_half, first, second))
        result.append(jnp.concatenate(blocks, axis=1))
    return jnp.concatenate(result, axis=0)


def gain_kernel(sz, z_ref, chip_ref, far_ref, hot_ref, near_ref, own_ref, sel_ref, gain_ref):
    nbp = sz.nbp
    state = z_ref[nbp:]
    tr = dot(own_ref[: 4 * sz.nqp], stack_rhs(split3(state), 0))
    other = neighbour_traces(sz, state, chip_ref[nbp:], far_ref[nbp:], hot_ref, near_ref, sel_ref)
    gain_ref[...] = 1.0 + 0.5 * jnp.abs(tr + other)


def image_kernel(sz, step, *refs):
    z_ref, chip_ref, far_ref, hot_ref, near_ref, sel_ref, gain_ref, back_ref, vol_ref, tr_ref, mask_ref = refs[:11]
    basis = refs[11 : 12 + step]
    w_ref, part_ref = refs[12 + step :]
    nbp = sz.nbp
    other = neighbour_traces(sz, z_ref[:nbp], chip_ref[:nbp], far_ref[:nbp], hot_ref, near_ref, sel_ref)
    flux = gain_ref[...] * (tr_ref[...] - other)
    face = dot(back_ref[...], stack_rhs(split3(flux), 0))
    image = (vol_ref[...] + face) * mask_ref[...]
    w_ref[...] = image
    values = [full_sum(b[...] * image) for b in basis] + [full_sum(image * image)]
    part_ref[...] = partial_rows(values, sz.peers)


def finish_kernel(sz, *refs):
    red_ref, heads, searches = refs[0], refs[1 : 1 + ITERS], refs[1 + ITERS : 1 + 2 * ITERS]
    out_ref, hess_ref = refs[1 + 2 * ITERS :]
    lane = iota((1, 128), 1)

    def entry(row, i):
        return jnp.sum(jnp.where(lane == i, row, 0.0), axis=1, keepdims=True)

    start_value = entry(heads[0][...], 0)
    zero = jnp.zeros((1, 1), F32)
    upper = [[zero] * ITERS for _ in range(ITERS + 1)]
    for k in range(ITERS - 1):
        row = heads[k + 1][...]
        for i in range(k + 2):
            upper[i][k] = entry(row, i)
    scalars = total_scalars(red_ref[...], ITERS + 1)
    square = scalars[ITERS]
    for i in range(ITERS):
        upper[i][ITERS - 1] = scalars[i]
        square = square - scalars[i] * scalars[i]
    upper[ITERS][ITERS - 1] = jnp.sqrt(square + EPSILON)
    shape = hess_ref.shape
    row_id, col_id = iota(shape, 0), iota(shape, 1)
    hess = jnp.zeros(shape, F32)
    for i in range(ITERS + 1):
        for k in range(max(i - 1, 0), ITERS):
            hess = jnp.where((row_id == i) & (col_id == k), upper[i][k], hess)
    hess_ref[...] = hess
    right = [start_value] + [zero] * ITERS
    for k in range(ITERS):
        lead, below = upper[k][k], upper[k + 1][k]
        radius = jnp.sqrt(lead * lead + below * below)
        cosine, sine = lead / radius, below / radius
        for j in range(k, ITERS):
            top, low = upper[k][j], upper[k + 1][j]
            upper[k][j] = cosine * top + sine * low
            upper[k + 1][j] = cosine * low - sine * top
        top, low = right[k], right[k + 1]
        right[k] = cosine * top + sine * low
        right[k + 1] = cosine * low - sine * top
    coeffs = [None] * ITERS
    for k in reversed(range(ITERS)):
        acc = right[k]
        for j in range(k + 1, ITERS):
            acc = acc - upper[k][j] * coeffs[j]
        coeffs[k] = acc / upper[k][k]
    total = coeffs[0] * searches[0][: sz.nbp]
    for k in range(1, ITERS):
        total = total + coeffs[k] * searches[k][: sz.nbp]
    for v in range(sz.nv):
        out_ref[v] = total[: sz.nb, v * sz.ne : (v + 1) * sz.ne]


def call(kernel, name, out_shape, *args, specs=None, scratch=(), limit=24 * 2**20):
    return pl.pallas_call(
        kernel,
        name=name,
        out_shape=out_shape,
        in_specs=specs or [VMEM] * len(args),
        out_specs=jax.tree.map(lambda _: VMEM, out_shape),
        scratch_shapes=list(scratch),
        compiler_params=pltpu.CompilerParams(vmem_limit_bytes=limit),
    )(*args)


def shape(*dims, dtype=F32):
    return jax.ShapeDtypeStruct(dims, dtype)


def copied(arrays):
    return [pltpu.VMEM(a.shape, a.dtype) for a in arrays] + [pltpu.SemaphoreType.DMA((len(arrays),))]


def body(
    peers, state_coeffs, residual_in, orders, neighbours, neighbour_face, orientation, precond, source,
    flux_jacobian, geometry, stiffness, trace_matrix,
):
    nv, nb, ne = state_coeffs.shape
    sz = Sizes(nv, nb, ne, trace_matrix.shape[1], peers)
    lanes, nbp, nqp = sz.lanes, sz.nbp, sz.nqp
    me = lax.axis_index(AXES).astype(jnp.int32).reshape(1)
    wide = shape(nbp, lanes)
    parts = shape(peers, 128)
    fetched = [
        residual_in, orders.reshape(1, ne), state_coeffs, neighbours, neighbour_face, orientation, source, flux_jacobian,
        geometry, stiffness, jnp.transpose(trace_matrix, (1, 0, 2)),
    ]
    start, mask, part, state, hot, coup, sel, own, near, back, blocks = call(
        functools.partial(init_kernel, sz),
        "init",
        (
            wide, wide, parts, wide,
            shape(2, 4 * ne, 4 * ne, dtype=BF16),
            shape(4, nv, lanes),
            shape(2, 4 * ne, dtype=jnp.int32),
            shape(4 * nqp + 3 * nbp, 6 * nbp, dtype=BF16),
            shape(8 * nqp, 6 * nbp, dtype=BF16),
            shape(nbp, 24 * nqp, dtype=BF16),
            shape(*precond.shape, dtype=BF16),
        ),
        me, *[pltpu.with_memory_space_constraint(a, pltpu.HBM) for a in [precond] + fetched],
        specs=[SMEM] + [ANY] * (1 + len(fetched)), scratch=copied(fetched) + [pltpu.SemaphoreType.DMA],
    )

    def exchange(rows):
        return lax.all_to_all(rows, AXES, 0, 0, tiled=True)

    on_chip = [(i, i ^ 1) for i in range(peers)]
    odd = range(1, peers - 1, 2)
    off_chip = [(i, i + 1) for i in odd] + [(i + 1, i) for i in odd]

    heads, searches, basis = [], [], []
    vec, gain = start, None
    for k in range(ITERS):
        red = exchange(part)
        kernel = functools.partial(precond_kernel, sz, k) if k else functools.partial(precond_start_kernel, sz)
        extra = basis if k else [state]
        search, new, head = call(
            kernel, f"precond{k}", (shape(nbp if k else 2 * nbp, lanes), wide, shape(1, 128)),
            red, vec, mask, blocks, *extra,
        )
        basis = basis + [new]
        heads.append(head)
        searches.append(search)
        far = lax.ppermute(search, AXES, off_chip)
        chip = lax.ppermute(search, AXES, on_chip)
        vol, tr = call(
            functools.partial(local_kernel, sz), "local", (wide, shape(4 * nqp, lanes)), search, own, coup
        )
        if k == 0:
            gain = call(
                functools.partial(gain_kernel, sz), "gain", shape(4 * nqp, lanes),
                search, chip, far, hot, near, own, sel,
            )
        vec, part = call(
            functools.partial(image_kernel, sz, k), f"image{k}", (wide, parts),
            search, chip, far, hot, near, sel, gain, back, vol, tr, mask, *basis,
        )
    red = exchange(part)
    return call(
        functools.partial(finish_kernel, sz), "finish", (shape(nv, nb, ne), shape(ITERS + 1, ITERS)),
        red, *heads, *searches,
    )


def solution(mesh):
    placed = (
        P(None, None, AXES),
        P(None, None, AXES),
        P(AXES),
        P(None, AXES),
        P(None, AXES),
        P(None, AXES),
        P(None, AXES),
        P(None, None, AXES),
        P(None, None, None, AXES),
        P(None, None, AXES),
        P(),
        P(),
    )
    peers = 1
    for axis in AXES:
        peers *= mesh.shape[axis]
    return jax.shard_map(
        functools.partial(body, peers),
        mesh=mesh,
        in_specs=placed,
        out_specs=(P(None, None, AXES), P()),
        check_vma=False,
    )
```

```python
import functools

import jax
import jax.numpy as jnp
from jax import lax
from jax.experimental import pallas as pl
from jax.experimental.pallas import tpu as pltpu
from jax.sharding import PartitionSpec as P

ITERS = 6
EPSILON = 1e-06
AXES = ("dom", "grp")
F32 = jnp.float32
BF16 = jnp.bfloat16
CHUNK = 256
VMEM = pl.BlockSpec(memory_space=pltpu.VMEM)
ANY = pl.BlockSpec(memory_space=pl.ANY)
SMEM = pl.BlockSpec(memory_space=pltpu.SMEM)


def ceil_to(n, m):
    return -(-n // m) * m


def iota(shape, dim):
    return lax.broadcasted_iota(jnp.int32, shape, dim)


def split3(x):
    hi = x.astype(BF16).astype(F32)
    rest = x - hi
    mid = rest.astype(BF16).astype(F32)
    return hi, mid, rest - mid


def stack_rhs(parts, axis):
    hi, mid, lo = parts
    return jnp.concatenate([hi, mid, lo, hi, mid, hi], axis=axis).astype(BF16)


def stack_lhs(x):
    hi, mid, lo = split3(x)
    return jnp.concatenate([hi, hi, hi, mid, mid, lo], axis=1).astype(BF16)


def dot(a, b):
    return jnp.dot(a, b, preferred_element_type=F32)


def pad_rows(x, rows):
    return jnp.concatenate([x, jnp.zeros((rows - x.shape[0], x.shape[1]), x.dtype)], axis=0)


class Sizes:
    def __init__(self, nv, nb, ne, nq, peers):
        self.nv, self.nb, self.ne, self.nq, self.peers = nv, nb, ne, nq, peers
        self.nbp = ceil_to(nb, 8)
        self.nqp = ceil_to(nq, 8)
        self.lanes = nv * ne
        self.width = nv * nb
        self.kwidth = ceil_to(self.width, 128)
        self.pair = 2 * ne


def to_wide(read, sz):
    return pad_rows(jnp.concatenate([read(v) for v in range(sz.nv)], axis=1), sz.nbp)


def partial_rows(values, peers):
    lane = iota((1, 128), 1)
    row = jnp.zeros((1, 128), F32)
    for i, val in enumerate(values):
        row = jnp.where(lane == i, val, row)
    return jnp.broadcast_to(row, (peers, 128))


def full_sum(x):
    return jnp.sum(jnp.sum(x, axis=0, keepdims=True), axis=1, keepdims=True)


def total_scalars(red, count):
    row = jnp.sum(red, axis=0, keepdims=True)
    return [row[:, i : i + 1] for i in range(count)]


def fetch(pairs, sems):
    copies = [pltpu.make_async_copy(src, dst, sems.at[i]) for i, (src, dst) in enumerate(pairs)]
    for copy in copies:
        copy.start()
    for copy in copies:
        copy.wait()


def init_kernel(sz, me_ref, p_hbm, *refs):
    args, outs, held, sems, p_sem = refs[:11], refs[11:22], refs[22:33], refs[33], refs[34]
    blocks = pltpu.make_async_copy(p_hbm, outs[10], p_sem)
    blocks.start()
    fetch(list(zip(args, held)), sems)
    (res_ref, orders_ref, state_ref, nbr_ref, face_ref, orient_ref, source_ref, flux_ref, geo_ref, stiff_ref, trace_ref) = held
    start_ref, mask_ref, part_ref, state2_ref, hot_ref, coup_ref, turn_ref, own_ref, near_ref, back_ref = outs[:10]
    nv, nb, ne, nq, nbp, nqp = sz.nv, sz.nb, sz.ne, sz.nq, sz.nbp, sz.nqp
    orders = orders_ref[...]
    count = (orders + 1) * (orders + 2) * (orders + 3) // 6
    count = jnp.concatenate([count] * nv, axis=1)
    mask = (iota((nbp, sz.lanes), 0) < count).astype(F32)
    mask_ref[...] = mask
    start = to_wide(lambda v: res_ref[v], sz) * mask
    start_ref[...] = start
    part_ref[...] = partial_rows([full_sum(start * start)], sz.peers)
    state2_ref[...] = to_wide(lambda v: state_ref[v], sz)

    me = me_ref[0]
    nbr = nbr_ref[...]
    rel = nbr - me * ne + ne
    face, orient = face_ref[...], orient_ref[...]
    flip = (orient >= 3).astype(jnp.int32)
    choice, turn = flip * 4 + face, orient - 3 * flip

    def by_face(x):
        return jnp.concatenate([x[f : f + 1] for f in range(4)], axis=1)

    turn_ref[...] = by_face(turn)
    cols = by_face(jnp.where(nbr >= 0, choice * 4 * ne + rel, -1))
    rows = iota((8 * ne, 4 * ne), 0)
    block = rows // ne
    code = block * 4 * ne + rows - block * ne
    chip_side = jnp.where(lax.rem(me, 2) == 0, 2, 0)
    for source, side in enumerate((1, chip_side, 2 - chip_side)):
        hot_ref[source] = (code + side * ne == cols).astype(F32).astype(BF16)

    for k in range(3):
        pieces = []
        for w in range(nv):
            tile = jnp.zeros((nv, ne), F32)
            for d in range(3):
                tile = tile + geo_ref[d, k : k + 1, :] * flux_ref[d, w]
            pieces.append(tile if w == 0 else jnp.concatenate([tile[w:], tile[:w]], axis=0))
        coup_ref[k] = jnp.concatenate(pieces, axis=1)
    pieces = []
    for w in range(nv):
        tile = source_ref[w]
        pieces.append(tile if w == 0 else jnp.concatenate([tile[w:], tile[:w]], axis=0))
    coup_ref[3] = jnp.concatenate(pieces, axis=1)

    def pad2(x, rows):
        x = jnp.concatenate([x, jnp.zeros((x.shape[0], nbp - x.shape[1]), F32)], axis=1)
        return pad_rows(x, rows)

    traces = [trace_ref[:, f, :] for f in range(4)]
    plain = [pad2(t, nqp) for t in traces]
    flipped = [
        pad2(jnp.concatenate([t[q : q + 1] for q in reversed(range(nq))], axis=0), nqp) for t in traces
    ]
    volume = [pad2(stiff_ref[d], nbp) for d in range(3)]
    own_ref[...] = stack_lhs(jnp.concatenate(plain + volume, axis=0))
    near_ref[...] = stack_lhs(jnp.concatenate(plain + flipped, axis=0))
    back_ref[...] = stack_lhs(jnp.concatenate(plain, axis=0).T)
    blocks.wait()


def apply_blocks(sz, vec, mask, blocks_ref):
    nb, ne, nv, width = sz.nb, sz.ne, sz.nv, sz.width
    tall = jnp.concatenate([vec[:nb, v * ne : (v + 1) * ne] for v in range(nv)], axis=0)
    turned = pad_rows(tall, CHUNK).T
    turned = jnp.concatenate(
        [pltpu.roll(turned[g : g + 8], g * width % CHUNK, 1) if g else turned[:8] for g in range(0, ne, 8)], axis=0
    )
    row = iota((ne, 1), 0)
    for bit in (1, 2, 4):
        turned = jnp.where((row & bit) != 0, pltpu.roll(turned, bit * width % CHUNK, 1), turned)
    total = ne * width
    acc = [jnp.zeros((8, width), F32)] * (ne // 8)
    for low in range(0, total, CHUNK):
        high = min(low + CHUNK, total)
        first, last = low // width // 8, (high - 1) // width // 8 + 1
        size = (8 * (last - first), high - low)
        entry = iota(size, 1) + low - (iota(size, 0) + 8 * first) * width
        lhs = jnp.where((entry >= 0) & (entry < width), turned[8 * first : 8 * last, : high - low], 0.0)
        out = lax.dot_general(
            lhs.astype(BF16), blocks_ref[:, low:high], (((1,), (1,)), ((), ())), preferred_element_type=F32
        )
        for g in range(first, last):
            acc[g] = acc[g] + out[8 * (g - first) : 8 * (g - first + 1)]
    done = jnp.concatenate(acc, axis=0)
    done = jnp.concatenate([done, jnp.zeros((ne, CHUNK - width), F32)], axis=1).T
    wide = jnp.concatenate([done[v * nb : (v + 1) * nb] for v in range(nv)], axis=1)
    return pad_rows(wide, sz.nbp) * mask


def precond_start_kernel(sz, red_ref, vec_ref, mask_ref, blocks_ref, state_ref, z_ref, v_ref, h_ref):
    norm = jnp.sqrt(total_scalars(red_ref[...], 1)[0] + EPSILON)
    new = vec_ref[...] * (1.0 / norm)
    v_ref[...] = new
    h_ref[...] = partial_rows([norm], 1)
    z_ref[: sz.nbp] = apply_blocks(sz, new, mask_ref[...], blocks_ref)
    z_ref[sz.nbp :] = state_ref[...]


def precond_kernel(sz, step, *refs):
    red_ref, vec_ref, mask_ref, blocks_ref = refs[:4]
    basis = refs[4 : 4 + step]
    z_ref, v_ref, h_ref = refs[4 + step :]
    vec = vec_ref[...]
    scalars = total_scalars(red_ref[...], step + 1)
    proj, square = scalars[:step], scalars[step]
    for h, b in zip(proj, basis):
        vec = vec - h * b[...]
        square = square - h * h
    norm = jnp.sqrt(square + EPSILON)
    new = vec * (1.0 / norm)
    v_ref[...] = new
    h_ref[...] = partial_rows(proj + [norm], 1)
    z_ref[...] = apply_blocks(sz, new, mask_ref[...], blocks_ref)


def roll_blocks(x, blocks, ne):
    shift = blocks * ne
    if shift == 0:
        return x
    return jnp.concatenate([x[:, shift:], x[:, :shift]], axis=1)


def gather(sz, sources, hot_refs, near_ref):
    nqp, ne, pair = sz.nqp, sz.ne, sz.pair
    low_half = iota((1, pair), 1) < ne
    lhs = []
    for source in sources:
        every = dot(near_ref[...], stack_rhs(split3(source), 0))
        rows = []
        for v in range(sz.nv):
            column = every[:, v // 2 * pair : (v // 2 + 1) * pair]
            turned = pltpu.roll(column, ne, 1)
            pieces = []
            for g in range(0, 8, 2):
                first, second = (slice((g + i) * nqp, (g + i + 1) * nqp) for i in range(2))
                if v % 2 == 0:
                    pieces.append(jnp.where(low_half, column[first], turned[second]))
                else:
                    pieces.append(jnp.where(low_half, turned[first], column[second]))
            rows.append(jnp.concatenate(pieces, axis=1))
        lhs.append(jnp.concatenate(rows, axis=0))
    lhs = split3(jnp.concatenate(lhs, axis=1))
    hot = jnp.concatenate([ref[...] for ref in hot_refs], axis=0)
    got = dot(jnp.concatenate(lhs, axis=0).astype(BF16), hot)
    size = sz.nv * nqp
    return got[:size] + got[size : 2 * size] + got[2 * size :]


def to_faces(sz, seen, turn):
    nqp, ne, pair = sz.nqp, sz.ne, sz.pair
    low_half = iota((1, pair), 1) < ne
    nq, third = sz.nq, sz.nq // 3
    turned = []
    for v in range(sz.nv):
        tr = seen[v * nqp : (v + 1) * nqp]
        fill = tr[nq:]
        once = jnp.concatenate([tr[third:nq], tr[:third], fill], axis=0)
        twice = jnp.concatenate([tr[2 * third : nq], tr[: 2 * third], fill], axis=0)
        turned.append(jnp.where(turn == 0, tr, jnp.where(turn == 1, once, twice)))
    result = []
    for f in range(4):
        start = f // 2 * pair
        blocks = []
        for p in range(sz.lanes // pair):
            first, second = (turned[2 * p + i][:, start : start + pair] for i in range(2))
            if f % 2 == 0:
                second = pltpu.roll(second, ne, 1)
            else:
                first = pltpu.roll(first, ne, 1)
            blocks.append(jnp.where(low_half, first, second))
        result.append(jnp.concatenate(blocks, axis=1))
    return jnp.concatenate(result, axis=0)


def spread(row, i):
    return jnp.broadcast_to(row[:, i : i + 1], (1, 128))


def rotate_column(step, row, square, turns_ref):
    entries = [spread(row, i) for i in range(step + 2)]
    if square:
        rest = entries[step + 1]
        for h in entries[:-1]:
            rest = rest - h * h
        entries[step + 1] = jnp.sqrt(rest + EPSILON)
    column = list(entries)
    for i in range(step):
        cosine, sine = turns_ref[2 * i : 2 * i + 1, :], turns_ref[2 * i + 1 : 2 * i + 2, :]
        top, low = column[i], column[i + 1]
        column[i] = cosine * top + sine * low
        column[i + 1] = cosine * low - sine * top
    lead, below = column[step], column[step + 1]
    radius = jnp.sqrt(lead * lead + below * below)
    cosine, sine = lead / radius, below / radius
    column[step] = cosine * lead + sine * below
    return entries, column, cosine, sine


def direction(sz, search, column, earlier):
    def across(x):
        return jnp.concatenate([x] * (sz.lanes // 128), axis=1)

    total = search
    for r, ref in zip(column, earlier):
        total = total - across(r) * ref[...]
    return total * across(1.0 / column[len(earlier)]), across


def fill_column(step, entries, hess):
    row_id, col_id = iota(hess.shape, 0), iota(hess.shape, 1)
    for i, entry in enumerate(entries):
        hess = jnp.where((row_id == i) & (col_id == step), entry[:, : hess.shape[1]], hess)
    return hess


def local_kernel(sz, z_ref, own_ref, coup_ref, vol_ref, tr_ref):
    search = z_ref[: sz.nbp]
    out = dot(own_ref[...], stack_rhs(split3(search), 0))
    faces = 4 * sz.nqp
    tr_ref[...] = out[:faces]
    acc = jnp.zeros((sz.nbp, sz.lanes), F32)
    for d in range(4):
        moved = search if d == 3 else out[faces + d * sz.nbp : faces + (d + 1) * sz.nbp]
        for s in range(sz.nv):
            acc = acc + coup_ref[d, s : s + 1, :] * roll_blocks(moved, s, sz.ne)
    vol_ref[...] = acc


def column_kernel(sz, step, *refs):
    head_ref, z_ref, turns_ref, hess_ref, sum_ref = refs[:5]
    earlier = refs[5 : 5 + step]
    turns_out, hess_out, sum_out, dir_ref = refs[5 + step :]
    entries, column, cosine, sine = rotate_column(step, head_ref[...], False, turns_ref)
    new, across = direction(sz, z_ref[: sz.nbp], column, earlier)
    dir_ref[...] = new
    last = turns_ref.shape[0] - 1
    right = spread(turns_ref[last:, :], 0) if step == 0 else turns_ref[last:, :]
    value = across(cosine * right) * new
    if step == 0:
        sum_out[...] = value
        hess = jnp.zeros(hess_out.shape, F32)
        turns_out[...] = jnp.zeros(turns_out.shape, F32)
    else:
        sum_out[...] = sum_ref[...] + value
        hess = hess_ref[...]
        turns_out[...] = turns_ref[...]
    hess_out[...] = fill_column(step, entries, hess)
    turns_out[2 * step : 2 * step + 1, :] = cosine
    turns_out[2 * step + 1 : 2 * step + 2, :] = sine
    turns_out[turns_out.shape[0] - 1 :, :] = -(sine * right)


def finish_kernel(sz, *refs):
    red_ref, z_ref, turns_ref, hess_ref, sum_ref = refs[:5]
    step = ITERS - 1
    earlier = refs[5 : 5 + step]
    out_ref, hess_out = refs[5 + step :]
    row = jnp.sum(red_ref[...], axis=0, keepdims=True)
    entries, column, cosine, sine = rotate_column(step, row, True, turns_ref)
    new, across = direction(sz, z_ref[...], column, earlier)
    last = turns_ref.shape[0] - 1
    total = sum_ref[...] + across(cosine * turns_ref[last:, :]) * new
    for v in range(sz.nv):
        out_ref[v] = total[: sz.nb, v * sz.ne : (v + 1) * sz.ne]
    hess_out[...] = fill_column(step, entries, hess_ref[...])[: ITERS + 1, :ITERS]


def near_kernel(sz, z_ref, chip_ref, hot_ref, near_ref, *outs):
    nbp = sz.nbp
    for i, out_ref in enumerate(outs):
        sources = [ref[i * nbp : (i + 1) * nbp] for ref in (z_ref, chip_ref)]
        out_ref[...] = gather(sz, sources, [hot_ref.at[0], hot_ref.at[1]], near_ref)


def gain_kernel(sz, z_ref, far_ref, hot_ref, near_ref, own_ref, turn_ref, seen_ref, gain_ref):
    nbp = sz.nbp
    tr = dot(own_ref[: 4 * sz.nqp], stack_rhs(split3(z_ref[nbp:]), 0))
    seen = seen_ref[...] + gather(sz, [far_ref[nbp:]], [hot_ref.at[2]], near_ref)
    gain_ref[...] = 1.0 + 0.5 * jnp.abs(tr + to_faces(sz, seen, turn_ref[...]))


def image_kernel(sz, step, *refs):
    far_ref, hot_ref, near_ref, turn_ref, seen_ref, gain_ref, back_ref, vol_ref, tr_ref, mask_ref = refs[:10]
    basis = refs[10 : 11 + step]
    part_ref = refs[11 + step]
    seen = seen_ref[...] + gather(sz, [far_ref[: sz.nbp]], [hot_ref.at[2]], near_ref)
    other = to_faces(sz, seen, turn_ref[...])
    flux = gain_ref[...] * (tr_ref[...] - other)
    face = dot(back_ref[...], stack_rhs(split3(flux), 0))
    image = (vol_ref[...] + face) * mask_ref[...]
    if step < ITERS - 1:
        refs[12 + step][...] = image
    values = [full_sum(b[...] * image) for b in basis] + [full_sum(image * image)]
    part_ref[...] = partial_rows(values, sz.peers)


def call(kernel, name, out_shape, *args, specs=None, scratch=(), limit=24 * 2**20):
    return pl.pallas_call(
        kernel,
        name=name,
        out_shape=out_shape,
        in_specs=specs or [VMEM] * len(args),
        out_specs=jax.tree.map(lambda _: VMEM, out_shape),
        scratch_shapes=list(scratch),
        compiler_params=pltpu.CompilerParams(vmem_limit_bytes=limit),
    )(*args)


def shape(*dims, dtype=F32):
    return jax.ShapeDtypeStruct(dims, dtype)


def copied(arrays):
    return [pltpu.VMEM(a.shape, a.dtype) for a in arrays] + [pltpu.SemaphoreType.DMA((len(arrays),))]


def body(
    peers, state_coeffs, residual_in, orders, neighbours, neighbour_face, orientation, precond, source,
    flux_jacobian, geometry, stiffness, trace_matrix,
):
    nv, nb, ne = state_coeffs.shape
    sz = Sizes(nv, nb, ne, trace_matrix.shape[1], peers)
    lanes, nbp, nqp = sz.lanes, sz.nbp, sz.nqp
    me = lax.axis_index(AXES).astype(jnp.int32).reshape(1)
    wide = shape(nbp, lanes)
    parts = shape(peers, 128)
    fetched = [
        residual_in, orders.reshape(1, ne), state_coeffs, neighbours, neighbour_face, orientation, source, flux_jacobian,
        geometry, stiffness, jnp.transpose(trace_matrix, (1, 0, 2)),
    ]
    start, mask, part, state, hot, coup, turn, own, near, back, blocks = call(
        functools.partial(init_kernel, sz),
        "init",
        (
            wide, wide, parts, wide,
            shape(3, 8 * ne, 4 * ne, dtype=BF16),
            shape(4, nv, lanes),
            shape(1, 4 * ne, dtype=jnp.int32),
            shape(4 * nqp + 3 * nbp, 6 * nbp, dtype=BF16),
            shape(8 * nqp, 6 * nbp, dtype=BF16),
            shape(nbp, 24 * nqp, dtype=BF16),
            shape(*precond.shape, dtype=BF16),
        ),
        me, *[pltpu.with_memory_space_constraint(a, pltpu.HBM) for a in [precond] + fetched],
        specs=[SMEM] + [ANY] * (1 + len(fetched)), scratch=copied(fetched) + [pltpu.SemaphoreType.DMA],
    )

    def exchange(rows):
        return lax.all_to_all(rows, AXES, 0, 0, tiled=True)

    on_chip = [(i, i ^ 1) for i in range(peers)]
    odd = range(1, peers - 1, 2)
    off_chip = [(i, i + 1) for i in odd] + [(i + 1, i) for i in odd]

    basis, directions = [], []
    vec, gain = start, None
    turns = hess = total = None
    face_shape, seen_shape = shape(4 * nqp, lanes), shape(nv * nqp, 4 * ne)
    state_shapes = (shape(2 * ITERS + 4, 128), shape(8, 128), wide, wide)
    for k in range(ITERS):
        red = exchange(part)
        kernel = functools.partial(precond_kernel, sz, k) if k else functools.partial(precond_start_kernel, sz)
        extra = basis if k else [state]
        previous = None if k == 0 else search
        search, new, head = call(
            kernel, f"precond{k}", (shape(nbp if k else 2 * nbp, lanes), wide, shape(1, 128)),
            red, vec, mask, blocks, *extra,
        )
        basis = basis + [new]
        far = lax.ppermute(search, AXES, off_chip)
        chip = lax.ppermute(search, AXES, on_chip)
        vol, tr = call(functools.partial(local_kernel, sz), "local", (wide, face_shape), search, own, coup)
        if k == 0:
            turns, hess, total = head, head, head
        else:
            turns, hess, total, new = call(
                functools.partial(column_kernel, sz, k - 1), f"column{k}", state_shapes,
                head, previous, turns, hess, total, *directions,
            )
            directions = directions + [new]
        seen = call(
            functools.partial(near_kernel, sz), "near", (seen_shape,) * (1 if k else 2), search, chip, hot, near
        )
        if k == 0:
            gain = call(
                functools.partial(gain_kernel, sz), "gain", face_shape, search, far, hot, near, own, turn, seen[1]
            )
        outs = call(
            functools.partial(image_kernel, sz, k), f"image{k}", (parts, wide) if k < ITERS - 1 else (parts,),
            far, hot, near, turn, seen[0], gain, back, vol, tr, mask, *basis,
        )
        part, vec = outs if k < ITERS - 1 else (outs[0], None)
    red = exchange(part)
    return call(
        functools.partial(finish_kernel, sz), "finish", (shape(nv, nb, ne), shape(ITERS + 1, ITERS)),
        red, search, turns, hess, total, *directions,
    )


def solution(mesh):
    placed = (
        P(None, None, AXES),
        P(None, None, AXES),
        P(AXES),
        P(None, AXES),
        P(None, AXES),
        P(None, AXES),
        P(None, AXES),
        P(None, None, AXES),
        P(None, None, None, AXES),
        P(None, None, AXES),
        P(),
        P(),
    )
    peers = 1
    for axis in AXES:
        peers *= mesh.shape[axis]
    return jax.shard_map(
        functools.partial(body, peers),
        mesh=mesh,
        in_specs=placed,
        out_specs=(P(None, None, AXES), P()),
        check_vma=False,
    )
```

```python
import functools

import jax
import jax.numpy as jnp
from jax import lax
from jax.experimental import pallas as pl
from jax.experimental.pallas import tpu as pltpu
from jax.sharding import PartitionSpec as P

ITERS = 6
EPSILON = 1e-06
AXES = ("dom", "grp")
F32 = jnp.float32
BF16 = jnp.bfloat16
CHUNK = 256
VMEM = pl.BlockSpec(memory_space=pltpu.VMEM)
ANY = pl.BlockSpec(memory_space=pl.ANY)
SMEM = pl.BlockSpec(memory_space=pltpu.SMEM)


def ceil_to(n, m):
    return -(-n // m) * m


def iota(shape, dim):
    return lax.broadcasted_iota(jnp.int32, shape, dim)


def split3(x):
    hi = x.astype(BF16).astype(F32)
    rest = x - hi
    mid = rest.astype(BF16).astype(F32)
    return hi, mid, rest - mid


def stack_rhs(parts, axis):
    hi, mid, lo = parts
    return jnp.concatenate([hi, mid, lo, hi, mid, hi], axis=axis).astype(BF16)


def stack_lhs(x):
    hi, mid, lo = split3(x)
    return jnp.concatenate([hi, hi, hi, mid, mid, lo], axis=1).astype(BF16)


def dot(a, b):
    return jnp.dot(a, b, preferred_element_type=F32)


def pad_rows(x, rows):
    return jnp.concatenate([x, jnp.zeros((rows - x.shape[0], x.shape[1]), x.dtype)], axis=0)


class Sizes:
    def __init__(self, nv, nb, ne, nq, peers):
        self.nv, self.nb, self.ne, self.nq, self.peers = nv, nb, ne, nq, peers
        self.nbp = ceil_to(nb, 8)
        self.nqp = ceil_to(nq, 8)
        self.lanes = nv * ne
        self.width = nv * nb
        self.kwidth = ceil_to(self.width, 128)
        self.pair = 2 * ne
        self.split = self.width * ne * 3 // 5 // CHUNK * CHUNK


def to_wide(read, sz):
    return pad_rows(jnp.concatenate([read(v) for v in range(sz.nv)], axis=1), sz.nbp)


def partial_rows(values, peers):
    lane = iota((1, 128), 1)
    row = jnp.zeros((1, 128), F32)
    for i, val in enumerate(values):
        row = jnp.where(lane == i, val, row)
    return jnp.broadcast_to(row, (peers, 128))


def full_sum(x):
    return jnp.sum(jnp.sum(x, axis=0, keepdims=True), axis=1, keepdims=True)


def total_scalars(red, count):
    row = jnp.sum(red, axis=0, keepdims=True)
    return [row[:, i : i + 1] for i in range(count)]


def fetch(pairs, sems):
    copies = [pltpu.make_async_copy(src, dst, sems.at[i]) for i, (src, dst) in enumerate(pairs)]
    for copy in copies:
        copy.start()
    for copy in copies:
        copy.wait()


def init_kernel(sz, me_ref, p_hbm, *refs):
    args, outs, held, sems, p_sem = refs[:11], refs[11:22], refs[22:33], refs[33], refs[34]
    blocks = pltpu.make_async_copy(p_hbm.at[:, : sz.split], outs[10], p_sem)
    blocks.start()
    fetch(list(zip(args, held)), sems)
    (res_ref, orders_ref, state_ref, nbr_ref, face_ref, orient_ref, source_ref, flux_ref, geo_ref, stiff_ref, trace_ref) = held
    start_ref, mask_ref, part_ref, state2_ref, hot_ref, coup_ref, turn_ref, own_ref, near_ref, back_ref = outs[:10]
    nv, nb, ne, nq, nbp, nqp = sz.nv, sz.nb, sz.ne, sz.nq, sz.nbp, sz.nqp
    orders = orders_ref[...]
    count = (orders + 1) * (orders + 2) * (orders + 3) // 6
    count = jnp.concatenate([count] * nv, axis=1)
    mask = (iota((nbp, sz.lanes), 0) < count).astype(F32)
    mask_ref[...] = mask
    start = to_wide(lambda v: res_ref[v], sz) * mask
    start_ref[...] = start
    part_ref[...] = partial_rows([full_sum(start * start)], sz.peers)
    state2_ref[...] = to_wide(lambda v: state_ref[v], sz)

    me = me_ref[0]
    nbr = nbr_ref[...]
    rel = nbr - me * ne + ne
    face, orient = face_ref[...], orient_ref[...]
    flip = (orient >= 3).astype(jnp.int32)
    choice, turn = flip * 4 + face, orient - 3 * flip

    def by_face(x):
        return jnp.concatenate([x[f : f + 1] for f in range(4)], axis=1)

    turn_ref[...] = by_face(turn)
    cols = by_face(jnp.where(nbr >= 0, choice * 4 * ne + rel, -1))
    rows = iota((8 * ne, 4 * ne), 0)
    block = rows // ne
    code = block * 4 * ne + rows - block * ne
    chip_side = jnp.where(lax.rem(me, 2) == 0, 2, 0)
    for source, side in enumerate((1, chip_side, 2 - chip_side)):
        hot_ref[source] = (code + side * ne == cols).astype(F32).astype(BF16)

    for k in range(3):
        pieces = []
        for w in range(nv):
            tile = jnp.zeros((nv, ne), F32)
            for d in range(3):
                tile = tile + geo_ref[d, k : k + 1, :] * flux_ref[d, w]
            pieces.append(tile if w == 0 else jnp.concatenate([tile[w:], tile[:w]], axis=0))
        coup_ref[k] = jnp.concatenate(pieces, axis=1)
    pieces = []
    for w in range(nv):
        tile = source_ref[w]
        pieces.append(tile if w == 0 else jnp.concatenate([tile[w:], tile[:w]], axis=0))
    coup_ref[3] = jnp.concatenate(pieces, axis=1)

    def pad2(x, rows):
        x = jnp.concatenate([x, jnp.zeros((x.shape[0], nbp - x.shape[1]), F32)], axis=1)
        return pad_rows(x, rows)

    traces = [trace_ref[:, f, :] for f in range(4)]
    plain = [pad2(t, nqp) for t in traces]
    flipped = [
        pad2(jnp.concatenate([t[q : q + 1] for q in reversed(range(nq))], axis=0), nqp) for t in traces
    ]
    volume = [pad2(stiff_ref[d], nbp) for d in range(3)]
    own_ref[...] = stack_lhs(jnp.concatenate(plain + volume, axis=0))
    near_ref[...] = stack_lhs(jnp.concatenate(plain + flipped, axis=0))
    back_ref[...] = stack_lhs(jnp.concatenate(plain, axis=0).T)
    blocks.wait()


def apply_blocks(sz, vec, mask, blocks):
    nb, ne, nv, width = sz.nb, sz.ne, sz.nv, sz.width
    tall = jnp.concatenate([vec[:nb, v * ne : (v + 1) * ne] for v in range(nv)], axis=0)
    turned = pad_rows(tall, CHUNK).T
    turned = jnp.concatenate(
        [pltpu.roll(turned[g : g + 8], g * width % CHUNK, 1) if g else turned[:8] for g in range(0, ne, 8)], axis=0
    )
    row = iota((ne, 1), 0)
    for bit in (1, 2, 4):
        turned = jnp.where((row & bit) != 0, pltpu.roll(turned, bit * width % CHUNK, 1), turned)
    total = ne * width
    acc = [jnp.zeros((8, width), F32)] * (ne // 8)
    for low in range(0, total, CHUNK):
        high = min(low + CHUNK, total)
        first, last = low // width // 8, (high - 1) // width // 8 + 1
        size = (8 * (last - first), high - low)
        entry = iota(size, 1) + low - (iota(size, 0) + 8 * first) * width
        lhs = jnp.where((entry >= 0) & (entry < width), turned[8 * first : 8 * last, : high - low], 0.0)
        out = lax.dot_general(
            lhs.astype(BF16), blocks(low, high), (((1,), (1,)), ((), ())), preferred_element_type=F32
        )
        for g in range(first, last):
            acc[g] = acc[g] + out[8 * (g - first) : 8 * (g - first + 1)]
    done = jnp.concatenate(acc, axis=0)
    done = jnp.concatenate([done, jnp.zeros((ne, CHUNK - width), F32)], axis=1).T
    wide = jnp.concatenate([done[v * nb : (v + 1) * nb] for v in range(nv)], axis=1)
    return pad_rows(wide, sz.nbp) * mask


def columns(sz, first_ref, rest_ref):
    def read(low, high):
        if high <= sz.split:
            return first_ref[:, low:high]
        return rest_ref[:, low - sz.split : high - sz.split]

    return read


def precond_start_kernel(
    sz, red_ref, vec_ref, mask_ref, first_ref, state_ref, p_hbm, z_ref, v_ref, h_ref, rest_ref, sem
):
    rest = pltpu.make_async_copy(p_hbm.at[:, sz.split :], rest_ref, sem)
    rest.start()
    norm = jnp.sqrt(total_scalars(red_ref[...], 1)[0] + EPSILON)
    new = vec_ref[...] * (1.0 / norm)
    v_ref[...] = new
    h_ref[...] = partial_rows([norm], 1)
    stored = columns(sz, first_ref, rest_ref)
    waited = []

    def read(low, high):
        if high > sz.split and not waited:
            rest.wait()
            waited.append(True)
        return stored(low, high)

    z_ref[: sz.nbp] = apply_blocks(sz, new, mask_ref[...], read)
    z_ref[sz.nbp :] = state_ref[...]


def precond_kernel(sz, step, *refs):
    red_ref, vec_ref, mask_ref, first_ref, rest_ref = refs[:5]
    basis = refs[5 : 5 + step]
    z_ref, v_ref, h_ref = refs[5 + step :]
    vec = vec_ref[...]
    scalars = total_scalars(red_ref[...], step + 1)
    proj, square = scalars[:step], scalars[step]
    for h, b in zip(proj, basis):
        vec = vec - h * b[...]
        square = square - h * h
    norm = jnp.sqrt(square + EPSILON)
    new = vec * (1.0 / norm)
    v_ref[...] = new
    h_ref[...] = partial_rows(proj + [norm], 1)
    z_ref[...] = apply_blocks(sz, new, mask_ref[...], columns(sz, first_ref, rest_ref))


def roll_blocks(x, blocks, ne):
    shift = blocks * ne
    if shift == 0:
        return x
    return jnp.concatenate([x[:, shift:], x[:, :shift]], axis=1)


def gather(sz, sources, hot_refs, near_ref):
    nqp, ne, pair = sz.nqp, sz.ne, sz.pair
    low_half = iota((1, pair), 1) < ne
    lhs = []
    for source in sources:
        every = dot(near_ref[...], stack_rhs(split3(source), 0))
        rows = []
        for v in range(sz.nv):
            column = every[:, v // 2 * pair : (v // 2 + 1) * pair]
            turned = pltpu.roll(column, ne, 1)
            pieces = []
            for g in range(0, 8, 2):
                first, second = (slice((g + i) * nqp, (g + i + 1) * nqp) for i in range(2))
                if v % 2 == 0:
                    pieces.append(jnp.where(low_half, column[first], turned[second]))
                else:
                    pieces.append(jnp.where(low_half, turned[first], column[second]))
            rows.append(jnp.concatenate(pieces, axis=1))
        lhs.append(jnp.concatenate(rows, axis=0))
    lhs = split3(jnp.concatenate(lhs, axis=1))
    hot = jnp.concatenate([ref[...] for ref in hot_refs], axis=0)
    got = dot(jnp.concatenate(lhs, axis=0).astype(BF16), hot)
    size = sz.nv * nqp
    return got[:size] + got[size : 2 * size] + got[2 * size :]


def to_faces(sz, seen, turn):
    nqp, ne, pair = sz.nqp, sz.ne, sz.pair
    low_half = iota((1, pair), 1) < ne
    nq, third = sz.nq, sz.nq // 3
    turned = []
    for v in range(sz.nv):
        tr = seen[v * nqp : (v + 1) * nqp]
        fill = tr[nq:]
        once = jnp.concatenate([tr[third:nq], tr[:third], fill], axis=0)
        twice = jnp.concatenate([tr[2 * third : nq], tr[: 2 * third], fill], axis=0)
        turned.append(jnp.where(turn == 0, tr, jnp.where(turn == 1, once, twice)))
    result = []
    for f in range(4):
        start = f // 2 * pair
        blocks = []
        for p in range(sz.lanes // pair):
            first, second = (turned[2 * p + i][:, start : start + pair] for i in range(2))
            if f % 2 == 0:
                second = pltpu.roll(second, ne, 1)
            else:
                first = pltpu.roll(first, ne, 1)
            blocks.append(jnp.where(low_half, first, second))
        result.append(jnp.concatenate(blocks, axis=1))
    return jnp.concatenate(result, axis=0)


def spread(row, i):
    return jnp.broadcast_to(row[:, i : i + 1], (1, 128))


def rotate_column(step, row, square, turns_ref):
    entries = [spread(row, i) for i in range(step + 2)]
    if square:
        rest = entries[step + 1]
        for h in entries[:-1]:
            rest = rest - h * h
        entries[step + 1] = jnp.sqrt(rest + EPSILON)
    column = list(entries)
    for i in range(step):
        cosine, sine = turns_ref[2 * i : 2 * i + 1, :], turns_ref[2 * i + 1 : 2 * i + 2, :]
        top, low = column[i], column[i + 1]
        column[i] = cosine * top + sine * low
        column[i + 1] = cosine * low - sine * top
    lead, below = column[step], column[step + 1]
    radius = jnp.sqrt(lead * lead + below * below)
    cosine, sine = lead / radius, below / radius
    column[step] = cosine * lead + sine * below
    return entries, column, cosine, sine


def direction(sz, search, column, earlier):
    def across(x):
        return jnp.concatenate([x] * (sz.lanes // 128), axis=1)

    total = search
    for r, ref in zip(column, earlier):
        total = total - across(r) * ref[...]
    return total * across(1.0 / column[len(earlier)]), across


def fill_column(step, entries, hess):
    row_id, col_id = iota(hess.shape, 0), iota(hess.shape, 1)
    for i, entry in enumerate(entries):
        hess = jnp.where((row_id == i) & (col_id == step), entry[:, : hess.shape[1]], hess)
    return hess


def local_kernel(sz, z_ref, own_ref, coup_ref, vol_ref, tr_ref):
    search = z_ref[: sz.nbp]
    out = dot(own_ref[...], stack_rhs(split3(search), 0))
    faces = 4 * sz.nqp
    tr_ref[...] = out[:faces]
    acc = jnp.zeros((sz.nbp, sz.lanes), F32)
    for d in range(4):
        moved = search if d == 3 else out[faces + d * sz.nbp : faces + (d + 1) * sz.nbp]
        for s in range(sz.nv):
            acc = acc + coup_ref[d, s : s + 1, :] * roll_blocks(moved, s, sz.ne)
    vol_ref[...] = acc


def column_kernel(sz, step, *refs):
    head_ref, z_ref, turns_ref, hess_ref, sum_ref = refs[:5]
    earlier = refs[5 : 5 + step]
    turns_out, hess_out, sum_out, dir_ref = refs[5 + step :]
    entries, column, cosine, sine = rotate_column(step, head_ref[...], False, turns_ref)
    new, across = direction(sz, z_ref[: sz.nbp], column, earlier)
    dir_ref[...] = new
    last = turns_ref.shape[0] - 1
    right = spread(turns_ref[last:, :], 0) if step == 0 else turns_ref[last:, :]
    value = across(cosine * right) * new
    if step == 0:
        sum_out[...] = value
        hess = jnp.zeros(hess_out.shape, F32)
        turns_out[...] = jnp.zeros(turns_out.shape, F32)
    else:
        sum_out[...] = sum_ref[...] + value
        hess = hess_ref[...]
        turns_out[...] = turns_ref[...]
    hess_out[...] = fill_column(step, entries, hess)
    turns_out[2 * step : 2 * step + 1, :] = cosine
    turns_out[2 * step + 1 : 2 * step + 2, :] = sine
    turns_out[turns_out.shape[0] - 1 :, :] = -(sine * right)


def finish_kernel(sz, *refs):
    red_ref, z_ref, turns_ref, hess_ref, sum_ref = refs[:5]
    step = ITERS - 1
    earlier = refs[5 : 5 + step]
    out_ref, hess_out = refs[5 + step :]
    row = jnp.sum(red_ref[...], axis=0, keepdims=True)
    entries, column, cosine, sine = rotate_column(step, row, True, turns_ref)
    new, across = direction(sz, z_ref[...], column, earlier)
    last = turns_ref.shape[0] - 1
    total = sum_ref[...] + across(cosine * turns_ref[last:, :]) * new
    for v in range(sz.nv):
        out_ref[v] = total[: sz.nb, v * sz.ne : (v + 1) * sz.ne]
    hess_out[...] = fill_column(step, entries, hess_ref[...])[: ITERS + 1, :ITERS]


def near_column_kernel(sz, step, *refs):
    near_kernel(sz, *refs[:4], refs[8 + step])
    column_kernel(sz, step - 1, *refs[4 : 8 + step], *refs[9 + step :])


def near_kernel(sz, z_ref, chip_ref, hot_ref, near_ref, *outs):
    nbp = sz.nbp
    for i, out_ref in enumerate(outs):
        sources = [ref[i * nbp : (i + 1) * nbp] for ref in (z_ref, chip_ref)]
        out_ref[...] = gather(sz, sources, [hot_ref.at[0], hot_ref.at[1]], near_ref)


def image_kernel(sz, step, *refs):
    far_ref, hot_ref, near_ref, turn_ref, seen_ref, gain_ref, back_ref, vol_ref, tr_ref, mask_ref = refs[:10]
    basis, refs = refs[10 : 11 + step], refs[11 + step :]
    nbp, turn = sz.nbp, turn_ref[...]
    if step == 0:
        z_ref, own_ref, refs = refs[0], refs[1], refs[2:]
        own = dot(own_ref[: 4 * sz.nqp], stack_rhs(split3(z_ref[nbp:]), 0))
        seen = gain_ref[...] + gather(sz, [far_ref[nbp:]], [hot_ref.at[2]], near_ref)
        gain = 1.0 + 0.5 * jnp.abs(own + to_faces(sz, seen, turn))
        refs[2][...] = gain
    else:
        gain = gain_ref[...]
    seen = seen_ref[...] + gather(sz, [far_ref[:nbp]], [hot_ref.at[2]], near_ref)
    flux = gain * (tr_ref[...] - to_faces(sz, seen, turn))
    face = dot(back_ref[...], stack_rhs(split3(flux), 0))
    image = (vol_ref[...] + face) * mask_ref[...]
    if step < ITERS - 1:
        refs[1][...] = image
    values = [full_sum(b[...] * image) for b in basis] + [full_sum(image * image)]
    refs[0][...] = partial_rows(values, sz.peers)


def call(kernel, name, out_shape, *args, specs=None, scratch=(), limit=24 * 2**20):
    return pl.pallas_call(
        kernel,
        name=name,
        out_shape=out_shape,
        in_specs=specs or [VMEM] * len(args),
        out_specs=jax.tree.map(lambda _: VMEM, out_shape),
        scratch_shapes=list(scratch),
        compiler_params=pltpu.CompilerParams(vmem_limit_bytes=limit),
    )(*args)


def shape(*dims, dtype=F32):
    return jax.ShapeDtypeStruct(dims, dtype)


def copied(arrays):
    return [pltpu.VMEM(a.shape, a.dtype) for a in arrays] + [pltpu.SemaphoreType.DMA((len(arrays),))]


def body(
    peers, state_coeffs, residual_in, orders, neighbours, neighbour_face, orientation, precond, source,
    flux_jacobian, geometry, stiffness, trace_matrix,
):
    nv, nb, ne = state_coeffs.shape
    sz = Sizes(nv, nb, ne, trace_matrix.shape[1], peers)
    lanes, nbp, nqp = sz.lanes, sz.nbp, sz.nqp
    me = lax.axis_index(AXES).astype(jnp.int32).reshape(1)
    wide = shape(nbp, lanes)
    parts = pltpu.VMEM((peers, 128), F32)
    fetched = [
        residual_in, orders.reshape(1, ne), state_coeffs, neighbours, neighbour_face, orientation, source, flux_jacobian,
        geometry, stiffness, jnp.transpose(trace_matrix, (1, 0, 2)),
    ]
    start, mask, part, state, hot, coup, turn, own, near, back, first = call(
        functools.partial(init_kernel, sz),
        "init",
        (
            wide, wide, parts, wide,
            shape(3, 8 * ne, 4 * ne, dtype=BF16),
            shape(4, nv, lanes),
            shape(1, 4 * ne, dtype=jnp.int32),
            shape(4 * nqp + 3 * nbp, 6 * nbp, dtype=BF16),
            shape(8 * nqp, 6 * nbp, dtype=BF16),
            shape(nbp, 24 * nqp, dtype=BF16),
            shape(sz.width, sz.split, dtype=BF16),
        ),
        me, *[pltpu.with_memory_space_constraint(a, pltpu.HBM) for a in [precond] + fetched],
        specs=[SMEM] + [ANY] * (1 + len(fetched)), scratch=copied(fetched) + [pltpu.SemaphoreType.DMA],
    )

    def exchange(rows):
        return lax.all_to_all(rows, AXES, 0, 0, tiled=True)

    on_chip = [(i, i ^ 1) for i in range(peers)]
    odd = range(1, peers - 1, 2)
    off_chip = [(i, i + 1) for i in odd] + [(i + 1, i) for i in odd]

    basis, directions = [], []
    vec, gain = start, None
    turns = hess = total = None
    face_shape, seen_shape = shape(4 * nqp, lanes), shape(nv * nqp, 4 * ne)
    state_shapes = (shape(2 * ITERS + 4, 128), shape(8, 128), wide, wide)
    for k in range(ITERS):
        red = exchange(part)
        previous = None if k == 0 else search
        if k == 0:
            search, new, head, rest = call(
                functools.partial(precond_start_kernel, sz), "precond0",
                (shape(2 * nbp, lanes), wide, shape(1, 128), shape(sz.width, precond.shape[1] - sz.split, dtype=BF16)),
                red, vec, mask, first, state, pltpu.with_memory_space_constraint(precond, pltpu.HBM),
                specs=[VMEM] * 5 + [ANY], scratch=[pltpu.SemaphoreType.DMA],
            )
        else:
            search, new, head = call(
                functools.partial(precond_kernel, sz, k), f"precond{k}", (wide, wide, shape(1, 128)),
                red, vec, mask, first, rest, *basis,
            )
        basis = basis + [new]
        far = lax.ppermute(search, AXES, off_chip)
        chip = lax.ppermute(search, AXES, on_chip)
        vol, tr = call(functools.partial(local_kernel, sz), "local", (wide, face_shape), search, own, coup)
        if k == 0:
            turns, hess, total = head, head, head
            seen, gain = call(
                functools.partial(near_kernel, sz), "near", (seen_shape, seen_shape), search, chip, hot, near
            )
        else:
            seen, turns, hess, total, new = call(
                functools.partial(near_column_kernel, sz, k), f"near{k}", (seen_shape,) + state_shapes,
                search, chip, hot, near, head, previous, turns, hess, total, *directions,
            )
            directions = directions + [new]
        extra = basis + ([search, own] if k == 0 else [])
        shapes = (parts,) if k == ITERS - 1 else (parts, wide, face_shape)[: 3 if k == 0 else 2]
        outs = call(
            functools.partial(image_kernel, sz, k), f"image{k}", shapes,
            far, hot, near, turn, seen, gain, back, vol, tr, mask, *extra,
        )
        part, vec = outs[0], outs[1 % len(outs)]
        gain = outs[2] if k == 0 else gain
    red = exchange(part)
    return call(
        functools.partial(finish_kernel, sz), "finish", (shape(nv, nb, ne), shape(ITERS + 1, ITERS)),
        red, search, turns, hess, total, *directions,
    )


def solution(mesh):
    placed = (
        P(None, None, AXES),
        P(None, None, AXES),
        P(AXES),
        P(None, AXES),
        P(None, AXES),
        P(None, AXES),
        P(None, AXES),
        P(None, None, AXES),
        P(None, None, None, AXES),
        P(None, None, AXES),
        P(),
        P(),
    )
    peers = 1
    for axis in AXES:
        peers *= mesh.shape[axis]
    return jax.shard_map(
        functools.partial(body, peers),
        mesh=mesh,
        in_specs=placed,
        out_specs=(P(None, None, AXES), P()),
        check_vma=False,
    )
```

```python
import functools

import jax
import jax.numpy as jnp
from jax import lax
from jax.experimental import pallas as pl
from jax.experimental.pallas import tpu as pltpu
from jax.sharding import PartitionSpec as P

ITERS = 6
EPSILON = 1e-06
AXES = ("dom", "grp")
F32 = jnp.float32
BF16 = jnp.bfloat16
CHUNK = 256
VMEM = pl.BlockSpec(memory_space=pltpu.VMEM)
ANY = pl.BlockSpec(memory_space=pl.ANY)
SMEM = pl.BlockSpec(memory_space=pltpu.SMEM)


def ceil_to(n, m):
    return -(-n // m) * m


def iota(shape, dim):
    return lax.broadcasted_iota(jnp.int32, shape, dim)


def split3(x):
    hi = x.astype(BF16).astype(F32)
    rest = x - hi
    mid = rest.astype(BF16).astype(F32)
    return hi, mid, rest - mid


def stack_rhs(parts, axis):
    hi, mid, lo = parts
    return jnp.concatenate([hi, mid, lo, hi, mid, hi], axis=axis).astype(BF16)


def stack_lhs(x):
    hi, mid, lo = split3(x)
    return jnp.concatenate([hi, hi, hi, mid, mid, lo], axis=1).astype(BF16)


def dot(a, b):
    return jnp.dot(a, b, preferred_element_type=F32)


def pad_rows(x, rows):
    return jnp.concatenate([x, jnp.zeros((rows - x.shape[0], x.shape[1]), x.dtype)], axis=0)


class Sizes:
    def __init__(self, nv, nb, ne, nq, peers):
        self.nv, self.nb, self.ne, self.nq, self.peers = nv, nb, ne, nq, peers
        self.nbp = ceil_to(nb, 8)
        self.nqp = ceil_to(nq, 8)
        self.lanes = nv * ne
        self.width = nv * nb
        self.kwidth = ceil_to(self.width, 128)
        self.pair = 2 * ne


def to_wide(read, sz):
    return pad_rows(jnp.concatenate([read(v) for v in range(sz.nv)], axis=1), sz.nbp)


def partial_rows(values, peers):
    lane = iota((1, 128), 1)
    row = jnp.zeros((1, 128), F32)
    for i, val in enumerate(values):
        row = jnp.where(lane == i, val, row)
    return jnp.broadcast_to(row, (peers, 128))


def full_sum(x):
    return jnp.sum(jnp.sum(x, axis=0, keepdims=True), axis=1, keepdims=True)


def total_scalars(red, count):
    row = jnp.sum(red, axis=0, keepdims=True)
    return [row[:, i : i + 1] for i in range(count)]


def fetch(pairs, sems):
    copies = [pltpu.make_async_copy(src, dst, sems.at[i]) for i, (src, dst) in enumerate(pairs)]
    for copy in copies:
        copy.start()
    return copies


def init_kernel(sz, me_ref, p_hbm, *refs):
    args, outs, held, sems, p_sem = refs[:11], refs[11:22], refs[22:33], refs[33], refs[34]
    small = fetch(list(zip(args, held)), sems)
    blocks = pltpu.make_async_copy(p_hbm, outs[10], p_sem)
    blocks.start()
    for copy in small:
        copy.wait()
    (res_ref, orders_ref, state_ref, nbr_ref, face_ref, orient_ref, source_ref, flux_ref, geo_ref, stiff_ref, trace_ref) = held
    start_ref, mask_ref, part_ref, state2_ref, hot_ref, coup_ref, turn_ref, own_ref, near_ref, back_ref = outs[:10]
    nv, nb, ne, nq, nbp, nqp = sz.nv, sz.nb, sz.ne, sz.nq, sz.nbp, sz.nqp
    orders = orders_ref[...]
    count = (orders + 1) * (orders + 2) * (orders + 3) // 6
    count = jnp.concatenate([count] * nv, axis=1)
    mask = (iota((nbp, sz.lanes), 0) < count).astype(F32)
    mask_ref[...] = mask
    start = to_wide(lambda v: res_ref[v], sz) * mask
    start_ref[...] = start
    part_ref[...] = partial_rows([full_sum(start * start)], sz.peers)
    state2_ref[...] = to_wide(lambda v: state_ref[v], sz)

    me = me_ref[0]
    nbr = nbr_ref[...]
    rel = nbr - me * ne + ne
    face, orient = face_ref[...], orient_ref[...]
    flip = (orient >= 3).astype(jnp.int32)
    choice, turn = flip * 4 + face, orient - 3 * flip

    def by_face(x):
        return jnp.concatenate([x[f : f + 1] for f in range(4)], axis=1)

    turn_ref[...] = by_face(turn)
    cols = by_face(jnp.where(nbr >= 0, choice * 4 * ne + rel, -1))
    rows = iota((8 * ne, 4 * ne), 0)
    block = rows // ne
    code = block * 4 * ne + rows - block * ne
    chip_side = jnp.where(lax.rem(me, 2) == 0, 2, 0)
    for source, side in enumerate((1, chip_side, 2 - chip_side)):
        hot_ref[source] = (code + side * ne == cols).astype(F32).astype(BF16)

    for k in range(3):
        pieces = []
        for w in range(nv):
            tile = jnp.zeros((nv, ne), F32)
            for d in range(3):
                tile = tile + geo_ref[d, k : k + 1, :] * flux_ref[d, w]
            pieces.append(tile if w == 0 else jnp.concatenate([tile[w:], tile[:w]], axis=0))
        coup_ref[k] = jnp.concatenate(pieces, axis=1)
    pieces = []
    for w in range(nv):
        tile = source_ref[w]
        pieces.append(tile if w == 0 else jnp.concatenate([tile[w:], tile[:w]], axis=0))
    coup_ref[3] = jnp.concatenate(pieces, axis=1)

    def pad2(x, rows):
        x = jnp.concatenate([x, jnp.zeros((x.shape[0], nbp - x.shape[1]), F32)], axis=1)
        return pad_rows(x, rows)

    traces = [trace_ref[:, f, :] for f in range(4)]
    plain = [pad2(t, nqp) for t in traces]
    flipped = [
        pad2(jnp.concatenate([t[q : q + 1] for q in reversed(range(nq))], axis=0), nqp) for t in traces
    ]
    volume = [pad2(stiff_ref[d], nbp) for d in range(3)]
    own_ref[...] = stack_lhs(jnp.concatenate(plain + volume, axis=0))
    near_ref[...] = stack_lhs(jnp.concatenate(plain + flipped, axis=0))
    back_ref[...] = stack_lhs(jnp.concatenate(plain, axis=0).T)
    blocks.wait()


def apply_blocks(sz, vec, mask, blocks_ref):
    nb, ne, nv, width = sz.nb, sz.ne, sz.nv, sz.width
    tall = jnp.concatenate([vec[:nb, v * ne : (v + 1) * ne] for v in range(nv)], axis=0)
    turned = pad_rows(tall, CHUNK).T
    turned = jnp.concatenate(
        [pltpu.roll(turned[g : g + 8], g * width % CHUNK, 1) if g else turned[:8] for g in range(0, ne, 8)], axis=0
    )
    row = iota((ne, 1), 0)
    for bit in (1, 2, 4):
        turned = jnp.where((row & bit) != 0, pltpu.roll(turned, bit * width % CHUNK, 1), turned)
    total = ne * width
    acc = [jnp.zeros((8, width), F32)] * (ne // 8)
    for low in range(0, total, CHUNK):
        high = min(low + CHUNK, total)
        first, last = low // width // 8, (high - 1) // width // 8 + 1
        size = (8 * (last - first), high - low)
        entry = iota(size, 1) + low - (iota(size, 0) + 8 * first) * width
        lhs = jnp.where((entry >= 0) & (entry < width), turned[8 * first : 8 * last, : high - low], 0.0)
        out = lax.dot_general(
            lhs.astype(BF16), blocks_ref[:, low:high], (((1,), (1,)), ((), ())), preferred_element_type=F32
        )
        for g in range(first, last):
            acc[g] = acc[g] + out[8 * (g - first) : 8 * (g - first + 1)]
    done = jnp.concatenate(acc, axis=0)
    done = jnp.concatenate([done, jnp.zeros((ne, CHUNK - width), F32)], axis=1).T
    wide = jnp.concatenate([done[v * nb : (v + 1) * nb] for v in range(nv)], axis=1)
    return pad_rows(wide, sz.nbp) * mask


def precond_start_kernel(sz, red_ref, vec_ref, mask_ref, blocks_ref, state_ref, z_ref, v_ref, h_ref):
    norm = jnp.sqrt(total_scalars(red_ref[...], 1)[0] + EPSILON)
    new = vec_ref[...] * (1.0 / norm)
    v_ref[...] = new
    h_ref[...] = partial_rows([norm], 1)
    z_ref[: sz.nbp] = apply_blocks(sz, new, mask_ref[...], blocks_ref)
    z_ref[sz.nbp :] = state_ref[...]


def precond_kernel(sz, step, *refs):
    red_ref, vec_ref, mask_ref, blocks_ref = refs[:4]
    basis = refs[4 : 4 + step]
    z_ref, v_ref, h_ref = refs[4 + step :]
    vec = vec_ref[...]
    scalars = total_scalars(red_ref[...], step + 1)
    proj, square = scalars[:step], scalars[step]
    for h, b in zip(proj, basis):
        vec = vec - h * b[...]
        square = square - h * h
    norm = jnp.sqrt(square + EPSILON)
    new = vec * (1.0 / norm)
    v_ref[...] = new
    h_ref[...] = partial_rows(proj + [norm], 1)
    z_ref[...] = apply_blocks(sz, new, mask_ref[...], blocks_ref)


def roll_blocks(x, blocks, ne):
    shift = blocks * ne
    if shift == 0:
        return x
    return jnp.concatenate([x[:, shift:], x[:, :shift]], axis=1)


def gather(sz, sources, hot_refs, near_ref):
    nqp, ne, pair = sz.nqp, sz.ne, sz.pair
    low_half = iota((1, pair), 1) < ne
    lhs = []
    for source in sources:
        every = dot(near_ref[...], stack_rhs(split3(source), 0))
        rows = []
        for v in range(sz.nv):
            column = every[:, v // 2 * pair : (v // 2 + 1) * pair]
            turned = pltpu.roll(column, ne, 1)
            pieces = []
            for g in range(0, 8, 2):
                first, second = (slice((g + i) * nqp, (g + i + 1) * nqp) for i in range(2))
                if v % 2 == 0:
                    pieces.append(jnp.where(low_half, column[first], turned[second]))
                else:
                    pieces.append(jnp.where(low_half, turned[first], column[second]))
            rows.append(jnp.concatenate(pieces, axis=1))
        lhs.append(jnp.concatenate(rows, axis=0))
    lhs = split3(jnp.concatenate(lhs, axis=1))
    hot = jnp.concatenate([ref[...] for ref in hot_refs], axis=0)
    got = dot(jnp.concatenate(lhs, axis=0).astype(BF16), hot)
    size = sz.nv * nqp
    return got[:size] + got[size : 2 * size] + got[2 * size :]


def to_faces(sz, seen, turn):
    nqp, ne, pair = sz.nqp, sz.ne, sz.pair
    low_half = iota((1, pair), 1) < ne
    nq, third = sz.nq, sz.nq // 3
    turned = []
    for v in range(sz.nv):
        tr = seen[v * nqp : (v + 1) * nqp]
        fill = tr[nq:]
        once = jnp.concatenate([tr[third:nq], tr[:third], fill], axis=0)
        twice = jnp.concatenate([tr[2 * third : nq], tr[: 2 * third], fill], axis=0)
        turned.append(jnp.where(turn == 0, tr, jnp.where(turn == 1, once, twice)))
    result = []
    for f in range(4):
        start = f // 2 * pair
        blocks = []
        for p in range(sz.lanes // pair):
            first, second = (turned[2 * p + i][:, start : start + pair] for i in range(2))
            if f % 2 == 0:
                second = pltpu.roll(second, ne, 1)
            else:
                first = pltpu.roll(first, ne, 1)
            blocks.append(jnp.where(low_half, first, second))
        result.append(jnp.concatenate(blocks, axis=1))
    return jnp.concatenate(result, axis=0)


def spread(row, i):
    return jnp.broadcast_to(row[:, i : i + 1], (1, 128))


def rotate_column(step, row, square, turns_ref):
    entries = [spread(row, i) for i in range(step + 2)]
    if square:
        rest = entries[step + 1]
        for h in entries[:-1]:
            rest = rest - h * h
        entries[step + 1] = jnp.sqrt(rest + EPSILON)
    column = list(entries)
    for i in range(step):
        cosine, sine = turns_ref[2 * i : 2 * i + 1, :], turns_ref[2 * i + 1 : 2 * i + 2, :]
        top, low = column[i], column[i + 1]
        column[i] = cosine * top + sine * low
        column[i + 1] = cosine * low - sine * top
    lead, below = column[step], column[step + 1]
    radius = jnp.sqrt(lead * lead + below * below)
    cosine, sine = lead / radius, below / radius
    column[step] = cosine * lead + sine * below
    return entries, column, cosine, sine


def direction(sz, search, column, earlier):
    def across(x):
        return jnp.concatenate([x] * (sz.lanes // 128), axis=1)

    total = search
    for r, ref in zip(column, earlier):
        total = total - across(r) * ref[...]
    return total * across(1.0 / column[len(earlier)]), across


def fill_column(step, entries, hess):
    row_id, col_id = iota(hess.shape, 0), iota(hess.shape, 1)
    for i, entry in enumerate(entries):
        hess = jnp.where((row_id == i) & (col_id == step), entry[:, : hess.shape[1]], hess)
    return hess


def local_kernel(sz, z_ref, own_ref, coup_ref, vol_ref, tr_ref):
    search = z_ref[: sz.nbp]
    out = dot(own_ref[...], stack_rhs(split3(search), 0))
    faces = 4 * sz.nqp
    tr_ref[...] = out[:faces]
    acc = jnp.zeros((sz.nbp, sz.lanes), F32)
    for d in range(4):
        moved = search if d == 3 else out[faces + d * sz.nbp : faces + (d + 1) * sz.nbp]
        for s in range(sz.nv):
            acc = acc + coup_ref[d, s : s + 1, :] * roll_blocks(moved, s, sz.ne)
    vol_ref[...] = acc


def column_kernel(sz, step, *refs):
    head_ref, z_ref, turns_ref, hess_ref, sum_ref = refs[:5]
    earlier = refs[5 : 5 + step]
    turns_out, hess_out, sum_out, dir_ref = refs[5 + step :]
    entries, column, cosine, sine = rotate_column(step, head_ref[...], False, turns_ref)
    new, across = direction(sz, z_ref[: sz.nbp], column, earlier)
    dir_ref[...] = new
    last = turns_ref.shape[0] - 1
    right = spread(turns_ref[last:, :], 0) if step == 0 else turns_ref[last:, :]
    value = across(cosine * right) * new
    if step == 0:
        sum_out[...] = value
        hess = jnp.zeros(hess_out.shape, F32)
        turns_out[...] = jnp.zeros(turns_out.shape, F32)
    else:
        sum_out[...] = sum_ref[...] + value
        hess = hess_ref[...]
        turns_out[...] = turns_ref[...]
    hess_out[...] = fill_column(step, entries, hess)
    turns_out[2 * step : 2 * step + 1, :] = cosine
    turns_out[2 * step + 1 : 2 * step + 2, :] = sine
    turns_out[turns_out.shape[0] - 1 :, :] = -(sine * right)


def finish_kernel(sz, *refs):
    red_ref, z_ref, turns_ref, hess_ref, sum_ref = refs[:5]
    step = ITERS - 1
    earlier = refs[5 : 5 + step]
    out_ref, hess_out = refs[5 + step :]
    row = jnp.sum(red_ref[...], axis=0, keepdims=True)
    entries, column, cosine, sine = rotate_column(step, row, True, turns_ref)
    new, across = direction(sz, z_ref[...], column, earlier)
    last = turns_ref.shape[0] - 1
    total = sum_ref[...] + across(cosine * turns_ref[last:, :]) * new
    for v in range(sz.nv):
        out_ref[v] = total[: sz.nb, v * sz.ne : (v + 1) * sz.ne]
    hess_out[...] = fill_column(step, entries, hess_ref[...])[: ITERS + 1, :ITERS]


def near_column_kernel(sz, step, *refs):
    near_kernel(sz, *refs[:4], refs[8 + step])
    column_kernel(sz, step - 1, *refs[4 : 8 + step], *refs[9 + step :])


def near_kernel(sz, z_ref, chip_ref, hot_ref, near_ref, *outs):
    nbp = sz.nbp
    for i, out_ref in enumerate(outs):
        sources = [ref[i * nbp : (i + 1) * nbp] for ref in (z_ref, chip_ref)]
        out_ref[...] = gather(sz, sources, [hot_ref.at[0], hot_ref.at[1]], near_ref)


def image_kernel(sz, step, *refs):
    far_ref, hot_ref, near_ref, turn_ref, seen_ref, gain_ref, back_ref, vol_ref, tr_ref, mask_ref = refs[:10]
    basis, refs = refs[10 : 11 + step], refs[11 + step :]
    nbp, turn = sz.nbp, turn_ref[...]
    if step == 0:
        z_ref, own_ref, refs = refs[0], refs[1], refs[2:]
        own = dot(own_ref[: 4 * sz.nqp], stack_rhs(split3(z_ref[nbp:]), 0))
        seen = gain_ref[...] + gather(sz, [far_ref[nbp:]], [hot_ref.at[2]], near_ref)
        gain = 1.0 + 0.5 * jnp.abs(own + to_faces(sz, seen, turn))
        refs[2][...] = gain
    else:
        gain = gain_ref[...]
    seen = seen_ref[...] + gather(sz, [far_ref[:nbp]], [hot_ref.at[2]], near_ref)
    flux = gain * (tr_ref[...] - to_faces(sz, seen, turn))
    face = dot(back_ref[...], stack_rhs(split3(flux), 0))
    image = (vol_ref[...] + face) * mask_ref[...]
    if step < ITERS - 1:
        refs[1][...] = image
    values = [full_sum(b[...] * image) for b in basis] + [full_sum(image * image)]
    refs[0][...] = partial_rows(values, sz.peers)


def call(kernel, name, out_shape, *args, specs=None, scratch=(), limit=24 * 2**20):
    return pl.pallas_call(
        kernel,
        name=name,
        out_shape=out_shape,
        in_specs=specs or [VMEM] * len(args),
        out_specs=jax.tree.map(lambda _: VMEM, out_shape),
        scratch_shapes=list(scratch),
        compiler_params=pltpu.CompilerParams(vmem_limit_bytes=limit),
    )(*args)


def shape(*dims, dtype=F32):
    return jax.ShapeDtypeStruct(dims, dtype)


def copied(arrays):
    return [pltpu.VMEM(a.shape, a.dtype) for a in arrays] + [pltpu.SemaphoreType.DMA((len(arrays),))]


def body(
    peers, state_coeffs, residual_in, orders, neighbours, neighbour_face, orientation, precond, source,
    flux_jacobian, geometry, stiffness, trace_matrix,
):
    nv, nb, ne = state_coeffs.shape
    sz = Sizes(nv, nb, ne, trace_matrix.shape[1], peers)
    lanes, nbp, nqp = sz.lanes, sz.nbp, sz.nqp
    me = lax.axis_index(AXES).astype(jnp.int32).reshape(1)
    wide = shape(nbp, lanes)
    parts = pltpu.VMEM((peers, 128), F32)
    fetched = [
        residual_in, orders.reshape(1, ne), state_coeffs, neighbours, neighbour_face, orientation, source, flux_jacobian,
        geometry, stiffness, jnp.transpose(trace_matrix, (1, 0, 2)),
    ]
    start, mask, part, state, hot, coup, turn, own, near, back, blocks = call(
        functools.partial(init_kernel, sz),
        "init",
        (
            wide, wide, parts, wide,
            shape(3, 8 * ne, 4 * ne, dtype=BF16),
            shape(4, nv, lanes),
            shape(1, 4 * ne, dtype=jnp.int32),
            shape(4 * nqp + 3 * nbp, 6 * nbp, dtype=BF16),
            shape(8 * nqp, 6 * nbp, dtype=BF16),
            shape(nbp, 24 * nqp, dtype=BF16),
            shape(*precond.shape, dtype=BF16),
        ),
        me, *[pltpu.with_memory_space_constraint(a, pltpu.HBM) for a in [precond] + fetched],
        specs=[SMEM] + [ANY] * (1 + len(fetched)), scratch=copied(fetched) + [pltpu.SemaphoreType.DMA],
    )

    def exchange(rows):
        return lax.all_to_all(rows, AXES, 0, 0, tiled=True)

    on_chip = [(i, i ^ 1) for i in range(peers)]
    odd = range(1, peers - 1, 2)
    off_chip = [(i, i + 1) for i in odd] + [(i + 1, i) for i in odd]

    basis, directions = [], []
    vec, gain = start, None
    turns = hess = total = None
    face_shape, seen_shape = shape(4 * nqp, lanes), shape(nv * nqp, 4 * ne)
    state_shapes = (shape(2 * ITERS + 4, 128), shape(8, 128), wide, wide)
    for k in range(ITERS):
        red = exchange(part)
        previous = None if k == 0 else search
        if k == 0:
            search, new, head = call(
                functools.partial(precond_start_kernel, sz), "precond0", (shape(2 * nbp, lanes), wide, shape(1, 128)),
                red, vec, mask, blocks, state,
            )
        else:
            search, new, head = call(
                functools.partial(precond_kernel, sz, k), f"precond{k}", (wide, wide, shape(1, 128)),
                red, vec, mask, blocks, *basis,
            )
        basis = basis + [new]
        far = lax.ppermute(search, AXES, off_chip)
        chip = lax.ppermute(search, AXES, on_chip)
        vol, tr = call(functools.partial(local_kernel, sz), "local", (wide, face_shape), search, own, coup)
        if k == 0:
            turns, hess, total = head, head, head
            seen, gain = call(
                functools.partial(near_kernel, sz), "near", (seen_shape, seen_shape), search, chip, hot, near
            )
        else:
            seen, turns, hess, total, new = call(
                functools.partial(near_column_kernel, sz, k), f"near{k}", (seen_shape,) + state_shapes,
                search, chip, hot, near, head, previous, turns, hess, total, *directions,
            )
            directions = directions + [new]
        extra = basis + ([search, own] if k == 0 else [])
        shapes = (parts,) if k == ITERS - 1 else (parts, wide, face_shape)[: 3 if k == 0 else 2]
        outs = call(
            functools.partial(image_kernel, sz, k), f"image{k}", shapes,
            far, hot, near, turn, seen, gain, back, vol, tr, mask, *extra,
        )
        part, vec = outs[0], outs[1 % len(outs)]
        gain = outs[2] if k == 0 else gain
    red = exchange(part)
    return call(
        functools.partial(finish_kernel, sz), "finish", (shape(nv, nb, ne), shape(ITERS + 1, ITERS)),
        red, search, turns, hess, total, *directions,
    )


def solution(mesh):
    placed = (
        P(None, None, AXES),
        P(None, None, AXES),
        P(AXES),
        P(None, AXES),
        P(None, AXES),
        P(None, AXES),
        P(None, AXES),
        P(None, None, AXES),
        P(None, None, None, AXES),
        P(None, None, AXES),
        P(),
        P(),
    )
    peers = 1
    for axis in AXES:
        peers *= mesh.shape[axis]
    return jax.shard_map(
        functools.partial(body, peers),
        mesh=mesh,
        in_specs=placed,
        out_specs=(P(None, None, AXES), P()),
        check_vma=False,
    )
```

```python
import functools

import jax
import jax.numpy as jnp
from jax import lax
from jax.experimental import pallas as pl
from jax.experimental.pallas import tpu as pltpu
from jax.sharding import PartitionSpec as P

ITERS = 6
EPSILON = 1e-06
AXES = ("dom", "grp")
F32 = jnp.float32
BF16 = jnp.bfloat16
CHUNK = 256
SIDE_TILES = 2
VMEM = pl.BlockSpec(memory_space=pltpu.VMEM)
ANY = pl.BlockSpec(memory_space=pl.ANY)
SMEM = pl.BlockSpec(memory_space=pltpu.SMEM)


def ceil_to(n, m):
    return -(-n // m) * m


def iota(shape, dim):
    return lax.broadcasted_iota(jnp.int32, shape, dim)


def split3(x):
    hi = x.astype(BF16).astype(F32)
    rest = x - hi
    mid = rest.astype(BF16).astype(F32)
    return hi, mid, rest - mid


def stack_rhs(parts, axis):
    hi, mid, lo = parts
    return jnp.concatenate([hi, mid, lo, hi, mid, hi], axis=axis).astype(BF16)


def stack_lhs(x):
    hi, mid, lo = split3(x)
    return jnp.concatenate([hi, hi, hi, mid, mid, lo], axis=1).astype(BF16)


def dot(a, b):
    return jnp.dot(a, b, preferred_element_type=F32)


def pad_rows(x, rows):
    return jnp.concatenate([x, jnp.zeros((rows - x.shape[0], x.shape[1]), x.dtype)], axis=0)


class Sizes:
    def __init__(self, nv, nb, ne, nq, peers):
        self.nv, self.nb, self.ne, self.nq, self.peers = nv, nb, ne, nq, peers
        self.nbp = ceil_to(nb, 8)
        self.nqp = ceil_to(nq, 8)
        self.lanes = nv * ne
        self.width = nv * nb
        self.kwidth = ceil_to(self.width, 128)
        self.pair = 2 * ne


def to_wide(read, sz):
    return pad_rows(jnp.concatenate([read(v) for v in range(sz.nv)], axis=1), sz.nbp)


def partial_rows(values, peers):
    lane = iota((1, 128), 1)
    row = jnp.zeros((1, 128), F32)
    for i, val in enumerate(values):
        row = jnp.where(lane == i, val, row)
    return jnp.broadcast_to(row, (peers, 128))


def full_sum(x):
    return jnp.sum(jnp.sum(x, axis=0, keepdims=True), axis=1, keepdims=True)


def total_scalars(red, count):
    row = jnp.sum(red, axis=0, keepdims=True)
    return [row[:, i : i + 1] for i in range(count)]


def fetch(pairs, sems):
    copies = [pltpu.make_async_copy(src, dst, sems.at[i]) for i, (src, dst) in enumerate(pairs)]
    for copy in copies:
        copy.start()
    return copies


def init_kernel(sz, me_ref, p_hbm, *refs):
    args, outs, held, sems, p_sem = refs[:11], refs[11:22], refs[22:33], refs[33], refs[34]
    small = fetch(list(zip(args, held)), sems)
    blocks = pltpu.make_async_copy(p_hbm, outs[10], p_sem)
    blocks.start()
    for copy in small:
        copy.wait()
    (res_ref, orders_ref, state_ref, nbr_ref, face_ref, orient_ref, source_ref, flux_ref, geo_ref, stiff_ref, trace_ref) = held
    start_ref, mask_ref, part_ref, state2_ref, hot_ref, coup_ref, turn_ref, own_ref, near_ref, back_ref = outs[:10]
    nv, nb, ne, nq, nbp, nqp = sz.nv, sz.nb, sz.ne, sz.nq, sz.nbp, sz.nqp
    orders = orders_ref[...]
    count = (orders + 1) * (orders + 2) * (orders + 3) // 6
    count = jnp.concatenate([count] * nv, axis=1)
    mask = (iota((nbp, sz.lanes), 0) < count).astype(F32)
    mask_ref[...] = mask
    start = to_wide(lambda v: res_ref[v], sz) * mask
    start_ref[...] = start
    part_ref[...] = partial_rows([full_sum(start * start)], sz.peers)
    state2_ref[...] = to_wide(lambda v: state_ref[v], sz)

    me = me_ref[0]
    nbr = nbr_ref[...]
    rel = nbr - me * ne + ne
    face, orient = face_ref[...], orient_ref[...]
    flip = (orient >= 3).astype(jnp.int32)
    choice, turn = flip * 4 + face, orient - 3 * flip

    def by_face(x):
        return jnp.concatenate([x[f : f + 1] for f in range(4)], axis=1)

    turn_ref[...] = by_face(turn)
    cols = by_face(jnp.where(nbr >= 0, choice * 4 * ne + rel, -1))
    rows = iota((8 * ne, 4 * ne), 0)
    block = rows // ne
    code = block * 4 * ne + rows - block * ne
    chip_side = jnp.where(lax.rem(me, 2) == 0, 2, 0)
    for source, side in enumerate((1, chip_side, 2 - chip_side)):
        hot_ref[source] = (code + side * ne == cols).astype(F32).astype(BF16)

    for k in range(3):
        pieces = []
        for w in range(nv):
            tile = jnp.zeros((nv, ne), F32)
            for d in range(3):
                tile = tile + geo_ref[d, k : k + 1, :] * flux_ref[d, w]
            pieces.append(tile if w == 0 else jnp.concatenate([tile[w:], tile[:w]], axis=0))
        coup_ref[k] = jnp.concatenate(pieces, axis=1)
    pieces = []
    for w in range(nv):
        tile = source_ref[w]
        pieces.append(tile if w == 0 else jnp.concatenate([tile[w:], tile[:w]], axis=0))
    coup_ref[3] = jnp.concatenate(pieces, axis=1)

    def pad2(x, rows):
        x = jnp.concatenate([x, jnp.zeros((x.shape[0], nbp - x.shape[1]), F32)], axis=1)
        return pad_rows(x, rows)

    traces = [trace_ref[:, f, :] for f in range(4)]
    plain = [pad2(t, nqp) for t in traces]
    flipped = [
        pad2(jnp.concatenate([t[q : q + 1] for q in reversed(range(nq))], axis=0), nqp) for t in traces
    ]
    volume = [pad2(stiff_ref[d], nbp) for d in range(3)]
    own_ref[...] = stack_lhs(jnp.concatenate(plain + volume, axis=0))
    near_ref[...] = stack_lhs(jnp.concatenate(plain + flipped, axis=0))
    back_ref[...] = stack_lhs(jnp.concatenate(plain, axis=0).T)
    blocks.wait()


def apply_blocks(sz, vec, mask, blocks_ref):
    nb, ne, nv, width = sz.nb, sz.ne, sz.nv, sz.width
    tall = jnp.concatenate([vec[:nb, v * ne : (v + 1) * ne] for v in range(nv)], axis=0)
    turned = pad_rows(tall, CHUNK).T
    turned = jnp.concatenate(
        [pltpu.roll(turned[g : g + 8], g * width % CHUNK, 1) if g else turned[:8] for g in range(0, ne, 8)], axis=0
    )
    row = iota((ne, 1), 0)
    for bit in (1, 2, 4):
        turned = jnp.where((row & bit) != 0, pltpu.roll(turned, bit * width % CHUNK, 1), turned)
    total, main = ne * width, (width // 16 - SIDE_TILES) * 16
    side_rows = width - main
    acc = [jnp.zeros((8, main), F32)] * (ne // 8)
    side = jnp.zeros((side_rows, ne), F32)
    side_acc = jnp.zeros((side_rows, 128), F32)
    lane = iota((1, ne), 1)
    for low in range(0, total, CHUNK):
        high = min(low + CHUNK, total)
        first, last = low // width // 8, (high - 1) // width // 8 + 1
        size = (8 * (last - first), high - low)
        entry = iota(size, 1) + low - (iota(size, 0) + 8 * first) * width
        lhs = jnp.where((entry >= 0) & (entry < width), turned[8 * first : 8 * last, : high - low], 0.0).astype(BF16)
        out = lax.dot_general(
            lhs, blocks_ref[:main, low:high], (((1,), (1,)), ((), ())), preferred_element_type=F32
        )
        for g in range(first, last):
            acc[g] = acc[g] + out[8 * (g - first) : 8 * (g - first + 1)]
        rows = lhs.astype(F32)
        for start in range(low, high, 128):
            tile = blocks_ref[main:, start : start + 128].astype(F32)
            for e in range(start // width, (start + 127) // width + 1):
                values = rows[e - 8 * first : e - 8 * first + 1, start - low : start - low + 128]
                side_acc = side_acc + tile * values
                if (e + 1) * width <= start + 128:
                    side = jnp.where(lane == e, jnp.sum(side_acc, axis=1, keepdims=True), side)
                    side_acc = jnp.zeros((side_rows, 128), F32)
    done = jnp.concatenate(acc, axis=0)
    done = jnp.concatenate([done, jnp.zeros((ne, CHUNK - main), F32)], axis=1).T
    done = jnp.concatenate([done[:main], side], axis=0)
    wide = jnp.concatenate([done[v * nb : (v + 1) * nb] for v in range(nv)], axis=1)
    return pad_rows(wide, sz.nbp) * mask


def precond_start_kernel(sz, red_ref, vec_ref, mask_ref, blocks_ref, state_ref, z_ref, v_ref, h_ref):
    norm = jnp.sqrt(total_scalars(red_ref[...], 1)[0] + EPSILON)
    new = vec_ref[...] * (1.0 / norm)
    v_ref[...] = new
    h_ref[...] = partial_rows([norm], 1)
    z_ref[: sz.nbp] = apply_blocks(sz, new, mask_ref[...], blocks_ref)
    z_ref[sz.nbp :] = state_ref[...]


def precond_kernel(sz, step, *refs):
    red_ref, vec_ref, mask_ref, blocks_ref = refs[:4]
    basis = refs[4 : 4 + step]
    z_ref, v_ref, h_ref = refs[4 + step :]
    vec = vec_ref[...]
    scalars = total_scalars(red_ref[...], step + 1)
    proj, square = scalars[:step], scalars[step]
    for h, b in zip(proj, basis):
        vec = vec - h * b[...]
        square = square - h * h
    norm = jnp.sqrt(square + EPSILON)
    new = vec * (1.0 / norm)
    v_ref[...] = new
    h_ref[...] = partial_rows(proj + [norm], 1)
    z_ref[...] = apply_blocks(sz, new, mask_ref[...], blocks_ref)


def roll_blocks(x, blocks, ne):
    shift = blocks * ne
    if shift == 0:
        return x
    return jnp.concatenate([x[:, shift:], x[:, :shift]], axis=1)


def gather(sz, sources, hot_refs, near_ref):
    nqp, ne, pair = sz.nqp, sz.ne, sz.pair
    low_half = iota((1, pair), 1) < ne
    lhs = []
    for source in sources:
        every = dot(near_ref[...], stack_rhs(split3(source), 0))
        rows = []
        for v in range(sz.nv):
            column = every[:, v // 2 * pair : (v // 2 + 1) * pair]
            turned = pltpu.roll(column, ne, 1)
            pieces = []
            for g in range(0, 8, 2):
                first, second = (slice((g + i) * nqp, (g + i + 1) * nqp) for i in range(2))
                if v % 2 == 0:
                    pieces.append(jnp.where(low_half, column[first], turned[second]))
                else:
                    pieces.append(jnp.where(low_half, turned[first], column[second]))
            rows.append(jnp.concatenate(pieces, axis=1))
        lhs.append(jnp.concatenate(rows, axis=0))
    lhs = split3(jnp.concatenate(lhs, axis=1))
    hot = jnp.concatenate([ref[...] for ref in hot_refs], axis=0)
    got = dot(jnp.concatenate(lhs, axis=0).astype(BF16), hot)
    size = sz.nv * nqp
    return got[:size] + got[size : 2 * size] + got[2 * size :]


def to_faces(sz, seen, turn):
    nqp, ne, pair = sz.nqp, sz.ne, sz.pair
    low_half = iota((1, pair), 1) < ne
    nq, third = sz.nq, sz.nq // 3
    turned = []
    for v in range(sz.nv):
        tr = seen[v * nqp : (v + 1) * nqp]
        fill = tr[nq:]
        once = jnp.concatenate([tr[third:nq], tr[:third], fill], axis=0)
        twice = jnp.concatenate([tr[2 * third : nq], tr[: 2 * third], fill], axis=0)
        turned.append(jnp.where(turn == 0, tr, jnp.where(turn == 1, once, twice)))
    result = []
    for f in range(4):
        start = f // 2 * pair
        blocks = []
        for p in range(sz.lanes // pair):
            first, second = (turned[2 * p + i][:, start : start + pair] for i in range(2))
            if f % 2 == 0:
                second = pltpu.roll(second, ne, 1)
            else:
                first = pltpu.roll(first, ne, 1)
            blocks.append(jnp.where(low_half, first, second))
        result.append(jnp.concatenate(blocks, axis=1))
    return jnp.concatenate(result, axis=0)


def spread(row, i):
    return jnp.broadcast_to(row[:, i : i + 1], (1, 128))


def rotate_column(step, row, square, turns_ref):
    entries = [spread(row, i) for i in range(step + 2)]
    if square:
        rest = entries[step + 1]
        for h in entries[:-1]:
            rest = rest - h * h
        entries[step + 1] = jnp.sqrt(rest + EPSILON)
    column = list(entries)
    for i in range(step):
        cosine, sine = turns_ref[2 * i : 2 * i + 1, :], turns_ref[2 * i + 1 : 2 * i + 2, :]
        top, low = column[i], column[i + 1]
        column[i] = cosine * top + sine * low
        column[i + 1] = cosine * low - sine * top
    lead, below = column[step], column[step + 1]
    radius = jnp.sqrt(lead * lead + below * below)
    cosine, sine = lead / radius, below / radius
    column[step] = cosine * lead + sine * below
    return entries, column, cosine, sine


def direction(sz, search, column, earlier):
    def across(x):
        return jnp.concatenate([x] * (sz.lanes // 128), axis=1)

    total = search
    for r, ref in zip(column, earlier):
        total = total - across(r) * ref[...]
    return total * across(1.0 / column[len(earlier)]), across


def fill_column(step, entries, hess):
    row_id, col_id = iota(hess.shape, 0), iota(hess.shape, 1)
    for i, entry in enumerate(entries):
        hess = jnp.where((row_id == i) & (col_id == step), entry[:, : hess.shape[1]], hess)
    return hess


def local_kernel(sz, z_ref, own_ref, coup_ref, vol_ref, tr_ref):
    search = z_ref[: sz.nbp]
    out = dot(own_ref[...], stack_rhs(split3(search), 0))
    faces = 4 * sz.nqp
    tr_ref[...] = out[:faces]
    acc = jnp.zeros((sz.nbp, sz.lanes), F32)
    for d in range(4):
        moved = search if d == 3 else out[faces + d * sz.nbp : faces + (d + 1) * sz.nbp]
        for s in range(sz.nv):
            acc = acc + coup_ref[d, s : s + 1, :] * roll_blocks(moved, s, sz.ne)
    vol_ref[...] = acc


def column_kernel(sz, step, *refs):
    head_ref, z_ref, turns_ref, hess_ref, sum_ref = refs[:5]
    earlier = refs[5 : 5 + step]
    turns_out, hess_out, sum_out, dir_ref = refs[5 + step :]
    entries, column, cosine, sine = rotate_column(step, head_ref[...], False, turns_ref)
    new, across = direction(sz, z_ref[: sz.nbp], column, earlier)
    dir_ref[...] = new
    last = turns_ref.shape[0] - 1
    right = spread(turns_ref[last:, :], 0) if step == 0 else turns_ref[last:, :]
    value = across(cosine * right) * new
    if step == 0:
        sum_out[...] = value
        hess = jnp.zeros(hess_out.shape, F32)
        turns_out[...] = jnp.zeros(turns_out.shape, F32)
    else:
        sum_out[...] = sum_ref[...] + value
        hess = hess_ref[...]
        turns_out[...] = turns_ref[...]
    hess_out[...] = fill_column(step, entries, hess)
    turns_out[2 * step : 2 * step + 1, :] = cosine
    turns_out[2 * step + 1 : 2 * step + 2, :] = sine
    turns_out[turns_out.shape[0] - 1 :, :] = -(sine * right)


def finish_kernel(sz, *refs):
    red_ref, z_ref, turns_ref, hess_ref, sum_ref = refs[:5]
    step = ITERS - 1
    earlier = refs[5 : 5 + step]
    out_ref, hess_out = refs[5 + step :]
    row = jnp.sum(red_ref[...], axis=0, keepdims=True)
    entries, column, cosine, sine = rotate_column(step, row, True, turns_ref)
    new, across = direction(sz, z_ref[...], column, earlier)
    last = turns_ref.shape[0] - 1
    total = sum_ref[...] + across(cosine * turns_ref[last:, :]) * new
    for v in range(sz.nv):
        out_ref[v] = total[: sz.nb, v * sz.ne : (v + 1) * sz.ne]
    hess_out[...] = fill_column(step, entries, hess_ref[...])[: ITERS + 1, :ITERS]


def near_column_kernel(sz, step, *refs):
    near_kernel(sz, *refs[:4], refs[8 + step])
    column_kernel(sz, step - 1, *refs[4 : 8 + step], *refs[9 + step :])


def near_kernel(sz, z_ref, chip_ref, hot_ref, near_ref, *outs):
    nbp = sz.nbp
    for i, out_ref in enumerate(outs):
        sources = [ref[i * nbp : (i + 1) * nbp] for ref in (z_ref, chip_ref)]
        out_ref[...] = gather(sz, sources, [hot_ref.at[0], hot_ref.at[1]], near_ref)


def image_kernel(sz, step, *refs):
    far_ref, hot_ref, near_ref, turn_ref, seen_ref, gain_ref, back_ref, vol_ref, tr_ref, mask_ref = refs[:10]
    basis, refs = refs[10 : 11 + step], refs[11 + step :]
    nbp, turn = sz.nbp, turn_ref[...]
    if step == 0:
        z_ref, own_ref, refs = refs[0], refs[1], refs[2:]
        own = dot(own_ref[: 4 * sz.nqp], stack_rhs(split3(z_ref[nbp:]), 0))
        seen = gain_ref[...] + gather(sz, [far_ref[nbp:]], [hot_ref.at[2]], near_ref)
        gain = 1.0 + 0.5 * jnp.abs(own + to_faces(sz, seen, turn))
        refs[2][...] = gain
    else:
        gain = gain_ref[...]
    seen = seen_ref[...] + gather(sz, [far_ref[:nbp]], [hot_ref.at[2]], near_ref)
    flux = gain * (tr_ref[...] - to_faces(sz, seen, turn))
    face = dot(back_ref[...], stack_rhs(split3(flux), 0))
    image = (vol_ref[...] + face) * mask_ref[...]
    if step < ITERS - 1:
        refs[1][...] = image
    values = [full_sum(b[...] * image) for b in basis] + [full_sum(image * image)]
    refs[0][...] = partial_rows(values, sz.peers)


def call(kernel, name, out_shape, *args, specs=None, scratch=(), limit=24 * 2**20):
    return pl.pallas_call(
        kernel,
        name=name,
        out_shape=out_shape,
        in_specs=specs or [VMEM] * len(args),
        out_specs=jax.tree.map(lambda _: VMEM, out_shape),
        scratch_shapes=list(scratch),
        compiler_params=pltpu.CompilerParams(vmem_limit_bytes=limit),
    )(*args)


def shape(*dims, dtype=F32):
    return jax.ShapeDtypeStruct(dims, dtype)


def copied(arrays):
    return [pltpu.VMEM(a.shape, a.dtype) for a in arrays] + [pltpu.SemaphoreType.DMA((len(arrays),))]


def body(
    peers, state_coeffs, residual_in, orders, neighbours, neighbour_face, orientation, precond, source,
    flux_jacobian, geometry, stiffness, trace_matrix,
):
    nv, nb, ne = state_coeffs.shape
    sz = Sizes(nv, nb, ne, trace_matrix.shape[1], peers)
    lanes, nbp, nqp = sz.lanes, sz.nbp, sz.nqp
    me = lax.axis_index(AXES).astype(jnp.int32).reshape(1)
    wide = shape(nbp, lanes)
    parts = pltpu.VMEM((peers, 128), F32)
    fetched = [
        residual_in, orders.reshape(1, ne), state_coeffs, neighbours, neighbour_face, orientation, source, flux_jacobian,
        geometry, stiffness, jnp.transpose(trace_matrix, (1, 0, 2)),
    ]
    start, mask, part, state, hot, coup, turn, own, near, back, blocks = call(
        functools.partial(init_kernel, sz),
        "init",
        (
            wide, wide, parts, wide,
            shape(3, 8 * ne, 4 * ne, dtype=BF16),
            shape(4, nv, lanes),
            shape(1, 4 * ne, dtype=jnp.int32),
            shape(4 * nqp + 3 * nbp, 6 * nbp, dtype=BF16),
            shape(8 * nqp, 6 * nbp, dtype=BF16),
            shape(nbp, 24 * nqp, dtype=BF16),
            shape(*precond.shape, dtype=BF16),
        ),
        me, *[pltpu.with_memory_space_constraint(a, pltpu.HBM) for a in [precond] + fetched],
        specs=[SMEM] + [ANY] * (1 + len(fetched)), scratch=copied(fetched) + [pltpu.SemaphoreType.DMA],
    )

    def exchange(rows):
        return lax.all_to_all(rows, AXES, 0, 0, tiled=True)

    on_chip = [(i, i ^ 1) for i in range(peers)]
    odd = range(1, peers - 1, 2)
    off_chip = [(i, i + 1) for i in odd] + [(i + 1, i) for i in odd]

    basis, directions = [], []
    vec, gain = start, None
    turns = hess = total = None
    face_shape, seen_shape = shape(4 * nqp, lanes), shape(nv * nqp, 4 * ne)
    state_shapes = (shape(2 * ITERS + 4, 128), shape(8, 128), wide, wide)
    for k in range(ITERS):
        red = exchange(part)
        previous = None if k == 0 else search
        if k == 0:
            search, new, head = call(
                functools.partial(precond_start_kernel, sz), "precond0", (shape(2 * nbp, lanes), wide, shape(1, 128)),
                red, vec, mask, blocks, state,
            )
        else:
            search, new, head = call(
                functools.partial(precond_kernel, sz, k), f"precond{k}", (wide, wide, shape(1, 128)),
                red, vec, mask, blocks, *basis,
            )
        basis = basis + [new]
        far = lax.ppermute(search, AXES, off_chip)
        chip = lax.ppermute(search, AXES, on_chip)
        vol, tr = call(functools.partial(local_kernel, sz), "local", (wide, face_shape), search, own, coup)
        if k == 0:
            turns, hess, total = head, head, head
            seen, gain = call(
                functools.partial(near_kernel, sz), "near", (seen_shape, seen_shape), search, chip, hot, near
            )
        else:
            seen, turns, hess, total, new = call(
                functools.partial(near_column_kernel, sz, k), f"near{k}", (seen_shape,) + state_shapes,
                search, chip, hot, near, head, previous, turns, hess, total, *directions,
            )
            directions = directions + [new]
        extra = basis + ([search, own] if k == 0 else [])
        shapes = (parts,) if k == ITERS - 1 else (parts, wide, face_shape)[: 3 if k == 0 else 2]
        outs = call(
            functools.partial(image_kernel, sz, k), f"image{k}", shapes,
            far, hot, near, turn, seen, gain, back, vol, tr, mask, *extra,
        )
        part, vec = outs[0], outs[1 % len(outs)]
        gain = outs[2] if k == 0 else gain
    red = exchange(part)
    return call(
        functools.partial(finish_kernel, sz), "finish", (shape(nv, nb, ne), shape(ITERS + 1, ITERS)),
        red, search, turns, hess, total, *directions,
    )


def solution(mesh):
    placed = (
        P(None, None, AXES),
        P(None, None, AXES),
        P(AXES),
        P(None, AXES),
        P(None, AXES),
        P(None, AXES),
        P(None, AXES),
        P(None, None, AXES),
        P(None, None, None, AXES),
        P(None, None, AXES),
        P(),
        P(),
    )
    peers = 1
    for axis in AXES:
        peers *= mesh.shape[axis]
    return jax.shard_map(
        functools.partial(body, peers),
        mesh=mesh,
        in_specs=placed,
        out_specs=(P(None, None, AXES), P()),
        check_vma=False,
    )
```

```python
import functools

import jax
import jax.numpy as jnp
from jax import lax
from jax.experimental import pallas as pl
from jax.experimental.pallas import tpu as pltpu
from jax.sharding import PartitionSpec as P

ITERS = 6
EPSILON = 1e-06
AXES = ("dom", "grp")
F32 = jnp.float32
BF16 = jnp.bfloat16
CHUNK = 256
SIDE_TILES = 3
VMEM = pl.BlockSpec(memory_space=pltpu.VMEM)
ANY = pl.BlockSpec(memory_space=pl.ANY)
SMEM = pl.BlockSpec(memory_space=pltpu.SMEM)


def ceil_to(n, m):
    return -(-n // m) * m


def iota(shape, dim):
    return lax.broadcasted_iota(jnp.int32, shape, dim)


def split3(x):
    hi = x.astype(BF16).astype(F32)
    rest = x - hi
    mid = rest.astype(BF16).astype(F32)
    return hi, mid, rest - mid


def stack_rhs(parts, axis):
    hi, mid, lo = parts
    return jnp.concatenate([hi, mid, lo, hi, mid, hi], axis=axis).astype(BF16)


def stack_lhs(x):
    hi, mid, lo = split3(x)
    return jnp.concatenate([hi, hi, hi, mid, mid, lo], axis=1).astype(BF16)


def dot(a, b):
    return jnp.dot(a, b, preferred_element_type=F32)


def pad_rows(x, rows):
    return jnp.concatenate([x, jnp.zeros((rows - x.shape[0], x.shape[1]), x.dtype)], axis=0)


class Sizes:
    def __init__(self, nv, nb, ne, nq, peers):
        self.nv, self.nb, self.ne, self.nq, self.peers = nv, nb, ne, nq, peers
        self.nbp = ceil_to(nb, 8)
        self.nqp = ceil_to(nq, 8)
        self.lanes = nv * ne
        self.width = nv * nb
        self.kwidth = ceil_to(self.width, 128)
        self.pair = 2 * ne


def to_wide(read, sz):
    return pad_rows(jnp.concatenate([read(v) for v in range(sz.nv)], axis=1), sz.nbp)


def partial_rows(values, peers):
    lane = iota((1, 128), 1)
    row = jnp.zeros((1, 128), F32)
    for i, val in enumerate(values):
        row = jnp.where(lane == i, val, row)
    return jnp.broadcast_to(row, (peers, 128))


def full_sum(x):
    return jnp.sum(jnp.sum(x, axis=0, keepdims=True), axis=1, keepdims=True)


def total_scalars(red, count):
    row = jnp.sum(red, axis=0, keepdims=True)
    return [row[:, i : i + 1] for i in range(count)]


def fetch(pairs, sems):
    copies = [pltpu.make_async_copy(src, dst, sems.at[i]) for i, (src, dst) in enumerate(pairs)]
    for copy in copies:
        copy.start()
    return copies


def init_kernel(sz, me_ref, p_hbm, *refs):
    args, outs, held, sems, p_sem = refs[:11], refs[11:22], refs[22:33], refs[33], refs[34]
    small = fetch(list(zip(args, held)), sems)
    blocks = pltpu.make_async_copy(p_hbm, outs[10], p_sem)
    blocks.start()
    for copy in small:
        copy.wait()
    (res_ref, orders_ref, state_ref, nbr_ref, face_ref, orient_ref, source_ref, flux_ref, geo_ref, stiff_ref, trace_ref) = held
    start_ref, mask_ref, part_ref, state2_ref, hot_ref, coup_ref, turn_ref, own_ref, near_ref, back_ref = outs[:10]
    nv, nb, ne, nq, nbp, nqp = sz.nv, sz.nb, sz.ne, sz.nq, sz.nbp, sz.nqp
    orders = orders_ref[...]
    count = (orders + 1) * (orders + 2) * (orders + 3) // 6
    count = jnp.concatenate([count] * nv, axis=1)
    mask = (iota((nbp, sz.lanes), 0) < count).astype(F32)
    mask_ref[...] = mask
    start = to_wide(lambda v: res_ref[v], sz) * mask
    start_ref[...] = start
    part_ref[...] = partial_rows([full_sum(start * start)], sz.peers)
    state2_ref[...] = to_wide(lambda v: state_ref[v], sz)

    me = me_ref[0]
    nbr = nbr_ref[...]
    rel = nbr - me * ne + ne
    face, orient = face_ref[...], orient_ref[...]
    flip = (orient >= 3).astype(jnp.int32)
    choice, turn = flip * 4 + face, orient - 3 * flip

    def by_face(x):
        return jnp.concatenate([x[f : f + 1] for f in range(4)], axis=1)

    turn_ref[...] = by_face(turn)
    cols = by_face(jnp.where(nbr >= 0, choice * 4 * ne + rel, -1))
    rows = iota((8 * ne, 4 * ne), 0)
    block = rows // ne
    code = block * 4 * ne + rows - block * ne
    chip_side = jnp.where(lax.rem(me, 2) == 0, 2, 0)
    for source, side in enumerate((1, chip_side, 2 - chip_side)):
        hot_ref[source] = (code + side * ne == cols).astype(F32).astype(BF16)

    for k in range(3):
        pieces = []
        for w in range(nv):
            tile = jnp.zeros((nv, ne), F32)
            for d in range(3):
                tile = tile + geo_ref[d, k : k + 1, :] * flux_ref[d, w]
            pieces.append(tile if w == 0 else jnp.concatenate([tile[w:], tile[:w]], axis=0))
        coup_ref[k] = jnp.concatenate(pieces, axis=1)
    pieces = []
    for w in range(nv):
        tile = source_ref[w]
        pieces.append(tile if w == 0 else jnp.concatenate([tile[w:], tile[:w]], axis=0))
    coup_ref[3] = jnp.concatenate(pieces, axis=1)

    def pad2(x, rows):
        x = jnp.concatenate([x, jnp.zeros((x.shape[0], nbp - x.shape[1]), F32)], axis=1)
        return pad_rows(x, rows)

    traces = [trace_ref[:, f, :] for f in range(4)]
    plain = [pad2(t, nqp) for t in traces]
    flipped = [
        pad2(jnp.concatenate([t[q : q + 1] for q in reversed(range(nq))], axis=0), nqp) for t in traces
    ]
    volume = [pad2(stiff_ref[d], nbp) for d in range(3)]
    own_ref[...] = stack_lhs(jnp.concatenate(plain + volume, axis=0))
    near_ref[...] = stack_lhs(jnp.concatenate(plain + flipped, axis=0))
    back_ref[...] = stack_lhs(jnp.concatenate(plain, axis=0).T)
    blocks.wait()


def apply_blocks(sz, vec, mask, blocks_ref):
    nb, ne, nv, width = sz.nb, sz.ne, sz.nv, sz.width
    tall = jnp.concatenate([vec[:nb, v * ne : (v + 1) * ne] for v in range(nv)], axis=0)
    turned = pad_rows(tall, CHUNK).T
    turned = jnp.concatenate(
        [pltpu.roll(turned[g : g + 8], g * width % CHUNK, 1) if g else turned[:8] for g in range(0, ne, 8)], axis=0
    )
    row = iota((ne, 1), 0)
    for bit in (1, 2, 4):
        turned = jnp.where((row & bit) != 0, pltpu.roll(turned, bit * width % CHUNK, 1), turned)
    turned = turned.astype(BF16).astype(F32)
    total, main = ne * width, (width // 16 - SIDE_TILES) * 16
    side_rows = width - main
    acc = [jnp.zeros((8, main), F32)] * (ne // 8)
    side = jnp.zeros((side_rows, ne), F32)
    side_acc = jnp.zeros((side_rows, 128), F32)
    lane = iota((1, ne), 1)
    for low in range(0, total, CHUNK):
        high = min(low + CHUNK, total)
        first, last = low // width // 8, (high - 1) // width // 8 + 1
        size = (8 * (last - first), high - low)
        entry = iota(size, 1) + low - (iota(size, 0) + 8 * first) * width
        lhs = jnp.where((entry >= 0) & (entry < width), turned[8 * first : 8 * last, : high - low], 0.0)
        out = lax.dot_general(
            lhs.astype(BF16), blocks_ref[:main, low:high], (((1,), (1,)), ((), ())), preferred_element_type=F32
        )
        for g in range(first, last):
            acc[g] = acc[g] + out[8 * (g - first) : 8 * (g - first + 1)]
        for start in range(low, high, 128):
            tile = blocks_ref[main:, start : start + 128].astype(F32)
            for e in range(start // width, (start + 127) // width + 1):
                values = lhs[e - 8 * first : e - 8 * first + 1, start - low : start - low + 128]
                side_acc = side_acc + tile * values
                if (e + 1) * width <= start + 128:
                    side = jnp.where(lane == e, jnp.sum(side_acc, axis=1, keepdims=True), side)
                    side_acc = jnp.zeros((side_rows, 128), F32)
    done = jnp.concatenate(acc, axis=0)
    done = jnp.concatenate([done, jnp.zeros((ne, CHUNK - main), F32)], axis=1).T
    done = jnp.concatenate([done[:main], side], axis=0)
    wide = jnp.concatenate([done[v * nb : (v + 1) * nb] for v in range(nv)], axis=1)
    return pad_rows(wide, sz.nbp) * mask


def precond_start_kernel(sz, red_ref, vec_ref, mask_ref, blocks_ref, state_ref, z_ref, v_ref, h_ref):
    norm = jnp.sqrt(total_scalars(red_ref[...], 1)[0] + EPSILON)
    new = vec_ref[...] * (1.0 / norm)
    v_ref[...] = new
    h_ref[...] = partial_rows([norm], 1)
    z_ref[: sz.nbp] = apply_blocks(sz, new, mask_ref[...], blocks_ref)
    z_ref[sz.nbp :] = state_ref[...]


def precond_kernel(sz, step, *refs):
    red_ref, vec_ref, mask_ref, blocks_ref = refs[:4]
    basis = refs[4 : 4 + step]
    z_ref, v_ref, h_ref = refs[4 + step :]
    vec = vec_ref[...]
    scalars = total_scalars(red_ref[...], step + 1)
    proj, square = scalars[:step], scalars[step]
    for h, b in zip(proj, basis):
        vec = vec - h * b[...]
        square = square - h * h
    norm = jnp.sqrt(square + EPSILON)
    new = vec * (1.0 / norm)
    v_ref[...] = new
    h_ref[...] = partial_rows(proj + [norm], 1)
    z_ref[...] = apply_blocks(sz, new, mask_ref[...], blocks_ref)


def roll_blocks(x, blocks, ne):
    shift = blocks * ne
    if shift == 0:
        return x
    return jnp.concatenate([x[:, shift:], x[:, :shift]], axis=1)


def gather(sz, sources, hot_refs, near_ref):
    nqp, ne, pair = sz.nqp, sz.ne, sz.pair
    low_half = iota((1, pair), 1) < ne
    lhs = []
    for source in sources:
        every = dot(near_ref[...], stack_rhs(split3(source), 0))
        rows = []
        for v in range(sz.nv):
            column = every[:, v // 2 * pair : (v // 2 + 1) * pair]
            turned = pltpu.roll(column, ne, 1)
            pieces = []
            for g in range(0, 8, 2):
                first, second = (slice((g + i) * nqp, (g + i + 1) * nqp) for i in range(2))
                if v % 2 == 0:
                    pieces.append(jnp.where(low_half, column[first], turned[second]))
                else:
                    pieces.append(jnp.where(low_half, turned[first], column[second]))
            rows.append(jnp.concatenate(pieces, axis=1))
        lhs.append(jnp.concatenate(rows, axis=0))
    lhs = split3(jnp.concatenate(lhs, axis=1))
    hot = jnp.concatenate([ref[...] for ref in hot_refs], axis=0)
    got = dot(jnp.concatenate(lhs, axis=0).astype(BF16), hot)
    size = sz.nv * nqp
    return got[:size] + got[size : 2 * size] + got[2 * size :]


def to_faces(sz, seen, turn):
    nqp, ne, pair = sz.nqp, sz.ne, sz.pair
    low_half = iota((1, pair), 1) < ne
    nq, third = sz.nq, sz.nq // 3
    turned = []
    for v in range(sz.nv):
        tr = seen[v * nqp : (v + 1) * nqp]
        fill = tr[nq:]
        once = jnp.concatenate([tr[third:nq], tr[:third], fill], axis=0)
        twice = jnp.concatenate([tr[2 * third : nq], tr[: 2 * third], fill], axis=0)
        turned.append(jnp.where(turn == 0, tr, jnp.where(turn == 1, once, twice)))
    result = []
    for f in range(4):
        start = f // 2 * pair
        blocks = []
        for p in range(sz.lanes // pair):
            first, second = (turned[2 * p + i][:, start : start + pair] for i in range(2))
            if f % 2 == 0:
                second = pltpu.roll(second, ne, 1)
            else:
                first = pltpu.roll(first, ne, 1)
            blocks.append(jnp.where(low_half, first, second))
        result.append(jnp.concatenate(blocks, axis=1))
    return jnp.concatenate(result, axis=0)


def spread(row, i):
    return jnp.broadcast_to(row[:, i : i + 1], (1, 128))


def rotate_column(step, row, square, turns_ref):
    entries = [spread(row, i) for i in range(step + 2)]
    if square:
        rest = entries[step + 1]
        for h in entries[:-1]:
            rest = rest - h * h
        entries[step + 1] = jnp.sqrt(rest + EPSILON)
    column = list(entries)
    for i in range(step):
        cosine, sine = turns_ref[2 * i : 2 * i + 1, :], turns_ref[2 * i + 1 : 2 * i + 2, :]
        top, low = column[i], column[i + 1]
        column[i] = cosine * top + sine * low
        column[i + 1] = cosine * low - sine * top
    lead, below = column[step], column[step + 1]
    radius = jnp.sqrt(lead * lead + below * below)
    cosine, sine = lead / radius, below / radius
    column[step] = cosine * lead + sine * below
    return entries, column, cosine, sine


def direction(sz, search, column, earlier):
    def across(x):
        return jnp.concatenate([x] * (sz.lanes // 128), axis=1)

    total = search
    for r, ref in zip(column, earlier):
        total = total - across(r) * ref[...]
    return total * across(1.0 / column[len(earlier)]), across


def fill_column(step, entries, hess):
    row_id, col_id = iota(hess.shape, 0), iota(hess.shape, 1)
    for i, entry in enumerate(entries):
        hess = jnp.where((row_id == i) & (col_id == step), entry[:, : hess.shape[1]], hess)
    return hess


def local_kernel(sz, z_ref, own_ref, coup_ref, vol_ref, tr_ref):
    search = z_ref[: sz.nbp]
    out = dot(own_ref[...], stack_rhs(split3(search), 0))
    faces = 4 * sz.nqp
    tr_ref[...] = out[:faces]
    acc = jnp.zeros((sz.nbp, sz.lanes), F32)
    for d in range(4):
        moved = search if d == 3 else out[faces + d * sz.nbp : faces + (d + 1) * sz.nbp]
        for s in range(sz.nv):
            acc = acc + coup_ref[d, s : s + 1, :] * roll_blocks(moved, s, sz.ne)
    vol_ref[...] = acc


def column_kernel(sz, step, *refs):
    head_ref, z_ref, turns_ref, hess_ref, sum_ref = refs[:5]
    earlier = refs[5 : 5 + step]
    turns_out, hess_out, sum_out, dir_ref = refs[5 + step :]
    entries, column, cosine, sine = rotate_column(step, head_ref[...], False, turns_ref)
    new, across = direction(sz, z_ref[: sz.nbp], column, earlier)
    dir_ref[...] = new
    last = turns_ref.shape[0] - 1
    right = spread(turns_ref[last:, :], 0) if step == 0 else turns_ref[last:, :]
    value = across(cosine * right) * new
    if step == 0:
        sum_out[...] = value
        hess = jnp.zeros(hess_out.shape, F32)
        turns_out[...] = jnp.zeros(turns_out.shape, F32)
    else:
        sum_out[...] = sum_ref[...] + value
        hess = hess_ref[...]
        turns_out[...] = turns_ref[...]
    hess_out[...] = fill_column(step, entries, hess)
    turns_out[2 * step : 2 * step + 1, :] = cosine
    turns_out[2 * step + 1 : 2 * step + 2, :] = sine
    turns_out[turns_out.shape[0] - 1 :, :] = -(sine * right)


def finish_kernel(sz, *refs):
    red_ref, z_ref, turns_ref, hess_ref, sum_ref = refs[:5]
    step = ITERS - 1
    earlier = refs[5 : 5 + step]
    out_ref, hess_out = refs[5 + step :]
    row = jnp.sum(red_ref[...], axis=0, keepdims=True)
    entries, column, cosine, sine = rotate_column(step, row, True, turns_ref)
    new, across = direction(sz, z_ref[...], column, earlier)
    last = turns_ref.shape[0] - 1
    total = sum_ref[...] + across(cosine * turns_ref[last:, :]) * new
    for v in range(sz.nv):
        out_ref[v] = total[: sz.nb, v * sz.ne : (v + 1) * sz.ne]
    hess_out[...] = fill_column(step, entries, hess_ref[...])[: ITERS + 1, :ITERS]


def near_column_kernel(sz, step, *refs):
    near_kernel(sz, *refs[:4], refs[8 + step])
    column_kernel(sz, step - 1, *refs[4 : 8 + step], *refs[9 + step :])


def near_kernel(sz, z_ref, chip_ref, hot_ref, near_ref, *outs):
    nbp = sz.nbp
    for i, out_ref in enumerate(outs):
        sources = [ref[i * nbp : (i + 1) * nbp] for ref in (z_ref, chip_ref)]
        out_ref[...] = gather(sz, sources, [hot_ref.at[0], hot_ref.at[1]], near_ref)


def image_kernel(sz, step, *refs):
    far_ref, hot_ref, near_ref, turn_ref, seen_ref, gain_ref, back_ref, vol_ref, tr_ref, mask_ref = refs[:10]
    basis, refs = refs[10 : 11 + step], refs[11 + step :]
    nbp, turn = sz.nbp, turn_ref[...]
    if step == 0:
        z_ref, own_ref, refs = refs[0], refs[1], refs[2:]
        own = dot(own_ref[: 4 * sz.nqp], stack_rhs(split3(z_ref[nbp:]), 0))
        seen = gain_ref[...] + gather(sz, [far_ref[nbp:]], [hot_ref.at[2]], near_ref)
        gain = 1.0 + 0.5 * jnp.abs(own + to_faces(sz, seen, turn))
        refs[2][...] = gain
    else:
        gain = gain_ref[...]
    seen = seen_ref[...] + gather(sz, [far_ref[:nbp]], [hot_ref.at[2]], near_ref)
    flux = gain * (tr_ref[...] - to_faces(sz, seen, turn))
    face = dot(back_ref[...], stack_rhs(split3(flux), 0))
    image = (vol_ref[...] + face) * mask_ref[...]
    if step < ITERS - 1:
        refs[1][...] = image
    values = [full_sum(b[...] * image) for b in basis] + [full_sum(image * image)]
    refs[0][...] = partial_rows(values, sz.peers)


def call(kernel, name, out_shape, *args, specs=None, scratch=(), limit=24 * 2**20):
    return pl.pallas_call(
        kernel,
        name=name,
        out_shape=out_shape,
        in_specs=specs or [VMEM] * len(args),
        out_specs=jax.tree.map(lambda _: VMEM, out_shape),
        scratch_shapes=list(scratch),
        compiler_params=pltpu.CompilerParams(vmem_limit_bytes=limit),
    )(*args)


def shape(*dims, dtype=F32):
    return jax.ShapeDtypeStruct(dims, dtype)


def copied(arrays):
    return [pltpu.VMEM(a.shape, a.dtype) for a in arrays] + [pltpu.SemaphoreType.DMA((len(arrays),))]


def body(
    peers, state_coeffs, residual_in, orders, neighbours, neighbour_face, orientation, precond, source,
    flux_jacobian, geometry, stiffness, trace_matrix,
):
    nv, nb, ne = state_coeffs.shape
    sz = Sizes(nv, nb, ne, trace_matrix.shape[1], peers)
    lanes, nbp, nqp = sz.lanes, sz.nbp, sz.nqp
    me = lax.axis_index(AXES).astype(jnp.int32).reshape(1)
    wide = shape(nbp, lanes)
    parts = pltpu.VMEM((peers, 128), F32)
    fetched = [
        residual_in, orders.reshape(1, ne), state_coeffs, neighbours, neighbour_face, orientation, source, flux_jacobian,
        geometry, stiffness, jnp.transpose(trace_matrix, (1, 0, 2)),
    ]
    start, mask, part, state, hot, coup, turn, own, near, back, blocks = call(
        functools.partial(init_kernel, sz),
        "init",
        (
            wide, wide, parts, wide,
            shape(3, 8 * ne, 4 * ne, dtype=BF16),
            shape(4, nv, lanes),
            shape(1, 4 * ne, dtype=jnp.int32),
            shape(4 * nqp + 3 * nbp, 6 * nbp, dtype=BF16),
            shape(8 * nqp, 6 * nbp, dtype=BF16),
            shape(nbp, 24 * nqp, dtype=BF16),
            shape(*precond.shape, dtype=BF16),
        ),
        me, *[pltpu.with_memory_space_constraint(a, pltpu.HBM) for a in [precond] + fetched],
        specs=[SMEM] + [ANY] * (1 + len(fetched)), scratch=copied(fetched) + [pltpu.SemaphoreType.DMA],
    )

    def exchange(rows):
        return lax.all_to_all(rows, AXES, 0, 0, tiled=True)

    on_chip = [(i, i ^ 1) for i in range(peers)]
    odd = range(1, peers - 1, 2)
    off_chip = [(i, i + 1) for i in odd] + [(i + 1, i) for i in odd]

    basis, directions = [], []
    vec, gain = start, None
    turns = hess = total = None
    face_shape, seen_shape = shape(4 * nqp, lanes), shape(nv * nqp, 4 * ne)
    state_shapes = (shape(2 * ITERS + 4, 128), shape(8, 128), wide, wide)
    for k in range(ITERS):
        red = exchange(part)
        previous = None if k == 0 else search
        if k == 0:
            search, new, head = call(
                functools.partial(precond_start_kernel, sz), "precond0", (shape(2 * nbp, lanes), wide, shape(1, 128)),
                red, vec, mask, blocks, state,
            )
        else:
            search, new, head = call(
                functools.partial(precond_kernel, sz, k), f"precond{k}", (wide, wide, shape(1, 128)),
                red, vec, mask, blocks, *basis,
            )
        basis = basis + [new]
        far = lax.ppermute(search, AXES, off_chip)
        chip = lax.ppermute(search, AXES, on_chip)
        vol, tr = call(functools.partial(local_kernel, sz), "local", (wide, face_shape), search, own, coup)
        if k == 0:
            turns, hess, total = head, head, head
            seen, gain = call(
                functools.partial(near_kernel, sz), "near", (seen_shape, seen_shape), search, chip, hot, near
            )
        else:
            seen, turns, hess, total, new = call(
                functools.partial(near_column_kernel, sz, k), f"near{k}", (seen_shape,) + state_shapes,
                search, chip, hot, near, head, previous, turns, hess, total, *directions,
            )
            directions = directions + [new]
        extra = basis + ([search, own] if k == 0 else [])
        shapes = (parts,) if k == ITERS - 1 else (parts, wide, face_shape)[: 3 if k == 0 else 2]
        outs = call(
            functools.partial(image_kernel, sz, k), f"image{k}", shapes,
            far, hot, near, turn, seen, gain, back, vol, tr, mask, *extra,
        )
        part, vec = outs[0], outs[1 % len(outs)]
        gain = outs[2] if k == 0 else gain
    red = exchange(part)
    return call(
        functools.partial(finish_kernel, sz), "finish", (shape(nv, nb, ne), shape(ITERS + 1, ITERS)),
        red, search, turns, hess, total, *directions,
    )


def solution(mesh):
    placed = (
        P(None, None, AXES),
        P(None, None, AXES),
        P(AXES),
        P(None, AXES),
        P(None, AXES),
        P(None, AXES),
        P(None, AXES),
        P(None, None, AXES),
        P(None, None, None, AXES),
        P(None, None, AXES),
        P(),
        P(),
    )
    peers = 1
    for axis in AXES:
        peers *= mesh.shape[axis]
    return jax.shard_map(
        functools.partial(body, peers),
        mesh=mesh,
        in_specs=placed,
        out_specs=(P(None, None, AXES), P()),
        check_vma=False,
    )
```

```python
import functools

import jax
import jax.numpy as jnp
from jax import lax
from jax.experimental import pallas as pl
from jax.experimental.pallas import tpu as pltpu
from jax.sharding import PartitionSpec as P

ITERS = 6
EPSILON = 1e-06
AXES = ("dom", "grp")
F32 = jnp.float32
BF16 = jnp.bfloat16
CHUNK = 256
SIDE_TILES = 3
VMEM = pl.BlockSpec(memory_space=pltpu.VMEM)
ANY = pl.BlockSpec(memory_space=pl.ANY)
SMEM = pl.BlockSpec(memory_space=pltpu.SMEM)


def ceil_to(n, m):
    return -(-n // m) * m


def iota(shape, dim):
    return lax.broadcasted_iota(jnp.int32, shape, dim)


def split3(x):
    hi = x.astype(BF16).astype(F32)
    rest = x - hi
    mid = rest.astype(BF16).astype(F32)
    return hi, mid, rest - mid


def stack_rhs(parts, axis):
    hi, mid, lo = parts
    return jnp.concatenate([hi, mid, lo, hi, mid, hi], axis=axis).astype(BF16)


def stack_lhs(x):
    hi, mid, lo = split3(x)
    return jnp.concatenate([hi, hi, hi, mid, mid, lo], axis=1).astype(BF16)


def dot(a, b):
    return jnp.dot(a, b, preferred_element_type=F32)


def pad_rows(x, rows):
    return jnp.concatenate([x, jnp.zeros((rows - x.shape[0], x.shape[1]), x.dtype)], axis=0)


class Sizes:
    def __init__(self, nv, nb, ne, nq, peers):
        self.nv, self.nb, self.ne, self.nq, self.peers = nv, nb, ne, nq, peers
        self.nbp = ceil_to(nb, 8)
        self.nqp = ceil_to(nq, 8)
        self.lanes = nv * ne
        self.width = nv * nb
        self.kwidth = ceil_to(self.width, 128)
        self.pair = 2 * ne


def to_wide(read, sz):
    return pad_rows(jnp.concatenate([read(v) for v in range(sz.nv)], axis=1), sz.nbp)


def partial_rows(values, peers):
    lane = iota((1, 128), 1)
    row = jnp.zeros((1, 128), F32)
    for i, val in enumerate(values):
        row = jnp.where(lane == i, val, row)
    return jnp.broadcast_to(row, (peers, 128))


def full_sum(x):
    return jnp.sum(jnp.sum(x, axis=0, keepdims=True), axis=1, keepdims=True)


def total_scalars(red, count):
    row = jnp.sum(red, axis=0, keepdims=True)
    return [row[:, i : i + 1] for i in range(count)]


def fetch(pairs, sems):
    copies = [pltpu.make_async_copy(src, dst, sems.at[i]) for i, (src, dst) in enumerate(pairs)]
    for copy in copies:
        copy.start()
    return copies


def init_kernel(sz, me_ref, p_hbm, *refs):
    args, outs, held, sems, p_sem = refs[:11], refs[11:22], refs[22:33], refs[33], refs[34]
    small = fetch(list(zip(args, held)), sems)
    blocks = pltpu.make_async_copy(p_hbm, outs[10], p_sem)
    blocks.start()
    for copy in small:
        copy.wait()
    (res_ref, orders_ref, state_ref, nbr_ref, face_ref, orient_ref, source_ref, flux_ref, geo_ref, stiff_ref, trace_ref) = held
    start_ref, mask_ref, part_ref, state2_ref, hot_ref, coup_ref, turn_ref, own_ref, near_ref, back_ref = outs[:10]
    nv, nb, ne, nq, nbp, nqp = sz.nv, sz.nb, sz.ne, sz.nq, sz.nbp, sz.nqp
    orders = orders_ref[...]
    count = (orders + 1) * (orders + 2) * (orders + 3) // 6
    count = jnp.concatenate([count] * nv, axis=1)
    mask = (iota((nbp, sz.lanes), 0) < count).astype(F32)
    mask_ref[...] = mask
    start = to_wide(lambda v: res_ref[v], sz) * mask
    start_ref[...] = start
    part_ref[...] = partial_rows([full_sum(start * start)], sz.peers)
    state2_ref[...] = to_wide(lambda v: state_ref[v], sz)

    me = me_ref[0]
    nbr = nbr_ref[...]
    rel = nbr - me * ne + ne
    face, orient = face_ref[...], orient_ref[...]
    flip = (orient >= 3).astype(jnp.int32)
    choice, turn = flip * 4 + face, orient - 3 * flip

    def by_face(x):
        return jnp.concatenate([x[f : f + 1] for f in range(4)], axis=1)

    turn_ref[...] = by_face(turn)
    cols = by_face(jnp.where(nbr >= 0, choice * 4 * ne + rel, -1))
    rows = iota((8 * ne, 4 * ne), 0)
    block = rows // ne
    code = block * 4 * ne + rows - block * ne
    chip_side = jnp.where(lax.rem(me, 2) == 0, 2, 0)
    for source, side in enumerate((1, chip_side, 2 - chip_side)):
        hot_ref[source] = (code + side * ne == cols).astype(F32).astype(BF16)

    for k in range(3):
        pieces = []
        for w in range(nv):
            tile = jnp.zeros((nv, ne), F32)
            for d in range(3):
                tile = tile + geo_ref[d, k : k + 1, :] * flux_ref[d, w]
            pieces.append(tile if w == 0 else jnp.concatenate([tile[w:], tile[:w]], axis=0))
        coup_ref[k] = jnp.concatenate(pieces, axis=1)
    pieces = []
    for w in range(nv):
        tile = source_ref[w]
        pieces.append(tile if w == 0 else jnp.concatenate([tile[w:], tile[:w]], axis=0))
    coup_ref[3] = jnp.concatenate(pieces, axis=1)

    def pad2(x, rows):
        x = jnp.concatenate([x, jnp.zeros((x.shape[0], nbp - x.shape[1]), F32)], axis=1)
        return pad_rows(x, rows)

    traces = [trace_ref[:, f, :] for f in range(4)]
    plain = [pad2(t, nqp) for t in traces]
    flipped = [
        pad2(jnp.concatenate([t[q : q + 1] for q in reversed(range(nq))], axis=0), nqp) for t in traces
    ]
    volume = [pad2(stiff_ref[d], nbp) for d in range(3)]
    own_ref[...] = stack_lhs(jnp.concatenate(plain + volume, axis=0))
    near_ref[...] = stack_lhs(jnp.concatenate(plain + flipped, axis=0))
    back_ref[...] = stack_lhs(jnp.concatenate(plain, axis=0).T)
    blocks.wait()


def apply_blocks(sz, vec, mask, blocks_ref):
    nb, ne, nv, width = sz.nb, sz.ne, sz.nv, sz.width
    tall = jnp.concatenate([vec[:nb, v * ne : (v + 1) * ne] for v in range(nv)], axis=0)
    turned = pad_rows(tall, CHUNK).T
    turned = jnp.concatenate(
        [pltpu.roll(turned[g : g + 8], g * width % CHUNK, 1) if g else turned[:8] for g in range(0, ne, 8)], axis=0
    )
    row = iota((ne, 1), 0)
    for bit in (1, 2, 4):
        turned = jnp.where((row & bit) != 0, pltpu.roll(turned, bit * width % CHUNK, 1), turned)
    turned = turned.astype(BF16).astype(F32)
    total, main = ne * width, (width // 16 - SIDE_TILES) * 16
    side_rows = width - main
    acc = [jnp.zeros((8, main), F32)] * (ne // 8)
    side = jnp.zeros((side_rows, ne), F32)
    side_acc = jnp.zeros((side_rows, 128), F32)
    lane = iota((1, ne), 1)
    for low in range(0, total, CHUNK):
        high = min(low + CHUNK, total)
        first, last = low // width // 8, (high - 1) // width // 8 + 1
        size = (8 * (last - first), high - low)
        entry = iota(size, 1) + low - (iota(size, 0) + 8 * first) * width
        lhs = jnp.where((entry >= 0) & (entry < width), turned[8 * first : 8 * last, : high - low], 0.0)
        out = lax.dot_general(
            lhs.astype(BF16), blocks_ref[:main, low:high], (((1,), (1,)), ((), ())), preferred_element_type=F32
        )
        for g in range(first, last):
            acc[g] = acc[g] + out[8 * (g - first) : 8 * (g - first + 1)]
        for start in range(low, high, 128):
            tile = blocks_ref[main:, start : start + 128].astype(F32)
            for e in range(start // width, (start + 127) // width + 1):
                values = lhs[e - 8 * first : e - 8 * first + 1, start - low : start - low + 128]
                side_acc = side_acc + tile * values
                if (e + 1) * width <= start + 128:
                    side = jnp.where(lane == e, jnp.sum(side_acc, axis=1, keepdims=True), side)
                    side_acc = jnp.zeros((side_rows, 128), F32)
    done = jnp.concatenate(acc, axis=0)
    done = jnp.concatenate([done, jnp.zeros((ne, CHUNK - main), F32)], axis=1).T
    done = jnp.concatenate([done[:main], side], axis=0)
    wide = jnp.concatenate([done[v * nb : (v + 1) * nb] for v in range(nv)], axis=1)
    return pad_rows(wide, sz.nbp) * mask


def precond_start_kernel(sz, red_ref, vec_ref, mask_ref, blocks_ref, state_ref, z_ref, v_ref, h_ref):
    norm = jnp.sqrt(total_scalars(red_ref[...], 1)[0] + EPSILON)
    new = vec_ref[...] * (1.0 / norm)
    v_ref[...] = new
    h_ref[...] = partial_rows([norm], 1)
    z_ref[: sz.nbp] = apply_blocks(sz, new, mask_ref[...], blocks_ref)
    z_ref[sz.nbp :] = state_ref[...]


def precond_kernel(sz, step, *refs):
    red_ref, vec_ref, mask_ref, blocks_ref = refs[:4]
    basis = refs[4 : 4 + step]
    z_ref, v_ref, h_ref = refs[4 + step :]
    vec = vec_ref[...]
    scalars = total_scalars(red_ref[...], step + 1)
    proj, square = scalars[:step], scalars[step]
    for h, b in zip(proj, basis):
        vec = vec - h * b[...]
        square = square - h * h
    norm = jnp.sqrt(jnp.maximum(square, 0.0) + EPSILON)
    new = vec * (1.0 / norm)
    v_ref[...] = new
    h_ref[...] = partial_rows(proj + [norm], 1)
    z_ref[...] = apply_blocks(sz, new, mask_ref[...], blocks_ref)


def roll_blocks(x, blocks, ne):
    shift = blocks * ne
    if shift == 0:
        return x
    return jnp.concatenate([x[:, shift:], x[:, :shift]], axis=1)


def gather(sz, sources, hot_refs, near_ref):
    nqp, ne, pair = sz.nqp, sz.ne, sz.pair
    low_half = iota((1, pair), 1) < ne
    lhs = []
    for source in sources:
        every = dot(near_ref[...], stack_rhs(split3(source), 0))
        rows = []
        for v in range(sz.nv):
            column = every[:, v // 2 * pair : (v // 2 + 1) * pair]
            turned = pltpu.roll(column, ne, 1)
            pieces = []
            for g in range(0, 8, 2):
                first, second = (slice((g + i) * nqp, (g + i + 1) * nqp) for i in range(2))
                if v % 2 == 0:
                    pieces.append(jnp.where(low_half, column[first], turned[second]))
                else:
                    pieces.append(jnp.where(low_half, turned[first], column[second]))
            rows.append(jnp.concatenate(pieces, axis=1))
        lhs.append(jnp.concatenate(rows, axis=0))
    lhs = split3(jnp.concatenate(lhs, axis=1))
    hot = jnp.concatenate([ref[...] for ref in hot_refs], axis=0)
    got = dot(jnp.concatenate(lhs, axis=0).astype(BF16), hot)
    size = sz.nv * nqp
    return got[:size] + got[size : 2 * size] + got[2 * size :]


def to_faces(sz, seen, turn):
    nqp, ne, pair = sz.nqp, sz.ne, sz.pair
    low_half = iota((1, pair), 1) < ne
    nq, third = sz.nq, sz.nq // 3
    turned = []
    for v in range(sz.nv):
        tr = seen[v * nqp : (v + 1) * nqp]
        fill = tr[nq:]
        once = jnp.concatenate([tr[third:nq], tr[:third], fill], axis=0)
        twice = jnp.concatenate([tr[2 * third : nq], tr[: 2 * third], fill], axis=0)
        turned.append(jnp.where(turn == 0, tr, jnp.where(turn == 1, once, twice)))
    result = []
    for f in range(4):
        start = f // 2 * pair
        blocks = []
        for p in range(sz.lanes // pair):
            first, second = (turned[2 * p + i][:, start : start + pair] for i in range(2))
            if f % 2 == 0:
                second = pltpu.roll(second, ne, 1)
            else:
                first = pltpu.roll(first, ne, 1)
            blocks.append(jnp.where(low_half, first, second))
        result.append(jnp.concatenate(blocks, axis=1))
    return jnp.concatenate(result, axis=0)


def spread(row, i):
    return jnp.broadcast_to(row[:, i : i + 1], (1, 128))


def rotate_column(step, row, square, turns_ref):
    entries = [spread(row, i) for i in range(step + 2)]
    if square:
        rest = entries[step + 1]
        for h in entries[:-1]:
            rest = rest - h * h
        entries[step + 1] = jnp.sqrt(jnp.maximum(rest, 0.0) + EPSILON)
    column = list(entries)
    for i in range(step):
        cosine, sine = turns_ref[2 * i : 2 * i + 1, :], turns_ref[2 * i + 1 : 2 * i + 2, :]
        top, low = column[i], column[i + 1]
        column[i] = cosine * top + sine * low
        column[i + 1] = cosine * low - sine * top
    lead, below = column[step], column[step + 1]
    radius = jnp.sqrt(lead * lead + below * below)
    cosine, sine = lead / radius, below / radius
    column[step] = cosine * lead + sine * below
    return entries, column, cosine, sine


def direction(sz, search, column, earlier):
    def across(x):
        return jnp.concatenate([x] * (sz.lanes // 128), axis=1)

    total = search
    for r, ref in zip(column, earlier):
        total = total - across(r) * ref[...]
    return total * across(1.0 / column[len(earlier)]), across


def fill_column(step, entries, hess):
    row_id, col_id = iota(hess.shape, 0), iota(hess.shape, 1)
    for i, entry in enumerate(entries):
        hess = jnp.where((row_id == i) & (col_id == step), entry[:, : hess.shape[1]], hess)
    return hess


def local_kernel(sz, z_ref, own_ref, coup_ref, vol_ref, tr_ref):
    search = z_ref[: sz.nbp]
    out = dot(own_ref[...], stack_rhs(split3(search), 0))
    faces = 4 * sz.nqp
    tr_ref[...] = out[:faces]
    acc = jnp.zeros((sz.nbp, sz.lanes), F32)
    for d in range(4):
        moved = search if d == 3 else out[faces + d * sz.nbp : faces + (d + 1) * sz.nbp]
        for s in range(sz.nv):
            acc = acc + coup_ref[d, s : s + 1, :] * roll_blocks(moved, s, sz.ne)
    vol_ref[...] = acc


def column_kernel(sz, step, *refs):
    head_ref, z_ref, turns_ref, hess_ref, sum_ref = refs[:5]
    earlier = refs[5 : 5 + step]
    turns_out, hess_out, sum_out, dir_ref = refs[5 + step :]
    entries, column, cosine, sine = rotate_column(step, head_ref[...], False, turns_ref)
    new, across = direction(sz, z_ref[: sz.nbp], column, earlier)
    dir_ref[...] = new
    last = turns_ref.shape[0] - 1
    right = spread(turns_ref[last:, :], 0) if step == 0 else turns_ref[last:, :]
    value = across(cosine * right) * new
    if step == 0:
        sum_out[...] = value
        hess = jnp.zeros(hess_out.shape, F32)
        turns_out[...] = jnp.zeros(turns_out.shape, F32)
    else:
        sum_out[...] = sum_ref[...] + value
        hess = hess_ref[...]
        turns_out[...] = turns_ref[...]
    hess_out[...] = fill_column(step, entries, hess)
    turns_out[2 * step : 2 * step + 1, :] = cosine
    turns_out[2 * step + 1 : 2 * step + 2, :] = sine
    turns_out[turns_out.shape[0] - 1 :, :] = -(sine * right)


def finish_kernel(sz, *refs):
    red_ref, z_ref, turns_ref, hess_ref, sum_ref = refs[:5]
    step = ITERS - 1
    earlier = refs[5 : 5 + step]
    out_ref, hess_out = refs[5 + step :]
    row = jnp.sum(red_ref[...], axis=0, keepdims=True)
    entries, column, cosine, sine = rotate_column(step, row, True, turns_ref)
    new, across = direction(sz, z_ref[...], column, earlier)
    last = turns_ref.shape[0] - 1
    total = sum_ref[...] + across(cosine * turns_ref[last:, :]) * new
    for v in range(sz.nv):
        out_ref[v] = total[: sz.nb, v * sz.ne : (v + 1) * sz.ne]
    hess_out[...] = fill_column(step, entries, hess_ref[...])[: ITERS + 1, :ITERS]


def near_column_kernel(sz, step, *refs):
    near_kernel(sz, *refs[:4], refs[8 + step])
    column_kernel(sz, step - 1, *refs[4 : 8 + step], *refs[9 + step :])


def near_kernel(sz, z_ref, chip_ref, hot_ref, near_ref, *outs):
    nbp = sz.nbp
    for i, out_ref in enumerate(outs):
        sources = [ref[i * nbp : (i + 1) * nbp] for ref in (z_ref, chip_ref)]
        out_ref[...] = gather(sz, sources, [hot_ref.at[0], hot_ref.at[1]], near_ref)


def image_kernel(sz, step, *refs):
    far_ref, hot_ref, near_ref, turn_ref, seen_ref, gain_ref, back_ref, vol_ref, tr_ref, mask_ref = refs[:10]
    basis, refs = refs[10 : 11 + step], refs[11 + step :]
    nbp, turn = sz.nbp, turn_ref[...]
    if step == 0:
        z_ref, own_ref, refs = refs[0], refs[1], refs[2:]
        own = dot(own_ref[: 4 * sz.nqp], stack_rhs(split3(z_ref[nbp:]), 0))
        seen = gain_ref[...] + gather(sz, [far_ref[nbp:]], [hot_ref.at[2]], near_ref)
        gain = 1.0 + 0.5 * jnp.abs(own + to_faces(sz, seen, turn))
        refs[2][...] = gain
    else:
        gain = gain_ref[...]
    seen = seen_ref[...] + gather(sz, [far_ref[:nbp]], [hot_ref.at[2]], near_ref)
    flux = gain * (tr_ref[...] - to_faces(sz, seen, turn))
    face = dot(back_ref[...], stack_rhs(split3(flux), 0))
    image = (vol_ref[...] + face) * mask_ref[...]
    if step < ITERS - 1:
        refs[1][...] = image
    values = [full_sum(b[...] * image) for b in basis] + [full_sum(image * image)]
    refs[0][...] = partial_rows(values, sz.peers)


def call(kernel, name, out_shape, *args, specs=None, scratch=(), limit=24 * 2**20):
    return pl.pallas_call(
        kernel,
        name=name,
        out_shape=out_shape,
        in_specs=specs or [VMEM] * len(args),
        out_specs=jax.tree.map(lambda _: VMEM, out_shape),
        scratch_shapes=list(scratch),
        compiler_params=pltpu.CompilerParams(vmem_limit_bytes=limit),
    )(*args)


def shape(*dims, dtype=F32):
    return jax.ShapeDtypeStruct(dims, dtype)


def copied(arrays):
    return [pltpu.VMEM(a.shape, a.dtype) for a in arrays] + [pltpu.SemaphoreType.DMA((len(arrays),))]


def body(
    peers, state_coeffs, residual_in, orders, neighbours, neighbour_face, orientation, precond, source,
    flux_jacobian, geometry, stiffness, trace_matrix,
):
    nv, nb, ne = state_coeffs.shape
    sz = Sizes(nv, nb, ne, trace_matrix.shape[1], peers)
    lanes, nbp, nqp = sz.lanes, sz.nbp, sz.nqp
    me = lax.axis_index(AXES).astype(jnp.int32).reshape(1)
    wide = shape(nbp, lanes)
    parts = pltpu.VMEM((peers, 128), F32)
    fetched = [
        residual_in, orders.reshape(1, ne), state_coeffs, neighbours, neighbour_face, orientation, source, flux_jacobian,
        geometry, stiffness, jnp.transpose(trace_matrix, (1, 0, 2)),
    ]
    start, mask, part, state, hot, coup, turn, own, near, back, blocks = call(
        functools.partial(init_kernel, sz),
        "init",
        (
            wide, wide, parts, wide,
            shape(3, 8 * ne, 4 * ne, dtype=BF16),
            shape(4, nv, lanes),
            shape(1, 4 * ne, dtype=jnp.int32),
            shape(4 * nqp + 3 * nbp, 6 * nbp, dtype=BF16),
            shape(8 * nqp, 6 * nbp, dtype=BF16),
            shape(nbp, 24 * nqp, dtype=BF16),
            shape(*precond.shape, dtype=BF16),
        ),
        me, *[pltpu.with_memory_space_constraint(a, pltpu.HBM) for a in [precond] + fetched],
        specs=[SMEM] + [ANY] * (1 + len(fetched)), scratch=copied(fetched) + [pltpu.SemaphoreType.DMA],
    )

    def exchange(rows):
        return lax.all_to_all(rows, AXES, 0, 0, tiled=True)

    on_chip = [(i, i ^ 1) for i in range(peers)]
    odd = range(1, peers - 1, 2)
    off_chip = [(i, i + 1) for i in odd] + [(i + 1, i) for i in odd]

    basis, directions = [], []
    vec, gain = start, None
    turns = hess = total = None
    face_shape, seen_shape = shape(4 * nqp, lanes), shape(nv * nqp, 4 * ne)
    state_shapes = (shape(2 * ITERS + 4, 128), shape(8, 128), wide, wide)
    for k in range(ITERS):
        red = exchange(part)
        previous = None if k == 0 else search
        if k == 0:
            search, new, head = call(
                functools.partial(precond_start_kernel, sz), "precond0", (shape(2 * nbp, lanes), wide, shape(1, 128)),
                red, vec, mask, blocks, state,
            )
        else:
            search, new, head = call(
                functools.partial(precond_kernel, sz, k), f"precond{k}", (wide, wide, shape(1, 128)),
                red, vec, mask, blocks, *basis,
            )
        basis = basis + [new]
        far = lax.ppermute(search, AXES, off_chip)
        chip = lax.ppermute(search, AXES, on_chip)
        vol, tr = call(functools.partial(local_kernel, sz), "local", (wide, face_shape), search, own, coup)
        if k == 0:
            turns, hess, total = head, head, head
            seen, gain = call(
                functools.partial(near_kernel, sz), "near", (seen_shape, seen_shape), search, chip, hot, near
            )
        else:
            seen, turns, hess, total, new = call(
                functools.partial(near_column_kernel, sz, k), f"near{k}", (seen_shape,) + state_shapes,
                search, chip, hot, near, head, previous, turns, hess, total, *directions,
            )
            directions = directions + [new]
        extra = basis + ([search, own] if k == 0 else [])
        shapes = (parts,) if k == ITERS - 1 else (parts, wide, face_shape)[: 3 if k == 0 else 2]
        outs = call(
            functools.partial(image_kernel, sz, k), f"image{k}", shapes,
            far, hot, near, turn, seen, gain, back, vol, tr, mask, *extra,
        )
        part, vec = outs[0], outs[1 % len(outs)]
        gain = outs[2] if k == 0 else gain
    red = exchange(part)
    return call(
        functools.partial(finish_kernel, sz), "finish", (shape(nv, nb, ne), shape(ITERS + 1, ITERS)),
        red, search, turns, hess, total, *directions,
    )


def solution(mesh):
    placed = (
        P(None, None, AXES),
        P(None, None, AXES),
        P(AXES),
        P(None, AXES),
        P(None, AXES),
        P(None, AXES),
        P(None, AXES),
        P(None, None, AXES),
        P(None, None, None, AXES),
        P(None, None, AXES),
        P(),
        P(),
    )
    peers = 1
    for axis in AXES:
        peers *= mesh.shape[axis]
    return jax.shard_map(
        functools.partial(body, peers),
        mesh=mesh,
        in_specs=placed,
        out_specs=(P(None, None, AXES), P()),
        check_vma=False,
    )
```

```python
import functools

import jax
import jax.numpy as jnp
from jax import lax
from jax.experimental import pallas as pl
from jax.experimental.pallas import tpu as pltpu
from jax.sharding import PartitionSpec as P

ITERS = 6
EPSILON = 1e-06
AXES = ("dom", "grp")
F32 = jnp.float32
BF16 = jnp.bfloat16
CHUNK = 256
SIDE_TILES = 3
VMEM = pl.BlockSpec(memory_space=pltpu.VMEM)
ANY = pl.BlockSpec(memory_space=pl.ANY)
SMEM = pl.BlockSpec(memory_space=pltpu.SMEM)


def ceil_to(n, m):
    return -(-n // m) * m


def iota(shape, dim):
    return lax.broadcasted_iota(jnp.int32, shape, dim)


def split3(x):
    hi = x.astype(BF16).astype(F32)
    rest = x - hi
    mid = rest.astype(BF16).astype(F32)
    return hi, mid, rest - mid


def stack_rhs(parts, axis):
    hi, mid, lo = parts
    return jnp.concatenate([hi, mid, lo, hi, mid, hi], axis=axis).astype(BF16)


def stack_lhs(x):
    hi, mid, lo = split3(x)
    return jnp.concatenate([hi, hi, hi, mid, mid, lo], axis=1).astype(BF16)


def dot(a, b):
    return jnp.dot(a, b, preferred_element_type=F32)


def pad_rows(x, rows):
    return jnp.concatenate([x, jnp.zeros((rows - x.shape[0], x.shape[1]), x.dtype)], axis=0)


class Sizes:
    def __init__(self, nv, nb, ne, nq, peers):
        self.nv, self.nb, self.ne, self.nq, self.peers = nv, nb, ne, nq, peers
        self.nbp = ceil_to(nb, 8)
        self.nqp = ceil_to(nq, 8)
        self.lanes = nv * ne
        self.width = nv * nb
        self.kwidth = ceil_to(self.width, 128)
        self.pair = 2 * ne


def to_wide(read, sz):
    return pad_rows(jnp.concatenate([read(v) for v in range(sz.nv)], axis=1), sz.nbp)


def partial_rows(values, peers):
    lane = iota((1, 128), 1)
    row = jnp.zeros((1, 128), F32)
    for i, val in enumerate(values):
        row = jnp.where(lane == i, val, row)
    return jnp.broadcast_to(row, (peers, 128))


def full_sum(x):
    tile = sum(
        x[r : r + 8, c : c + 128] for r in range(0, x.shape[0], 8) for c in range(0, x.shape[1], 128)
    )
    return jnp.sum(jnp.sum(tile, axis=1, keepdims=True), axis=0, keepdims=True)


def total_scalars(red, count):
    row = jnp.sum(red, axis=0, keepdims=True)
    return [row[:, i : i + 1] for i in range(count)]


def fetch(pairs, sems):
    copies = [pltpu.make_async_copy(src, dst, sems.at[i]) for i, (src, dst) in enumerate(pairs)]
    for copy in copies:
        copy.start()
    return copies


def init_kernel(sz, me_ref, p_hbm, *refs):
    args, outs, held, sems, p_sem = refs[:11], refs[11:22], refs[22:33], refs[33], refs[34]
    small = fetch(list(zip(args, held)), sems)
    blocks = pltpu.make_async_copy(p_hbm, outs[10], p_sem)
    blocks.start()
    for copy in small:
        copy.wait()
    (res_ref, orders_ref, state_ref, nbr_ref, face_ref, orient_ref, source_ref, flux_ref, geo_ref, stiff_ref, trace_ref) = held
    start_ref, mask_ref, part_ref, state2_ref, hot_ref, coup_ref, turn_ref, own_ref, near_ref, back_ref = outs[:10]
    nv, nb, ne, nq, nbp, nqp = sz.nv, sz.nb, sz.ne, sz.nq, sz.nbp, sz.nqp
    orders = orders_ref[...]
    count = (orders + 1) * (orders + 2) * (orders + 3) // 6
    count = jnp.concatenate([count] * nv, axis=1)
    mask = (iota((nbp, sz.lanes), 0) < count).astype(F32)
    mask_ref[...] = mask
    start = to_wide(lambda v: res_ref[v], sz) * mask
    start_ref[...] = start
    part_ref[...] = partial_rows([full_sum(start * start)], sz.peers)
    state2_ref[...] = to_wide(lambda v: state_ref[v], sz)

    me = me_ref[0]
    nbr = nbr_ref[...]
    rel = nbr - me * ne + ne
    face, orient = face_ref[...], orient_ref[...]
    flip = (orient >= 3).astype(jnp.int32)
    choice, turn = flip * 4 + face, orient - 3 * flip

    def by_face(x):
        return jnp.concatenate([x[f : f + 1] for f in range(4)], axis=1)

    turn_ref[...] = by_face(turn)
    cols = by_face(jnp.where(nbr >= 0, choice * 4 * ne + rel, -1))
    rows = iota((8 * ne, 4 * ne), 0)
    block = rows // ne
    code = block * 4 * ne + rows - block * ne
    chip_side = jnp.where(lax.rem(me, 2) == 0, 2, 0)
    for source, side in enumerate((1, chip_side, 2 - chip_side)):
        hot_ref[source] = (code + side * ne == cols).astype(F32).astype(BF16)

    for k in range(3):
        pieces = []
        for w in range(nv):
            tile = jnp.zeros((nv, ne), F32)
            for d in range(3):
                tile = tile + geo_ref[d, k : k + 1, :] * flux_ref[d, w]
            pieces.append(tile if w == 0 else jnp.concatenate([tile[w:], tile[:w]], axis=0))
        coup_ref[k] = jnp.concatenate(pieces, axis=1)
    pieces = []
    for w in range(nv):
        tile = source_ref[w]
        pieces.append(tile if w == 0 else jnp.concatenate([tile[w:], tile[:w]], axis=0))
    coup_ref[3] = jnp.concatenate(pieces, axis=1)

    def pad2(x, rows):
        x = jnp.concatenate([x, jnp.zeros((x.shape[0], nbp - x.shape[1]), F32)], axis=1)
        return pad_rows(x, rows)

    traces = [trace_ref[:, f, :] for f in range(4)]
    plain = [pad2(t, nqp) for t in traces]
    flipped = [
        pad2(jnp.concatenate([t[q : q + 1] for q in reversed(range(nq))], axis=0), nqp) for t in traces
    ]
    volume = [pad2(stiff_ref[d], nbp) for d in range(3)]
    own_ref[...] = stack_lhs(jnp.concatenate(plain + volume, axis=0))
    near_ref[...] = stack_lhs(jnp.concatenate(plain + flipped, axis=0))
    back_ref[...] = stack_lhs(jnp.concatenate(plain, axis=0).T)
    blocks.wait()


def apply_blocks(sz, vec, mask, blocks_ref):
    nb, ne, nv, width = sz.nb, sz.ne, sz.nv, sz.width
    tall = jnp.concatenate([vec[:nb, v * ne : (v + 1) * ne] for v in range(nv)], axis=0)
    turned = pad_rows(tall, CHUNK).T
    turned = jnp.concatenate(
        [pltpu.roll(turned[g : g + 8], g * width % CHUNK, 1) if g else turned[:8] for g in range(0, ne, 8)], axis=0
    )
    row = iota((ne, 1), 0)
    for bit in (1, 2, 4):
        turned = jnp.where((row & bit) != 0, pltpu.roll(turned, bit * width % CHUNK, 1), turned)
    turned = turned.astype(BF16).astype(F32)
    total, main = ne * width, (width // 16 - SIDE_TILES) * 16
    side_rows = width - main
    acc = [jnp.zeros((8, main), F32)] * (ne // 8)
    side = jnp.zeros((side_rows, ne), F32)
    side_acc = jnp.zeros((side_rows, 128), F32)
    lane = iota((1, ne), 1)
    for low in range(0, total, CHUNK):
        high = min(low + CHUNK, total)
        first, last = low // width // 8, (high - 1) // width // 8 + 1
        size = (8 * (last - first), high - low)
        entry = iota(size, 1) + low - (iota(size, 0) + 8 * first) * width
        lhs = jnp.where((entry >= 0) & (entry < width), turned[8 * first : 8 * last, : high - low], 0.0)
        out = lax.dot_general(
            lhs.astype(BF16), blocks_ref[:main, low:high], (((1,), (1,)), ((), ())), preferred_element_type=F32
        )
        for g in range(first, last):
            acc[g] = acc[g] + out[8 * (g - first) : 8 * (g - first + 1)]
        for start in range(low, high, 128):
            tile = blocks_ref[main:, start : start + 128].astype(F32)
            for e in range(start // width, (start + 127) // width + 1):
                values = lhs[e - 8 * first : e - 8 * first + 1, start - low : start - low + 128]
                side_acc = side_acc + tile * values
                if (e + 1) * width <= start + 128:
                    side = jnp.where(lane == e, jnp.sum(side_acc, axis=1, keepdims=True), side)
                    side_acc = jnp.zeros((side_rows, 128), F32)
    done = jnp.concatenate(acc, axis=0)
    done = jnp.concatenate([done, jnp.zeros((ne, CHUNK - main), F32)], axis=1).T
    done = jnp.concatenate([done[:main], side], axis=0)
    wide = jnp.concatenate([done[v * nb : (v + 1) * nb] for v in range(nv)], axis=1)
    return pad_rows(wide, sz.nbp) * mask


def precond_start_kernel(sz, red_ref, vec_ref, mask_ref, blocks_ref, state_ref, z_ref, v_ref, h_ref):
    norm = jnp.sqrt(total_scalars(red_ref[...], 1)[0] + EPSILON)
    new = vec_ref[...] * (1.0 / norm)
    v_ref[...] = new
    h_ref[...] = partial_rows([norm], 1)
    z_ref[: sz.nbp] = apply_blocks(sz, new, mask_ref[...], blocks_ref)
    z_ref[sz.nbp :] = state_ref[...]


def precond_kernel(sz, step, *refs):
    red_ref, vec_ref, mask_ref, blocks_ref = refs[:4]
    basis = refs[4 : 4 + step]
    z_ref, v_ref, h_ref = refs[4 + step :]
    vec = vec_ref[...]
    scalars = total_scalars(red_ref[...], step + 1)
    proj, square = scalars[:step], scalars[step]
    for h, b in zip(proj, basis):
        vec = vec - h * b[...]
        square = square - h * h
    norm = jnp.sqrt(jnp.maximum(square, 0.0) + EPSILON)
    new = vec * (1.0 / norm)
    v_ref[...] = new
    h_ref[...] = partial_rows(proj + [norm], 1)
    z_ref[...] = apply_blocks(sz, new, mask_ref[...], blocks_ref)


def roll_blocks(x, blocks, ne):
    shift = blocks * ne
    if shift == 0:
        return x
    return jnp.concatenate([x[:, shift:], x[:, :shift]], axis=1)


def gather(sz, sources, hot_refs, near_ref):
    nqp, ne, pair = sz.nqp, sz.ne, sz.pair
    low_half = iota((1, pair), 1) < ne
    lhs = []
    for source in sources:
        every = dot(near_ref[...], stack_rhs(split3(source), 0))
        rows = []
        for v in range(sz.nv):
            column = every[:, v // 2 * pair : (v // 2 + 1) * pair]
            turned = pltpu.roll(column, ne, 1)
            pieces = []
            for g in range(0, 8, 2):
                first, second = (slice((g + i) * nqp, (g + i + 1) * nqp) for i in range(2))
                if v % 2 == 0:
                    pieces.append(jnp.where(low_half, column[first], turned[second]))
                else:
                    pieces.append(jnp.where(low_half, turned[first], column[second]))
            rows.append(jnp.concatenate(pieces, axis=1))
        lhs.append(jnp.concatenate(rows, axis=0))
    lhs = split3(jnp.concatenate(lhs, axis=1))
    hot = jnp.concatenate([ref[...] for ref in hot_refs], axis=0)
    got = dot(jnp.concatenate(lhs, axis=0).astype(BF16), hot)
    size = sz.nv * nqp
    return got[:size] + got[size : 2 * size] + got[2 * size :]


def to_faces(sz, seen, turn):
    nqp, ne, pair = sz.nqp, sz.ne, sz.pair
    low_half = iota((1, pair), 1) < ne
    nq, third = sz.nq, sz.nq // 3
    turned = []
    for v in range(sz.nv):
        tr = seen[v * nqp : (v + 1) * nqp]
        fill = tr[nq:]
        once = jnp.concatenate([tr[third:nq], tr[:third], fill], axis=0)
        twice = jnp.concatenate([tr[2 * third : nq], tr[: 2 * third], fill], axis=0)
        turned.append(jnp.where(turn == 0, tr, jnp.where(turn == 1, once, twice)))
    result = []
    for f in range(4):
        start = f // 2 * pair
        blocks = []
        for p in range(sz.lanes // pair):
            first, second = (turned[2 * p + i][:, start : start + pair] for i in range(2))
            if f % 2 == 0:
                second = pltpu.roll(second, ne, 1)
            else:
                first = pltpu.roll(first, ne, 1)
            blocks.append(jnp.where(low_half, first, second))
        result.append(jnp.concatenate(blocks, axis=1))
    return jnp.concatenate(result, axis=0)


def spread(row, i):
    return jnp.broadcast_to(row[:, i : i + 1], (1, 128))


def rotate_column(step, row, square, turns_ref):
    entries = [spread(row, i) for i in range(step + 2)]
    if square:
        rest = entries[step + 1]
        for h in entries[:-1]:
            rest = rest - h * h
        entries[step + 1] = jnp.sqrt(jnp.maximum(rest, 0.0) + EPSILON)
    column = list(entries)
    for i in range(step):
        cosine, sine = turns_ref[2 * i : 2 * i + 1, :], turns_ref[2 * i + 1 : 2 * i + 2, :]
        top, low = column[i], column[i + 1]
        column[i] = cosine * top + sine * low
        column[i + 1] = cosine * low - sine * top
    lead, below = column[step], column[step + 1]
    radius = jnp.sqrt(lead * lead + below * below)
    cosine, sine = lead / radius, below / radius
    column[step] = cosine * lead + sine * below
    return entries, column, cosine, sine


def direction(sz, search, column, earlier):
    def across(x):
        return jnp.concatenate([x] * (sz.lanes // 128), axis=1)

    total = search
    for r, ref in zip(column, earlier):
        total = total - across(r) * ref[...]
    return total * across(1.0 / column[len(earlier)]), across


def fill_column(step, entries, hess):
    row_id, col_id = iota(hess.shape, 0), iota(hess.shape, 1)
    for i, entry in enumerate(entries):
        hess = jnp.where((row_id == i) & (col_id == step), entry[:, : hess.shape[1]], hess)
    return hess


def local_kernel(sz, z_ref, own_ref, coup_ref, vol_ref, tr_ref):
    search = z_ref[: sz.nbp]
    out = dot(own_ref[...], stack_rhs(split3(search), 0))
    faces = 4 * sz.nqp
    tr_ref[...] = out[:faces]
    acc = jnp.zeros((sz.nbp, sz.lanes), F32)
    for d in range(4):
        moved = search if d == 3 else out[faces + d * sz.nbp : faces + (d + 1) * sz.nbp]
        for s in range(sz.nv):
            acc = acc + coup_ref[d, s : s + 1, :] * roll_blocks(moved, s, sz.ne)
    vol_ref[...] = acc


def column_kernel(sz, step, *refs):
    head_ref, z_ref, turns_ref, hess_ref, sum_ref = refs[:5]
    earlier = refs[5 : 5 + step]
    turns_out, hess_out, sum_out, dir_ref = refs[5 + step :]
    entries, column, cosine, sine = rotate_column(step, head_ref[...], False, turns_ref)
    new, across = direction(sz, z_ref[: sz.nbp], column, earlier)
    dir_ref[...] = new
    last = turns_ref.shape[0] - 1
    right = spread(turns_ref[last:, :], 0) if step == 0 else turns_ref[last:, :]
    value = across(cosine * right) * new
    if step == 0:
        sum_out[...] = value
        hess = jnp.zeros(hess_out.shape, F32)
        turns_out[...] = jnp.zeros(turns_out.shape, F32)
    else:
        sum_out[...] = sum_ref[...] + value
        hess = hess_ref[...]
        turns_out[...] = turns_ref[...]
    hess_out[...] = fill_column(step, entries, hess)
    turns_out[2 * step : 2 * step + 1, :] = cosine
    turns_out[2 * step + 1 : 2 * step + 2, :] = sine
    turns_out[turns_out.shape[0] - 1 :, :] = -(sine * right)


def finish_kernel(sz, *refs):
    red_ref, z_ref, turns_ref, hess_ref, sum_ref = refs[:5]
    step = ITERS - 1
    earlier = refs[5 : 5 + step]
    out_ref, hess_out = refs[5 + step :]
    row = jnp.sum(red_ref[...], axis=0, keepdims=True)
    entries, column, cosine, sine = rotate_column(step, row, True, turns_ref)
    new, across = direction(sz, z_ref[...], column, earlier)
    last = turns_ref.shape[0] - 1
    total = sum_ref[...] + across(cosine * turns_ref[last:, :]) * new
    for v in range(sz.nv):
        out_ref[v] = total[: sz.nb, v * sz.ne : (v + 1) * sz.ne]
    hess_out[...] = fill_column(step, entries, hess_ref[...])[: ITERS + 1, :ITERS]


def near_column_kernel(sz, step, *refs):
    near_kernel(sz, *refs[:4], refs[8 + step])
    column_kernel(sz, step - 1, *refs[4 : 8 + step], *refs[9 + step :])


def near_kernel(sz, z_ref, chip_ref, hot_ref, near_ref, *outs):
    nbp = sz.nbp
    for i, out_ref in enumerate(outs):
        sources = [ref[i * nbp : (i + 1) * nbp] for ref in (z_ref, chip_ref)]
        out_ref[...] = gather(sz, sources, [hot_ref.at[0], hot_ref.at[1]], near_ref)


def image_kernel(sz, step, *refs):
    far_ref, hot_ref, near_ref, turn_ref, seen_ref, gain_ref, back_ref, vol_ref, tr_ref, mask_ref = refs[:10]
    basis, refs = refs[10 : 11 + step], refs[11 + step :]
    nbp, turn = sz.nbp, turn_ref[...]
    if step == 0:
        z_ref, own_ref, refs = refs[0], refs[1], refs[2:]
        own = dot(own_ref[: 4 * sz.nqp], stack_rhs(split3(z_ref[nbp:]), 0))
        seen = gain_ref[...] + gather(sz, [far_ref[nbp:]], [hot_ref.at[2]], near_ref)
        gain = 1.0 + 0.5 * jnp.abs(own + to_faces(sz, seen, turn))
        refs[2][...] = gain
    else:
        gain = gain_ref[...]
    seen = seen_ref[...] + gather(sz, [far_ref[:nbp]], [hot_ref.at[2]], near_ref)
    flux = gain * (tr_ref[...] - to_faces(sz, seen, turn))
    face = dot(back_ref[...], stack_rhs(split3(flux), 0))
    image = (vol_ref[...] + face) * mask_ref[...]
    if step < ITERS - 1:
        refs[1][...] = image
    values = [full_sum(b[...] * image) for b in basis] + [full_sum(image * image)]
    refs[0][...] = partial_rows(values, sz.peers)


def call(kernel, name, out_shape, *args, specs=None, scratch=(), limit=24 * 2**20):
    return pl.pallas_call(
        kernel,
        name=name,
        out_shape=out_shape,
        in_specs=specs or [VMEM] * len(args),
        out_specs=jax.tree.map(lambda _: VMEM, out_shape),
        scratch_shapes=list(scratch),
        compiler_params=pltpu.CompilerParams(vmem_limit_bytes=limit),
    )(*args)


def shape(*dims, dtype=F32):
    return jax.ShapeDtypeStruct(dims, dtype)


def copied(arrays):
    return [pltpu.VMEM(a.shape, a.dtype) for a in arrays] + [pltpu.SemaphoreType.DMA((len(arrays),))]


def body(
    peers, state_coeffs, residual_in, orders, neighbours, neighbour_face, orientation, precond, source,
    flux_jacobian, geometry, stiffness, trace_matrix,
):
    nv, nb, ne = state_coeffs.shape
    sz = Sizes(nv, nb, ne, trace_matrix.shape[1], peers)
    lanes, nbp, nqp = sz.lanes, sz.nbp, sz.nqp
    me = lax.axis_index(AXES).astype(jnp.int32).reshape(1)
    wide = shape(nbp, lanes)
    parts = pltpu.VMEM((peers, 128), F32)
    fetched = [
        residual_in, orders.reshape(1, ne), state_coeffs, neighbours, neighbour_face, orientation, source, flux_jacobian,
        geometry, stiffness, jnp.transpose(trace_matrix, (1, 0, 2)),
    ]
    start, mask, part, state, hot, coup, turn, own, near, back, blocks = call(
        functools.partial(init_kernel, sz),
        "init",
        (
            wide, wide, parts, wide,
            shape(3, 8 * ne, 4 * ne, dtype=BF16),
            shape(4, nv, lanes),
            shape(1, 4 * ne, dtype=jnp.int32),
            shape(4 * nqp + 3 * nbp, 6 * nbp, dtype=BF16),
            shape(8 * nqp, 6 * nbp, dtype=BF16),
            shape(nbp, 24 * nqp, dtype=BF16),
            shape(*precond.shape, dtype=BF16),
        ),
        me, *[pltpu.with_memory_space_constraint(a, pltpu.HBM) for a in [precond] + fetched],
        specs=[SMEM] + [ANY] * (1 + len(fetched)), scratch=copied(fetched) + [pltpu.SemaphoreType.DMA],
    )

    def exchange(rows):
        return lax.all_to_all(rows, AXES, 0, 0, tiled=True)

    on_chip = [(i, i ^ 1) for i in range(peers)]
    odd = range(1, peers - 1, 2)
    off_chip = [(i, i + 1) for i in odd] + [(i + 1, i) for i in odd]

    basis, directions = [], []
    vec, gain = start, None
    turns = hess = total = None
    face_shape, seen_shape = shape(4 * nqp, lanes), shape(nv * nqp, 4 * ne)
    state_shapes = (shape(2 * ITERS + 4, 128), shape(8, 128), wide, wide)
    for k in range(ITERS):
        red = exchange(part)
        previous = None if k == 0 else search
        if k == 0:
            search, new, head = call(
                functools.partial(precond_start_kernel, sz), "precond0", (shape(2 * nbp, lanes), wide, shape(1, 128)),
                red, vec, mask, blocks, state,
            )
        else:
            search, new, head = call(
                functools.partial(precond_kernel, sz, k), f"precond{k}", (wide, wide, shape(1, 128)),
                red, vec, mask, blocks, *basis,
            )
        basis = basis + [new]
        far = lax.ppermute(search, AXES, off_chip)
        chip = lax.ppermute(search, AXES, on_chip)
        vol, tr = call(functools.partial(local_kernel, sz), "local", (wide, face_shape), search, own, coup)
        if k == 0:
            turns, hess, total = head, head, head
            seen, gain = call(
                functools.partial(near_kernel, sz), "near", (seen_shape, seen_shape), search, chip, hot, near
            )
        else:
            seen, turns, hess, total, new = call(
                functools.partial(near_column_kernel, sz, k), f"near{k}", (seen_shape,) + state_shapes,
                search, chip, hot, near, head, previous, turns, hess, total, *directions,
            )
            directions = directions + [new]
        extra = basis + ([search, own] if k == 0 else [])
        shapes = (parts,) if k == ITERS - 1 else (parts, wide, face_shape)[: 3 if k == 0 else 2]
        outs = call(
            functools.partial(image_kernel, sz, k), f"image{k}", shapes,
            far, hot, near, turn, seen, gain, back, vol, tr, mask, *extra,
        )
        part, vec = outs[0], outs[1 % len(outs)]
        gain = outs[2] if k == 0 else gain
    red = exchange(part)
    return call(
        functools.partial(finish_kernel, sz), "finish", (shape(nv, nb, ne), shape(ITERS + 1, ITERS)),
        red, search, turns, hess, total, *directions,
    )


def solution(mesh):
    placed = (
        P(None, None, AXES),
        P(None, None, AXES),
        P(AXES),
        P(None, AXES),
        P(None, AXES),
        P(None, AXES),
        P(None, AXES),
        P(None, None, AXES),
        P(None, None, None, AXES),
        P(None, None, AXES),
        P(),
        P(),
    )
    peers = 1
    for axis in AXES:
        peers *= mesh.shape[axis]
    return jax.shard_map(
        functools.partial(body, peers),
        mesh=mesh,
        in_specs=placed,
        out_specs=(P(None, None, AXES), P()),
        check_vma=False,
    )
```
